32 devices in a mesh: group: 2 (over y), replica: 16 (over z, x, core).
Axes of the slice: x: 2, y: 2, z: 4, core: 2. Of those that a mesh axis runs over, the one named last changes fastest.
Arguments:
- tokens: bfloat16 [32, 144, 896], P(('group', 'replica')), may hold values from -6 to 6
- segments: int32 [32, 144], P(('group', 'replica')), may hold values from 0 to 35, never falling along the last dimension, each value on 1 to 72 neighbouring positions
- norm1_gain: bfloat16 [896], P('group'), may hold values from 0.5 to 1.5
- qkv_weight: bfloat16 [896, 1152], P('group'), may hold values from -0.1875 to 0.1875
- qkv_bias: bfloat16 [1152], P('group'), may hold values from -2.5 to 2.5
- out_weight: bfloat16 [896, 896], P('group'), may hold values from -0.375 to 0.375
- norm2_gain: bfloat16 [896], P('group'), may hold values from 0.5 to 1.5
- gate_weight: bfloat16 [896, 4864], P(None, 'group'), may hold values from -0.1875 to 0.1875
- up_weight: bfloat16 [896, 4864], P(None, 'group'), may hold values from -0.1875 to 0.1875
- down_weight: bfloat16 [4864, 896], P('group'), may hold values from -0.078125 to 0.078125
- cotangent: bfloat16 [32, 144, 896], P(('group', 'replica')), may hold values from -6 to 6
Outputs:
- result: float32 [32, 144, 896], P(('group', 'replica'))
- back_tokens: float32 [32, 144, 896], P(('group', 'replica'))
- grad_norm1: float32 [896], P('group')
- grad_qkv: float32 [896, 1152], P('group')
- grad_bias: float32 [1152], P('group')
- grad_out: float32 [896, 896], P('group')
- grad_norm2: float32 [896], P('group')
- grad_gate: float32 [896, 4864], P(None, 'group')
- grad_up: float32 [896, 4864], P(None, 'group')
- grad_down: float32 [4864, 896], P('group')
The draws below stay inside these ranges and needn't reach their ends.
Inputs may be any that keep to these rules, and one draw needn't show every extreme that they name: `segments`: segment ids never fall along a sequence.
All inputs are finite; a program needn't handle non-finite values.
Results may differ from the reference program's by a relative error of at most 0.023.
Values may be sent and summed in bfloat16 or wider, within the bound.
A program may use at most 192 MiB of HBM per device.

```python
import math
import jax
import jax.numpy as jnp
import numpy as np
from jax import lax

D = 896
H = 14
KV = 2
HD = 64
FF = 4864
SEQ = 144
QKV = 1152
HQ = 896
SEQS = 32


def draw_qkv_bias(key, part):
    key_base = jax.random.fold_in(key, 17)
    values = 0.5 * jax.random.normal(key_base, (QKV,), jnp.float32)
    return jnp.clip(values, -2.5, 2.5).astype(jnp.bfloat16)


def block_levels(stream_key, extent, cuts, least, top_value):
    loudness = 1.0
    for axis_at, shards_of in cuts:
        draws = jax.random.uniform(jax.random.fold_in(jax.random.fold_in(stream_key, 6), axis_at), (shards_of,), jnp.float32, least / len(cuts), top_value / len(cuts))
        loudness = loudness * jnp.repeat(jnp.exp(draws), extent[axis_at] // shards_of).reshape((-1,) + (1,) * (len(extent) - 1 - axis_at))
    return loudness


def split_up(number_of, total, limit, lean):
    weights = [(1 << 20) // math.isqrt(rank ** lean) + 1 for rank in range(2, number_of + 1)]
    spare, holding = total - limit - (number_of - 1), [1] * (number_of - 1)
    while spare > 0:
        free = [i for i in range(number_of - 1) if holding[i] < limit]
        pool, left = sum([weights[i] for i in free]), spare
        for i in free:
            addition = min(limit - holding[i], max(1, left * weights[i] // pool), spare)
            holding[i] = holding[i] + addition
            spare = spare - addition
    return np.array([limit] + holding)


def uneven(key, number_of, total, reach, slope):
    if number_of == 2:
        one = jax.random.randint(key, (), max(1, total - reach), min(reach, total - 1) + 1)
        return jnp.stack([one, total - one])
    tallies = jnp.asarray(split_up(number_of, total, reach, slope), jnp.int32)
    twos = (number_of - 1) // 2
    donor, receiver = tallies[1:1 + 2 * twos:2], tallies[2:2 + 2 * twos:2]
    margin = jnp.minimum(donor - 1, reach - receiver)
    shifted = jax.random.randint(jax.random.fold_in(key, 1), (twos,), 0, 1 << 20) % (margin + 1)
    tallies = tallies.at[1:1 + 2 * twos:2].set(donor - shifted).at[2:2 + 2 * twos:2].set(receiver + shifted)
    return tallies[jax.random.permutation(jax.random.fold_in(key, 2), number_of)]


def scatter_about(rng, dims, spread, reach, cuts=(), kind=jnp.bfloat16):
    gain = block_levels(rng, dims, cuts, -0.22, 0.18) if cuts else 1.0
    array = jax.random.normal(rng, dims, jnp.float32) * spread * gain
    return jnp.minimum(jnp.maximum(array, -reach), reach).astype(kind)


def setup_inputs(seed: int = 0) -> dict:
    streams_of = jax.random.split(jax.random.key(seed), 12)
    return {
        "tokens": scatter_about(streams_of[0], (SEQS, SEQ, D), 1.0, 6.0, ((0, 32),)),
        "segments": jax.vmap(lambda own: jnp.searchsorted(jnp.cumsum(uneven(own, SEQ // 4, SEQ, SEQ // 2, 2)), jnp.arange(SEQ), side="right"))(jax.random.split(streams_of[1], SEQS)).reshape((SEQS, SEQ)).astype(jnp.int32),
        "norm1_gain": jnp.clip(1.0 + 0.1 * jax.random.normal(streams_of[2], (D,), jnp.float32), 0.5, 1.5).astype(jnp.bfloat16),
        "qkv_weight": scatter_about(streams_of[3], (D, QKV), D ** -0.5, 0.1875, ((0, 2),)),
        "qkv_bias": draw_qkv_bias(jax.random.fold_in(streams_of[11], 71), 0),
        "out_weight": scatter_about(streams_of[5], (HQ, D), (HQ // 4) ** -0.5, 0.375, ((0, 2),)),
        "norm2_gain": jnp.clip(1.0 + 0.1 * jax.random.normal(streams_of[6], (D,), jnp.float32), 0.5, 1.5).astype(jnp.bfloat16),
        "gate_weight": scatter_about(streams_of[7], (D, FF), D ** -0.5, 0.1875, ((1, 2),)),
        "up_weight": scatter_about(streams_of[8], (D, FF), D ** -0.5, 0.1875, ((1, 2),)),
        "down_weight": scatter_about(streams_of[9], (FF, D), FF ** -0.5, 0.078125, ((0, 2),)),
        "cotangent": scatter_about(streams_of[10], (SEQS, SEQ, D), 1.0, 6.0, ((0, 32),)),
    }


EPSILON = 1e-06
ROPE_BASE = 1000000.0
NEG_LARGE = -1e+30

def doc_layout(segments, head_dim):
    length = segments.shape[1]
    places = jnp.arange(length, dtype=jnp.int32)
    same_doc = segments[:, :, None] == segments[:, None, :]
    earlier = places[None, None, :] < places[None, :, None]
    positions = lax.optimization_barrier(jnp.sum(jnp.where(same_doc & earlier, 1.0, 0.0).astype(jnp.float32), axis=2))
    allowed = jnp.where(same_doc & (places[None, None, :] <= places[None, :, None]), 1, 0).astype(jnp.int32)
    half_dim = head_dim // 2
    frequency = ROPE_BASE ** (-2.0 * jnp.arange(half_dim, dtype=jnp.float32) / head_dim)
    angles = positions[:, :, None] * frequency[None, None, :]
    return (allowed, jnp.cos(angles)[:, :, None, :], jnp.sin(angles)[:, :, None, :])

def rotate(values, cosine, sine):
    half_dim = values.shape[-1] // 2
    front_half = values[..., :half_dim]
    back_half = values[..., half_dim:]
    return jnp.concatenate([front_half * cosine - back_half * sine, back_half * cosine + front_half * sine], axis=-1)

def unrotate(gradients, cosine, sine):
    half_dim = gradients.shape[-1] // 2
    front_half = gradients[..., :half_dim]
    back_half = gradients[..., half_dim:]
    return jnp.concatenate([front_half * cosine + back_half * sine, back_half * cosine - front_half * sine], axis=-1)

def inverse_rms(hidden):
    return lax.rsqrt(lax.optimization_barrier(jnp.mean(hidden * hidden, axis=-1, keepdims=True)) + EPSILON)

def norm_backward(hidden, inv_rms, gain_f, back_normed):
    weighted = back_normed * gain_f
    inner = lax.optimization_barrier(jnp.mean(weighted * hidden, axis=-1, keepdims=True))
    back_hidden = inv_rms * weighted - hidden * (inv_rms * inv_rms * inv_rms) * inner
    back_gain = lax.optimization_barrier(jnp.sum(back_normed * hidden * inv_rms, axis=0))
    return (back_hidden, back_gain)

def matmul(left, right):
    return jnp.dot(left, right, preferred_element_type=jnp.float32)

def outer_sum(left, right):
    return lax.dot_general(left, right, (((0,), (0,)), ((), ())), preferred_element_type=jnp.float32)

def times_transposed(left, right):
    return lax.dot_general(left, right, (((1,), (1,)), ((), ())), preferred_element_type=jnp.float32)

def score_block(query_b, keys_b, allowed, score_scale):
    scores = jnp.einsum('sqkgd,spkd->skgqp', query_b.astype(jnp.float32), keys_b.astype(jnp.float32)) * score_scale
    return jnp.where(allowed[:, None, None, :, :] > 0, scores, NEG_LARGE)

def block_pass(tokens, segments, cotangent, params):
    norm1_gain, qkv_weight, qkv_bias, out_weight, norm2_gain, gate_weight, up_weight, down_weight = params
    sequences, length, model_width = tokens.shape
    row_count = sequences * length
    q_width = H * HD
    kv_width = KV * HD
    groups = H // KV
    score_scale = HD ** (-0.5)
    allowed, cosine, sine = doc_layout(segments, HD)
    resid_in = tokens.reshape(row_count, model_width).astype(jnp.float32)
    inv_rms1 = inverse_rms(resid_in)
    gain1 = norm1_gain.astype(jnp.float32)
    normed1 = (resid_in * inv_rms1 * gain1).astype(jnp.bfloat16)
    projected = matmul(normed1, qkv_weight) + qkv_bias.astype(jnp.float32)
    query = projected[:, :q_width].reshape(sequences, length, H, HD)
    keys_raw = projected[:, q_width:q_width + kv_width].reshape(sequences, length, KV, HD)
    values_raw = projected[:, q_width + kv_width:].reshape(sequences, length, KV, HD)
    query_b = rotate(query, cosine, sine).astype(jnp.bfloat16).reshape(sequences, length, KV, groups, HD)
    keys_b = rotate(keys_raw, cosine, sine).astype(jnp.bfloat16)
    values_b = values_raw.astype(jnp.bfloat16)
    scores = score_block(query_b, keys_b, allowed, score_scale)
    top_score = lax.optimization_barrier(jnp.max(scores, axis=-1, keepdims=True))
    log_total = top_score + jnp.log(lax.optimization_barrier(jnp.sum(jnp.exp(scores - top_score), axis=-1, keepdims=True)))
    soft = jnp.exp(scores - log_total)
    soft_b = soft.astype(jnp.bfloat16)
    context = jnp.einsum('skgqp,spkd->sqkgd', soft_b.astype(jnp.float32), values_b.astype(jnp.float32))
    context_b = context.astype(jnp.bfloat16).reshape(row_count, q_width)
    middle = resid_in + matmul(context_b, out_weight)
    inv_rms2 = inverse_rms(middle)
    gain2 = norm2_gain.astype(jnp.float32)
    normed2 = (middle * inv_rms2 * gain2).astype(jnp.bfloat16)
    gate_pre = matmul(normed2, gate_weight)
    up_proj = matmul(normed2, up_weight)
    sigmoid_gate = jax.nn.sigmoid(gate_pre)
    silu_gate = gate_pre * sigmoid_gate
    activ_b = (silu_gate * up_proj).astype(jnp.bfloat16)
    result = middle + matmul(activ_b, down_weight)
    back_rows = cotangent.reshape(row_count, model_width)
    back_activ = times_transposed(back_rows, down_weight)
    back_gate = (back_activ * up_proj * sigmoid_gate * (1.0 + gate_pre * (1.0 - sigmoid_gate))).astype(jnp.bfloat16)
    back_up = (back_activ * silu_gate).astype(jnp.bfloat16)
    grad_down = outer_sum(activ_b, back_rows)
    grad_gate = outer_sum(normed2, back_gate)
    grad_up = outer_sum(normed2, back_up)
    back_normed2 = times_transposed(back_gate, gate_weight) + times_transposed(back_up, up_weight)
    back_norm2, grad_norm2 = norm_backward(middle, inv_rms2, gain2, back_normed2)
    back_middle = back_rows.astype(jnp.float32) + back_norm2
    back_middle_b = back_middle.astype(jnp.bfloat16)
    grad_out = outer_sum(context_b, back_middle_b)
    back_context = times_transposed(back_middle_b, out_weight).astype(jnp.bfloat16)
    back_context = back_context.reshape(sequences, length, KV, groups, HD).astype(jnp.float32)
    back_values = jnp.einsum('skgqp,sqkgd->spkd', soft_b.astype(jnp.float32), back_context)
    back_soft = jnp.einsum('sqkgd,spkd->skgqp', back_context, values_b.astype(jnp.float32))
    row_dot = lax.optimization_barrier(jnp.sum(soft * back_soft, axis=-1, keepdims=True))
    back_scores = (soft * (back_soft - row_dot) * score_scale).astype(jnp.bfloat16).astype(jnp.float32)
    back_query = jnp.einsum('skgqp,spkd->sqkgd', back_scores, keys_b.astype(jnp.float32))
    back_keys = jnp.einsum('skgqp,sqkgd->spkd', back_scores, query_b.astype(jnp.float32))
    back_query = unrotate(back_query.reshape(sequences, length, H, HD), cosine, sine)
    back_keys = unrotate(back_keys, cosine, sine)
    back_proj = jnp.concatenate([back_query.reshape(row_count, q_width), back_keys.reshape(row_count, kv_width), back_values.reshape(row_count, kv_width)], axis=1)
    grad_bias = lax.optimization_barrier(jnp.sum(back_proj, axis=0))
    back_proj_b = back_proj.astype(jnp.bfloat16)
    grad_qkv = outer_sum(normed1, back_proj_b)
    back_normed1 = times_transposed(back_proj_b, qkv_weight)
    back_norm1, grad_norm1 = norm_backward(resid_in, inv_rms1, gain1, back_normed1)
    back_tokens = back_middle + back_norm1
    shape_out = (sequences, length, model_width)
    gradients = (grad_norm1, grad_qkv, grad_bias, grad_out, grad_norm2, grad_gate, grad_up, grad_down)
    return (result.reshape(shape_out), back_tokens.reshape(shape_out), gradients)

def reference(tokens, segments, norm1_gain, qkv_weight, qkv_bias, out_weight, norm2_gain, gate_weight, up_weight, down_weight, cotangent):
    params = (norm1_gain, qkv_weight, qkv_bias, out_weight, norm2_gain, gate_weight, up_weight, down_weight)
    block_seqs = 32 if SEQS % 32 == 0 else SEQS
    block_count = SEQS // block_seqs
    tok_blocks = tokens.reshape(block_count, block_seqs, SEQ, D)
    seg_blocks = segments.reshape(block_count, block_seqs, SEQ)
    cot_blocks = cotangent.reshape(block_count, block_seqs, SEQ, D)
    start = tuple((jnp.zeros(weight.shape, jnp.float32) for weight in params))

    def advance(carry, pieces):
        tok_piece, seg_piece, cot_piece = pieces
        result_piece, back_piece, gradients = block_pass(tok_piece, seg_piece, cot_piece, params)
        return (jax.tree.map(jnp.add, carry, gradients), (result_piece, back_piece))
    totals, outputs = lax.scan(advance, start, (tok_blocks, seg_blocks, cot_blocks))
    result = outputs[0].reshape(SEQS, SEQ, D)
    back_tokens = outputs[1].reshape(SEQS, SEQ, D)
    return (result, back_tokens, totals[0], totals[1], totals[2], totals[3], totals[4], totals[5], totals[6], totals[7])
```

```python
import functools

import jax
import jax.numpy as jnp
from jax import lax
from jax.experimental import pallas as pl
from jax.experimental.pallas import tpu as pltpu
from jax.sharding import PartitionSpec as P

H = 14
KV = 2
HD = 64


EPSILON = 1e-06
ROPE_BASE = 1000000.0
NEG_LARGE = -1e30


def doc_layout(segments, head_dim):
    length = segments.shape[1]
    places = jnp.arange(length, dtype=jnp.int32)
    same_doc = segments[:, :, None] == segments[:, None, :]
    earlier = places[None, None, :] < places[None, :, None]
    positions = jnp.sum(jnp.where(same_doc & earlier, 1.0, 0.0).astype(jnp.float32), axis=2)
    allowed = jnp.where(same_doc & (places[None, None, :] <= places[None, :, None]), 1, 0).astype(
        jnp.int32
    )
    half_dim = head_dim // 2
    frequency = ROPE_BASE ** (-2.0 * jnp.arange(half_dim, dtype=jnp.float32) / head_dim)
    angles = positions[:, :, None] * frequency[None, None, :]
    return (allowed, jnp.cos(angles)[:, :, None, :], jnp.sin(angles)[:, :, None, :])


def rotate(values, cosine, sine):
    half_dim = values.shape[-1] // 2
    front_half = values[..., :half_dim]
    back_half = values[..., half_dim:]
    return jnp.concatenate(
        [front_half * cosine - back_half * sine, back_half * cosine + front_half * sine], axis=-1
    )


def unrotate(gradients, cosine, sine):
    half_dim = gradients.shape[-1] // 2
    front_half = gradients[..., :half_dim]
    back_half = gradients[..., half_dim:]
    return jnp.concatenate(
        [front_half * cosine + back_half * sine, back_half * cosine - front_half * sine], axis=-1
    )


def inverse_rms(hidden):
    return lax.rsqrt(jnp.mean(hidden * hidden, axis=-1, keepdims=True) + EPSILON)


def norm_backward(hidden, inv_rms, gain_f, back_normed):
    weighted = back_normed * gain_f
    inner = jnp.mean(weighted * hidden, axis=-1, keepdims=True)
    back_hidden = inv_rms * weighted - hidden * (inv_rms * inv_rms * inv_rms) * inner
    back_gain = jnp.sum(back_normed * hidden * inv_rms, axis=0)
    return (back_hidden, back_gain)


def matmul(left, right):
    return jnp.dot(left, right, preferred_element_type=jnp.float32)


def outer_sum(left, right):
    return lax.dot_general(
        left, right, (((0,), (0,)), ((), ())), preferred_element_type=jnp.float32
    )


def times_transposed(left, right):
    return lax.dot_general(
        left, right, (((1,), (1,)), ((), ())), preferred_element_type=jnp.float32
    )


def score_block(query_b, keys_b, allowed, score_scale):
    scores = (
        jnp.einsum("sqkgd,spkd->skgqp", query_b, keys_b, preferred_element_type=jnp.float32)
        * score_scale
    )
    return jnp.where(allowed[:, None, None, :, :] > 0, scores, NEG_LARGE)


MESH_ID = pl.DeviceIdType.MESH
TILE = 128
SLICE = 640
CHUNK = 64
SMALL_ROWS = 480


def relative(delta):
    me = lax.axis_index("replica")
    pair = lax.axis_index("group")
    core, x = me % 2, lax.div(me, 2) % 2
    d_core, d_x, d_y = delta % 2, lax.div(delta, 2) % 2, lax.div(delta, 4) % 2
    shift = d_core * (1 - 2 * core) + 2 * d_x * (1 - 2 * x)
    return {"group": pair + d_y * (1 - 2 * pair), "replica": me + shift}


def greet(devices):
    barrier = pltpu.get_barrier_semaphore()
    for device in devices:
        pl.semaphore_signal(barrier, inc=1, device_id=device, device_id_type=MESH_ID)
    return barrier


def remote(src, dst, sems, where, device):
    return pltpu.make_async_remote_copy(
        src_ref=src,
        dst_ref=dst,
        send_sem=sems[0].at[where],
        recv_sem=sems[1].at[where],
        device_id=device,
        device_id_type=MESH_ID,
    )


def contract(left, right, left_dim, right_dim):
    return lax.dot_general(
        left,
        right,
        (((left_dim,), (right_dim,)), ((), ())),
        preferred_element_type=jnp.float32,
    )


def ff_kernel(
    normed_ref,
    cot_ref,
    gate_ref,
    up_ref,
    down_ref,
    result_ref,
    back_ref,
    grads_ref,
    rows_n,
    rows_c,
    w_gate,
    w_up,
    w_down,
    activ,
    d_gate,
    d_up,
    part_b,
    part_r,
    sib_b,
    sib_r,
    land_b,
    land_r,
    total,
    local,
    link,
    core_n,
    core_c,
    core_b,
    core_r,
    link_b,
    link_r,
):
    length, width = normed_ref.shape
    me = lax.axis_index("replica")
    quarter = me % 4
    start = pl.multiple_of(TILE * (5 * quarter - lax.div(quarter, 3)), TILE)
    columns = pl.ds(start, SLICE)
    loads = [
        pltpu.make_async_copy(gate_ref.at[:, columns], w_gate, local.at[0]),
        pltpu.make_async_copy(up_ref.at[:, columns], w_up, local.at[1]),
        pltpu.make_async_copy(down_ref.at[columns, :], w_down, local.at[2]),
    ]
    rows_n[0:length] = normed_ref[...]
    for p in range(4):
        rows_c[2 * p * length : (2 * p + 1) * length] = cot_ref[p]
    barrier = greet([relative(k) for k in (1, 2, 4, 6)])
    pl.semaphore_wait(barrier, 4)

    def block(ref, slot):
        return ref.at[pl.ds(pl.multiple_of(slot * length, 16), length)]

    sends = []
    for p in (1, 2, 3):
        copy = remote(block(rows_n, 0), block(rows_n, 2 * p), link, p, relative(2 * p))
        copy.start()
        sends.append(copy)

    def forward_n(p):
        return remote(
            block(rows_n, 2 * p), block(rows_n, 2 * p + 1), core_n, p, relative(1)
        )

    forward_n(0).start()
    for load in loads:
        load.start()
    shares = []
    for p in range(4):
        copy = remote(block(rows_c, 2 * p), block(rows_c, 2 * p + 1), core_c, p, relative(1))
        copy.start()
        shares.append(copy)
    for load in loads:
        load.wait()

    def pair_step(p, carry):
        @pl.when(p > 0)
        def _():
            arrived = remote(block(rows_n, 0), block(rows_n, 2 * p), link, p, relative(2 * p))
            arrived.wait_recv()
            forward_n(p).start()

        forward_n(p).wait()
        remote(block(rows_c, 2 * p), block(rows_c, 2 * p + 1), core_c, p, relative(1)).wait()
        both = pl.ds(pl.multiple_of(2 * p * length, 32), 2 * length)
        normed, cot = rows_n[both, :], rows_c[both, :]
        gate_pre = contract(normed, w_gate[...], 1, 0)
        up_proj = contract(normed, w_up[...], 1, 0)
        back_activ = contract(cot, w_down[...], 1, 1)
        sigmoid_gate = jax.nn.sigmoid(gate_pre)
        silu_gate = gate_pre * sigmoid_gate
        column = lax.broadcasted_iota(jnp.int32, gate_pre.shape, 1)
        own = column >= jnp.where(quarter == 3, TILE, 0)
        activ[both, :] = jnp.where(own, silu_gate * up_proj, 0.0).astype(jnp.bfloat16)
        d_gate[both, :] = jnp.where(
            own,
            back_activ * up_proj * sigmoid_gate * (1.0 + gate_pre * (1.0 - sigmoid_gate)),
            0.0,
        ).astype(jnp.bfloat16)
        d_up[both, :] = jnp.where(own, back_activ * silu_gate, 0.0).astype(jnp.bfloat16)
        part_b[both, :] = (
            contract(d_gate[both, :], w_gate[...], 1, 1)
            + contract(d_up[both, :], w_up[...], 1, 1)
        ).astype(jnp.bfloat16)
        remote(block(part_b, 2 * p + 1), sib_b.at[p], core_b, p, relative(1)).start()
        part_r[both, :] = contract(activ[both, :], w_down[...], 1, 0).astype(jnp.bfloat16)
        remote(block(part_r, 2 * p + 1), sib_r.at[p], core_r, p, relative(1)).start()
        return carry

    lax.fori_loop(0, 4, pair_step, 0)

    def fold(part, sib, core, land, hop):
        for p in (1, 2, 3, 0):
            remote(block(part, 2 * p + 1), sib.at[p], core, p, relative(1)).wait()
            rows = slice(2 * p * length, (2 * p + 1) * length)
            joined = part[rows, :].astype(jnp.float32) + sib[p].astype(jnp.float32)
            if p == 0:
                total[...] = joined
            else:
                part[rows, :] = joined.astype(jnp.bfloat16)
                remote(block(part, 2 * p), land.at[p - 1], hop, p, relative(2 * p)).start()

    def finish(part, land, hop, goal):
        value = goal[...]
        for p in (1, 2, 3):
            remote(block(part, 2 * p), land.at[p - 1], hop, p, relative(2 * p)).wait()
            value = value + land[p - 1].astype(jnp.float32)
        goal[...] = value

    fold(part_b, sib_b, core_b, land_b, link_b)
    back_ref[...] = total[...]
    fold(part_r, sib_r, core_r, land_r, link_r)
    result_ref[...] = total[...]

    half = width // 2

    def grad_step(h, carry):
        lanes = pl.ds(pl.multiple_of(h * TILE, TILE), TILE)
        left = rows_n[:, lanes]
        grads_ref[pl.ds(pl.multiple_of(h * TILE, TILE), TILE), :] = contract(
            left, d_gate[...], 0, 0
        ).astype(jnp.bfloat16)
        grads_ref[pl.ds(pl.multiple_of(width + h * TILE, TILE), TILE), :] = contract(
            left, d_up[...], 0, 0
        ).astype(jnp.bfloat16)
        down = contract(activ[...], rows_c[:, lanes], 0, 0).astype(jnp.bfloat16)
        for i in range(SLICE // TILE):
            grads_ref[
                pl.ds(pl.multiple_of(2 * width + h * TILE, TILE), TILE), i * TILE : (i + 1) * TILE
            ] = down[i * TILE : (i + 1) * TILE]
        return carry

    lax.fori_loop(0, width // TILE, grad_step, 0)
    finish(part_b, land_b, link_b, back_ref)
    finish(part_r, land_r, link_r, result_ref)
    for copy in sends:
        copy.wait_send()


def feed_forward(normed, cot_slots, gate_weight, up_weight, down_weight):
    length, width = normed.shape
    rows = 8 * length
    bf16, f32 = jnp.bfloat16, jnp.float32
    vmem = pl.BlockSpec(memory_space=pltpu.VMEM)
    hbm = pl.BlockSpec(memory_space=pl.ANY)
    pairs4 = [pltpu.SemaphoreType.DMA((4,)), pltpu.SemaphoreType.DMA((4,))]

    def body(*refs):
        plain, sems = refs[: 8 + 15], refs[8 + 15 :]
        local, rest = sems[0], sems[1:]
        grouped = [(rest[2 * i], rest[2 * i + 1]) for i in range(7)]
        ff_kernel(*plain, local, *grouped)

    return pl.pallas_call(
        body,
        out_shape=[
            jax.ShapeDtypeStruct((length, width), f32),
            jax.ShapeDtypeStruct((length, width), f32),
            jax.ShapeDtypeStruct((3 * width, SLICE), bf16),
        ],
        in_specs=[vmem, vmem, hbm, hbm, hbm],
        out_specs=[vmem, vmem, vmem],
        scratch_shapes=[
            pltpu.VMEM((rows, width), bf16),
            pltpu.VMEM((rows, width), bf16),
            pltpu.VMEM((width, SLICE), bf16),
            pltpu.VMEM((width, SLICE), bf16),
            pltpu.VMEM((SLICE, width), bf16),
            pltpu.VMEM((rows, SLICE), bf16),
            pltpu.VMEM((rows, SLICE), bf16),
            pltpu.VMEM((rows, SLICE), bf16),
            pltpu.VMEM((rows, width), bf16),
            pltpu.VMEM((rows, width), bf16),
            pltpu.VMEM((4, length, width), bf16),
            pltpu.VMEM((4, length, width), bf16),
            pltpu.VMEM((3, length, width), bf16),
            pltpu.VMEM((3, length, width), bf16),
            pltpu.VMEM((length, width), f32),
            pltpu.SemaphoreType.DMA((3,)),
        ]
        + pairs4 * 7,
        compiler_params=pltpu.CompilerParams(
            collective_id=1, has_side_effects=True, vmem_limit_bytes=56 * 1024 * 1024
        ),
        name="feed_forward",
    )(normed, cot_slots, gate_weight, up_weight, down_weight)


def sum_kernel(
    grads_ref,
    small_ref,
    out_ref,
    own,
    land_u,
    land_m,
    total,
    mine,
    sib,
    across,
    beside,
    local,
    early,
    ring,
):
    count = own.shape[0] // CHUNK
    bulk = grads_ref.shape[0]
    first = bulk // CHUNK
    me = lax.axis_index("replica")
    pair = lax.axis_index("group")
    core, x, z = me % 2, lax.div(me, 2) % 2, lax.div(me, 4)
    quarter = me % 4
    beside_quarter = quarter + 2 * (1 - 2 * x)
    middle = (z == 1) | (z == 2)
    is_end = (z == 0) | (z == 3)
    near = {"replica": me + 4 * (1 - 2 * (z % 2))}
    far = {"replica": me + 4 * (1 - 2 * lax.div(z, 2))}
    sibling, neighbour, peer = relative(1), relative(2), relative(4)
    up, mid, down, side, out1, out2 = ring

    half = small_ref.shape[2] // 2

    def halves(which):
        return pl.ds(pl.multiple_of(which * half, 16), half)

    load = pltpu.make_async_copy(grads_ref, own.at[0:bulk], local.at[0])
    load.start()
    load_small = pltpu.make_async_copy(small_ref.at[:, core], mine, local.at[1])
    load_small.start()
    barrier = greet([sibling, neighbour, peer, near])

    @pl.when(middle)
    def _():
        pl.semaphore_signal(barrier, inc=1, device_id=far, device_id_type=MESH_ID)

    pl.semaphore_wait(barrier, jnp.where(middle, 5, 4))

    swap0 = remote(small_ref.at[:, 1 - core], sib, early, 0, sibling)
    swap0.start()
    load.wait()

    def chunk(c):
        return pl.ds(pl.multiple_of(c * CHUNK, CHUNK), CHUNK)

    def up_copy(c):
        return remote(own.at[chunk(c)], land_u.at[chunk(c)], up, c, near)

    def mid_copy(c):
        return remote(own.at[chunk(c)], land_m.at[chunk(c)], mid, c, far)

    def down_copy(c):
        return remote(total.at[chunk(c)], total.at[chunk(c)], down, c, near)

    def side_copy(c):
        return remote(
            total.at[chunk(c)], out_ref.at[quarter].at[chunk(c)], side, c, neighbour
        )

    def side_arrival(c):
        return remote(
            total.at[chunk(c)], out_ref.at[beside_quarter].at[chunk(c)], side, c, neighbour
        )

    def out_copy(c):
        return remote(total.at[chunk(c)], out_ref.at[quarter].at[chunk(c)], out1, c, sibling)

    def pass_copy(c):
        place = out_ref.at[beside_quarter].at[chunk(c)]
        return remote(place, place, out2, c, sibling)

    def store(c):
        return pltpu.make_async_copy(
            total.at[chunk(c)], out_ref.at[quarter].at[chunk(c)], local.at[2 + c]
        )

    def hand_out(c):
        side_copy(c).start()
        out_copy(c).start()
        store(c).start()

    def add(goal, left, right, rows):
        goal[rows, :] = (
            left[rows, :].astype(jnp.float32) + right[rows, :].astype(jnp.float32)
        ).astype(jnp.bfloat16)

    def send_up(lo, hi):
        @pl.when(is_end)
        def _():
            def go(c, carry):
                up_copy(c).start()
                return carry

            lax.fori_loop(lo, hi, go, 0)

    skew1, skew2 = 3, 6

    def service(i, carry):
        a, b, d = i, i - skew1, i - skew2

        @pl.when(middle & (a < count))
        def _():
            up_copy(a).wait_recv()
            add(own, own, land_u, chunk(a))
            mid_copy(a).start()

        @pl.when((b >= 0) & (b < count))
        def _():
            @pl.when(middle)
            def _():
                mid_copy(b).wait_recv()
                add(total, own, land_m, chunk(b))
                down_copy(b).start()

            @pl.when(is_end)
            def _():
                down_copy(b).wait_recv()

            hand_out(b)

        @pl.when(d >= 0)
        def _():
            side_arrival(d).wait_recv()
            pass_copy(d).start()

        return carry

    send_up(0, first)
    load_small.wait()
    swap0.wait()

    def add_small(r, carry):
        rows = pl.ds(pl.multiple_of(r * 48, 16), 48)
        for g in range(2):
            mine[g, rows, :] = (
                mine[g, rows, :].astype(jnp.float32) + sib[g, rows, :].astype(jnp.float32)
            ).astype(jnp.bfloat16)
        return carry

    lax.fori_loop(0, small_ref.shape[2] // 48, add_small, 0)

    def swap_copy(which):
        return remote(
            mine.at[1 - pair].at[halves(which)], across.at[halves(which)], early, 1 + which, peer
        )

    swap_copy(1 - x).start()
    swap_copy(x).start()
    lax.fori_loop(0, 14, service, 0)

    def add_across(which):
        def go(r, carry):
            rows = pl.ds(pl.multiple_of(which * half + r * 48, 16), 48)
            across[rows, :] = (
                across[rows, :].astype(jnp.float32) + mine[pair, rows, :].astype(jnp.float32)
            ).astype(jnp.bfloat16)
            return carry

        lax.fori_loop(0, half // 48, go, 0)

    swap_copy(1 - x).wait()
    add_across(1 - x)
    side_small = remote(across.at[halves(1 - x)], beside, early, 3, neighbour)
    side_small.start()
    lax.fori_loop(14, 28, service, 0)
    swap_copy(x).wait()
    side_small.wait()
    for s in range(half // 48):
        rows = pl.ds(pl.multiple_of(x * half + s * 48, 16), 48)
        value = (
            across[rows, :].astype(jnp.float32)
            + mine[pair, rows, :].astype(jnp.float32)
            + beside[s * 48 : (s + 1) * 48, :].astype(jnp.float32)
        ).astype(jnp.bfloat16)
        for t in range(small_ref.shape[3] // TILE):
            own[bulk + t * 48 : bulk + (t + 1) * 48, s * TILE : (s + 1) * TILE] = value[
                :, t * TILE : (t + 1) * TILE
            ]
    send_up(first, count)
    lax.fori_loop(28, count + skew2, service, 0)

    def drain(c, carry):
        @pl.when(is_end)
        def _():
            up_copy(c).wait_send()

        @pl.when(middle)
        def _():
            mid_copy(c).wait_send()
            down_copy(c).wait_send()

        side_copy(c).wait_send()
        out_copy(c).wait_send()
        out_copy(c).wait_recv()
        pass_copy(c).wait_send()
        pass_copy(c).wait_recv()
        store(c).wait()
        return carry

    lax.fori_loop(0, count, drain, 0)


def replica_sum(grads, small):
    bulk = grads.shape[0]
    rows = bulk + small.shape[2] * small.shape[3] // (2 * SLICE)
    count = rows // CHUNK
    bf16 = jnp.bfloat16
    hbm = pl.BlockSpec(memory_space=pl.ANY)
    lines, half = small.shape[2], small.shape[3]

    def body(*refs):
        plain, sems = refs[:11], refs[11:]
        local, rest = sems[0], sems[1:]
        grouped = [(rest[2 * i], rest[2 * i + 1]) for i in range(7)]
        sum_kernel(*plain, local, grouped[0], grouped[1:])

    return pl.pallas_call(
        body,
        out_shape=jax.ShapeDtypeStruct((4, rows, SLICE), bf16),
        in_specs=[hbm, hbm],
        out_specs=hbm,
        scratch_shapes=[pltpu.VMEM((rows, SLICE), bf16)] * 4
        + [
            pltpu.VMEM((2, lines, half), bf16),
            pltpu.VMEM((2, lines, half), bf16),
            pltpu.VMEM((lines, half), bf16),
            pltpu.VMEM((lines // 2, half), bf16),
            pltpu.SemaphoreType.DMA((2 + count,)),
            pltpu.SemaphoreType.DMA((4,)),
            pltpu.SemaphoreType.DMA((4,)),
        ]
        + [pltpu.SemaphoreType.DMA((count,))] * 12,
        compiler_params=pltpu.CompilerParams(
            collective_id=2, has_side_effects=True, vmem_limit_bytes=56 * 1024 * 1024
        ),
        name="replica_sum",
    )(grads, small)


def fits(pairs, copies, tokens, segments, qkv, out, gate, down):
    return (
        pairs == 2
        and copies == 16
        and tokens.shape == (1, 144, 896)
        and qkv.shape == (448, 1152)
        and out.shape == (448, 896)
        and gate.shape == (896, 2432)
        and down.shape == (2432, 896)
    )


def sum_owned_fast(norm1, norm2, bias, qkv, out, grads):
    bf16 = jnp.bfloat16
    joined = jnp.concatenate([qkv.astype(bf16), out.astype(bf16)], axis=1)
    half = joined.shape[1] // 2
    depth = joined.shape[0] // 2
    extra = SMALL_ROWS - depth
    width = norm1.shape[0]
    gains = jnp.stack([norm1, norm2]).astype(bf16)
    gains = jnp.pad(gains, ((0, extra - 2), (0, half - width)))
    line = jnp.stack([bias[:half], jnp.pad(bias[half:], (0, 2 * half - bias.shape[0]))]).astype(bf16)
    line = jnp.pad(line, ((0, extra - 2), (0, 0)))
    rest = jnp.stack([gains, line])
    small = joined.reshape(2, depth, 2, half).transpose(0, 2, 1, 3)
    small = jnp.concatenate([small, jnp.broadcast_to(rest[None], (2, 2, extra, half))], axis=2)
    full = replica_sum(grads, small)
    f32 = jnp.float32
    bulk = grads.shape[0]

    def columns(first):
        parts = [full[k, first : first + width] for k in range(3)]
        parts.append(full[3, first : first + width, TILE:])
        return jnp.concatenate(parts, axis=1).astype(f32)

    grad_gate, grad_up = columns(0), columns(width)
    tiles = SLICE // TILE
    downs = full[:, 2 * width : bulk].reshape(4, width // TILE, TILE, tiles, TILE)
    downs = downs.transpose(0, 3, 2, 1, 4).reshape(4, SLICE, width)
    grad_down = jnp.concatenate([downs[0], downs[1], downs[2], downs[3, TILE:]], axis=0)
    rows = full[:, bulk:].reshape(2, 2, half // TILE, 48, tiles, TILE)
    rows = rows.transpose(0, 4, 3, 1, 2, 5).reshape(SMALL_ROWS, 2 * half)
    main = rows[:depth]
    group = lax.axis_index("group")

    def mine(v):
        return lax.dynamic_slice_in_dim(v, group * (v.shape[0] // 2), v.shape[0] // 2).astype(f32)

    bias_sum = jnp.concatenate([rows[depth, half:], rows[depth + 1, half:]])[: bias.shape[0]]
    return (
        mine(rows[depth, :width]),
        main[:, : qkv.shape[1]].astype(f32),
        mine(bias_sum),
        main[:, qkv.shape[1] :].astype(f32),
        mine(rows[depth + 1, :width]),
        grad_gate,
        grad_up,
        grad_down.astype(f32),
    )


def swap(values):
    return lax.ppermute(values, "group", [(0, 1), (1, 0)])


def gather_weight(shard, pairs, copies):
    if pairs != 2 or copies % 2:
        return lax.all_gather(shard, "group", axis=0, tiled=True)
    half = shard.shape[0] // 2
    core = lax.axis_index("replica") % 2
    mine = swap(lax.dynamic_slice_in_dim(shard, core * half, half, 0))
    sibling = lax.ppermute(mine, "replica", [(i, i + 1 - 2 * (i % 2)) for i in range(copies)])
    front = jnp.where(core == 0, mine, sibling)
    back = jnp.where(core == 0, sibling, mine)
    first = lax.axis_index("group") == 0
    other = jnp.concatenate([front, back], axis=0)
    return jnp.concatenate(
        [jnp.where(first, shard, other), jnp.where(first, other, shard)], axis=0
    )


def gather_vectors(vectors, pairs):
    if pairs != 2:
        return [lax.all_gather(v, "group", axis=0, tiled=True) for v in vectors]
    joined = jnp.concatenate(vectors)
    other = swap(joined)
    first = lax.axis_index("group") == 0
    low, high = jnp.where(first, joined, other), jnp.where(first, other, joined)
    found, at = [], 0
    for v in vectors:
        size = v.shape[0]
        found.append(jnp.concatenate([low[at : at + size], high[at : at + size]]))
        at += size
    return found


def gather_rows(rows, pairs):
    if pairs != 2:
        return lax.all_gather(rows, "group", axis=0, tiled=True)
    return jnp.concatenate([rows, swap(rows)], axis=0)


def scatter_rows(partial, pairs):
    if pairs != 2:
        return lax.psum_scatter(
            partial.astype(jnp.bfloat16), "group", scatter_dimension=0, tiled=True
        ).astype(jnp.float32)
    half = partial.shape[0] // 2
    return partial[:half] + swap(partial[half:].astype(jnp.bfloat16)).astype(jnp.float32)


def scatter_owned(partial):
    return lax.psum_scatter(
        partial.astype(jnp.bfloat16), "group", scatter_dimension=0, tiled=True
    ).astype(jnp.float32)


def sum_owned(small, qkv, out, gate, up, down):
    owned = [scatter_owned(a) for a in (small, qkv, out)]
    return lax.psum(tuple(a.astype(jnp.bfloat16) for a in (*owned, gate, up, down)), "replica")


def on_device(
    tokens,
    segments,
    norm1_gain,
    qkv_weight,
    qkv_bias,
    out_weight,
    norm2_gain,
    gate_weight,
    up_weight,
    down_weight,
    cotangent,
    *,
    pairs,
    copies,
):
    sequences, length, model_width = tokens.shape
    row_count = sequences * length
    q_width = H * HD
    kv_width = KV * HD
    groups = H // KV
    score_scale = HD ** (-0.5)
    gain1_b, b_qkv, gain2_b = gather_vectors([norm1_gain, qkv_bias, norm2_gain], pairs)
    w_qkv = gather_weight(qkv_weight, pairs, copies)
    fast = fits(
        pairs, copies, tokens, segments, qkv_weight, out_weight, gate_weight, down_weight
    )
    cot_rows = cotangent.reshape(row_count, model_width)
    if fast:
        flips = [(i, i + 2 - 4 * (i // 2 % 2)) for i in range(copies)]
        cot_pair = jnp.stack([cot_rows, lax.ppermute(cot_rows, "replica", flips)])
        cot_slots = jnp.concatenate([cot_pair, swap(cot_pair)])
    else:
        back_all = gather_rows(cot_rows, pairs)
    w_out = gather_weight(out_weight, pairs, copies)
    allowed, cosine, sine = doc_layout(segments, HD)
    resid_in = tokens.reshape(row_count, model_width).astype(jnp.float32)
    inv_rms1 = inverse_rms(resid_in)
    gain1 = gain1_b.astype(jnp.float32)
    normed1 = (resid_in * inv_rms1 * gain1).astype(jnp.bfloat16)
    projected = matmul(normed1, w_qkv) + b_qkv.astype(jnp.float32)
    query = projected[:, :q_width].reshape(sequences, length, H, HD)
    keys_raw = projected[:, q_width : q_width + kv_width].reshape(sequences, length, KV, HD)
    values_raw = projected[:, q_width + kv_width :].reshape(sequences, length, KV, HD)
    query_b = (
        rotate(query, cosine, sine).astype(jnp.bfloat16).reshape(sequences, length, KV, groups, HD)
    )
    keys_b = rotate(keys_raw, cosine, sine).astype(jnp.bfloat16)
    values_b = values_raw.astype(jnp.bfloat16)
    scores = score_block(query_b, keys_b, allowed, score_scale)
    top_score = jnp.max(scores, axis=-1, keepdims=True)
    log_total = top_score + jnp.log(jnp.sum(jnp.exp(scores - top_score), axis=-1, keepdims=True))
    soft_b = jnp.exp(scores - log_total).astype(jnp.bfloat16)
    context = jnp.einsum("skgqp,spkd->sqkgd", soft_b, values_b, preferred_element_type=jnp.float32)
    context_b = context.astype(jnp.bfloat16).reshape(row_count, q_width)
    middle = resid_in + matmul(context_b, w_out)
    inv_rms2 = inverse_rms(middle)
    gain2 = gain2_b.astype(jnp.float32)
    normed2 = (middle * inv_rms2 * gain2).astype(jnp.bfloat16)
    back_rows = cotangent.reshape(row_count, model_width)
    if fast:
        added, back_normed2, grads = feed_forward(
            normed2, cot_slots, gate_weight, up_weight, down_weight
        )
        result = middle + added
    else:
        normed_all = gather_rows(normed2, pairs)
        gate_pre = matmul(normed_all, gate_weight)
        up_proj = matmul(normed_all, up_weight)
        sigmoid_gate = jax.nn.sigmoid(gate_pre)
        silu_gate = gate_pre * sigmoid_gate
        activ_b = (silu_gate * up_proj).astype(jnp.bfloat16)
        result = middle + scatter_rows(matmul(activ_b, down_weight), pairs)
        back_activ = times_transposed(back_all, down_weight)
        back_gate = (
            back_activ * up_proj * sigmoid_gate * (1.0 + gate_pre * (1.0 - sigmoid_gate))
        ).astype(jnp.bfloat16)
        back_up = (back_activ * silu_gate).astype(jnp.bfloat16)
        grad_down = outer_sum(activ_b, back_all)
        grad_gate = outer_sum(normed_all, back_gate)
        grad_up = outer_sum(normed_all, back_up)
        local_normed = times_transposed(back_gate, gate_weight) + times_transposed(back_up, up_weight)
        back_normed2 = scatter_rows(local_normed, pairs)
    back_norm2, grad_norm2_part = norm_backward(middle, inv_rms2, gain2, back_normed2)
    back_middle = back_rows.astype(jnp.float32) + back_norm2
    back_middle_b = back_middle.astype(jnp.bfloat16)
    grad_out_part = outer_sum(context_b, back_middle_b)
    back_context = times_transposed(back_middle_b, w_out).astype(jnp.bfloat16)
    back_context = back_context.reshape(sequences, length, KV, groups, HD)
    soft = jnp.exp(score_block(query_b, keys_b, allowed, score_scale) - log_total)
    soft_again = soft.astype(jnp.bfloat16)
    back_values = jnp.einsum(
        "skgqp,sqkgd->spkd", soft_again, back_context, preferred_element_type=jnp.float32
    )
    back_soft = jnp.einsum(
        "sqkgd,spkd->skgqp", back_context, values_b, preferred_element_type=jnp.float32
    )
    row_dot = jnp.sum(soft * back_soft, axis=-1, keepdims=True)
    back_scores = (soft * (back_soft - row_dot) * score_scale).astype(jnp.bfloat16)
    back_query = jnp.einsum(
        "skgqp,spkd->sqkgd", back_scores, keys_b, preferred_element_type=jnp.float32
    )
    back_keys = jnp.einsum(
        "skgqp,sqkgd->spkd", back_scores, query_b, preferred_element_type=jnp.float32
    )
    back_query = unrotate(back_query.reshape(sequences, length, H, HD), cosine, sine)
    back_keys = unrotate(back_keys, cosine, sine)
    back_proj = jnp.concatenate(
        [
            back_query.reshape(row_count, q_width),
            back_keys.reshape(row_count, kv_width),
            back_values.reshape(row_count, kv_width),
        ],
        axis=1,
    )
    grad_bias_part = jnp.sum(back_proj, axis=0)
    back_proj_b = back_proj.astype(jnp.bfloat16)
    grad_qkv_part = outer_sum(normed1, back_proj_b)
    back_normed1 = times_transposed(back_proj_b, w_qkv)
    back_norm1, grad_norm1_part = norm_backward(resid_in, inv_rms1, gain1, back_normed1)
    back_tokens = back_middle + back_norm1
    shape_out = (sequences, length, model_width)
    if fast:
        return (
            result.reshape(shape_out),
            back_tokens.reshape(shape_out),
            *sum_owned_fast(
                grad_norm1_part,
                grad_norm2_part,
                grad_bias_part,
                grad_qkv_part,
                grad_out_part,
                grads,
            ),
        )
    small = jnp.stack([v.reshape(pairs, -1) for v in (grad_norm1_part, grad_norm2_part)], axis=1)
    small = jnp.concatenate(
        [small.reshape(pairs, -1), grad_bias_part.reshape(pairs, -1)], axis=1
    ).reshape(-1)
    owned = sum_owned(
        small,
        grad_qkv_part,
        grad_out_part,
        grad_gate,
        grad_up,
        grad_down,
    )
    small, grad_qkv, grad_out, grad_gate, grad_up, grad_down = (
        a.astype(jnp.float32) for a in owned
    )
    gains = norm1_gain.shape[0]
    grad_norm1, grad_norm2, grad_bias = (
        small[:gains],
        small[gains : 2 * gains],
        small[2 * gains :],
    )
    return (
        result.reshape(shape_out),
        back_tokens.reshape(shape_out),
        grad_norm1,
        grad_qkv,
        grad_bias,
        grad_out,
        grad_norm2,
        grad_gate,
        grad_up,
        grad_down,
    )


def solution(mesh):
    in_specs = (
        P(("group", "replica"), None, None),
        P(("group", "replica"), None),
        P("group"),
        P("group", None),
        P("group"),
        P("group", None),
        P("group"),
        P(None, "group"),
        P(None, "group"),
        P("group", None),
        P(("group", "replica"), None, None),
    )
    out_specs = (
        P(("group", "replica"), None, None),
        P(("group", "replica"), None, None),
        P("group"),
        P("group", None),
        P("group"),
        P("group", None),
        P("group"),
        P(None, "group"),
        P(None, "group"),
        P("group", None),
    )
    program = functools.partial(
        on_device, pairs=mesh.shape["group"], copies=mesh.shape["replica"]
    )
    return jax.shard_map(
        program, mesh=mesh, in_specs=in_specs, out_specs=out_specs, check_vma=False
    )
```

```python
import functools

import jax
import jax.numpy as jnp
from jax import lax
from jax.experimental import pallas as pl
from jax.experimental.pallas import tpu as pltpu
from jax.sharding import PartitionSpec as P

H = 14
KV = 2
HD = 64


EPSILON = 1e-06
ROPE_BASE = 1000000.0
NEG_LARGE = -1e30


def doc_layout(segments, head_dim):
    length = segments.shape[1]
    places = jnp.arange(length, dtype=jnp.int32)
    same_doc = segments[:, :, None] == segments[:, None, :]
    earlier = places[None, None, :] < places[None, :, None]
    positions = jnp.sum(jnp.where(same_doc & earlier, 1.0, 0.0).astype(jnp.float32), axis=2)
    allowed = jnp.where(same_doc & (places[None, None, :] <= places[None, :, None]), 1, 0).astype(
        jnp.int32
    )
    half_dim = head_dim // 2
    frequency = ROPE_BASE ** (-2.0 * jnp.arange(half_dim, dtype=jnp.float32) / head_dim)
    angles = positions[:, :, None] * frequency[None, None, :]
    return (allowed, jnp.cos(angles)[:, :, None, :], jnp.sin(angles)[:, :, None, :])


def rotate(values, cosine, sine):
    half_dim = values.shape[-1] // 2
    front_half = values[..., :half_dim]
    back_half = values[..., half_dim:]
    return jnp.concatenate(
        [front_half * cosine - back_half * sine, back_half * cosine + front_half * sine], axis=-1
    )


def unrotate(gradients, cosine, sine):
    half_dim = gradients.shape[-1] // 2
    front_half = gradients[..., :half_dim]
    back_half = gradients[..., half_dim:]
    return jnp.concatenate(
        [front_half * cosine + back_half * sine, back_half * cosine - front_half * sine], axis=-1
    )


def inverse_rms(hidden):
    return lax.rsqrt(jnp.mean(hidden * hidden, axis=-1, keepdims=True) + EPSILON)


def norm_backward(hidden, inv_rms, gain_f, back_normed):
    weighted = back_normed * gain_f
    inner = jnp.mean(weighted * hidden, axis=-1, keepdims=True)
    back_hidden = inv_rms * weighted - hidden * (inv_rms * inv_rms * inv_rms) * inner
    back_gain = jnp.sum(back_normed * hidden * inv_rms, axis=0)
    return (back_hidden, back_gain)


def matmul(left, right):
    return jnp.dot(left, right, preferred_element_type=jnp.float32)


def outer_sum(left, right):
    return lax.dot_general(
        left, right, (((0,), (0,)), ((), ())), preferred_element_type=jnp.float32
    )


def times_transposed(left, right):
    return lax.dot_general(
        left, right, (((1,), (1,)), ((), ())), preferred_element_type=jnp.float32
    )


def score_block(query_b, keys_b, allowed, score_scale):
    scores = (
        jnp.einsum("sqkgd,spkd->skgqp", query_b, keys_b, preferred_element_type=jnp.float32)
        * score_scale
    )
    return jnp.where(allowed[:, None, None, :, :] > 0, scores, NEG_LARGE)


MESH_ID = pl.DeviceIdType.MESH
TILE = 128
SLICE = 640
CHUNK = 64
SMALL_ROWS = 480


def relative(delta):
    me = lax.axis_index("replica")
    pair = lax.axis_index("group")
    core, x = me % 2, lax.div(me, 2) % 2
    d_core, d_x, d_y = delta % 2, lax.div(delta, 2) % 2, lax.div(delta, 4) % 2
    shift = d_core * (1 - 2 * core) + 2 * d_x * (1 - 2 * x)
    return {"group": pair + d_y * (1 - 2 * pair), "replica": me + shift}


def greet(devices):
    barrier = pltpu.get_barrier_semaphore()
    for device in devices:
        pl.semaphore_signal(barrier, inc=1, device_id=device, device_id_type=MESH_ID)
    return barrier


def remote(src, dst, sems, where, device):
    return pltpu.make_async_remote_copy(
        src_ref=src,
        dst_ref=dst,
        send_sem=sems[0].at[where],
        recv_sem=sems[1].at[where],
        device_id=device,
        device_id_type=MESH_ID,
    )


def contract(left, right, left_dim, right_dim):
    return lax.dot_general(
        left,
        right,
        (((left_dim,), (right_dim,)), ((), ())),
        preferred_element_type=jnp.float32,
    )


def ff_kernel(
    normed_ref,
    cot_ref,
    gate_ref,
    up_ref,
    down_ref,
    result_ref,
    back_ref,
    grads_ref,
    rows_n,
    rows_c,
    w_gate,
    w_up,
    w_down,
    activ,
    d_gate,
    d_up,
    part_b,
    part_r,
    sib_b,
    sib_r,
    land_b,
    land_r,
    total,
    local,
    link,
    core_n,
    core_c,
    core_b,
    core_r,
    link_b,
    link_r,
):
    length, width = normed_ref.shape
    me = lax.axis_index("replica")
    quarter = me % 4
    start = pl.multiple_of(TILE * (5 * quarter - lax.div(quarter, 3)), TILE)
    columns = pl.ds(start, SLICE)
    loads = [
        pltpu.make_async_copy(gate_ref.at[:, columns], w_gate, local.at[0]),
        pltpu.make_async_copy(up_ref.at[:, columns], w_up, local.at[1]),
        pltpu.make_async_copy(down_ref.at[columns, :], w_down, local.at[2]),
    ]
    rows_n[0:length] = normed_ref[...]
    for p in range(4):
        rows_c[2 * p * length : (2 * p + 1) * length] = cot_ref[p]
    barrier = greet([relative(k) for k in (1, 2, 4, 6)])
    pl.semaphore_wait(barrier, 4)

    def block(ref, slot):
        return ref.at[pl.ds(pl.multiple_of(slot * length, 16), length)]

    sends = []
    for p in (1, 2, 3):
        copy = remote(block(rows_n, 0), block(rows_n, 2 * p), link, p, relative(2 * p))
        copy.start()
        sends.append(copy)

    def forward_n(p):
        return remote(
            block(rows_n, 2 * p), block(rows_n, 2 * p + 1), core_n, p, relative(1)
        )

    forward_n(0).start()
    for load in loads:
        load.start()
    shares = []
    for p in range(4):
        copy = remote(block(rows_c, 2 * p), block(rows_c, 2 * p + 1), core_c, p, relative(1))
        copy.start()
        shares.append(copy)
    for load in loads:
        load.wait()

    def pair_step(p, carry):
        @pl.when(p > 0)
        def _():
            arrived = remote(block(rows_n, 0), block(rows_n, 2 * p), link, p, relative(2 * p))
            arrived.wait_recv()
            forward_n(p).start()

        forward_n(p).wait()
        remote(block(rows_c, 2 * p), block(rows_c, 2 * p + 1), core_c, p, relative(1)).wait()
        both = pl.ds(pl.multiple_of(2 * p * length, 32), 2 * length)
        normed, cot = rows_n[both, :], rows_c[both, :]
        gate_pre = contract(normed, w_gate[...], 1, 0)
        up_proj = contract(normed, w_up[...], 1, 0)
        back_activ = contract(cot, w_down[...], 1, 1)
        sigmoid_gate = jax.nn.sigmoid(gate_pre)
        silu_gate = gate_pre * sigmoid_gate
        column = lax.broadcasted_iota(jnp.int32, gate_pre.shape, 1)
        own = column >= jnp.where(quarter == 3, TILE, 0)
        activ[both, :] = jnp.where(own, silu_gate * up_proj, 0.0).astype(jnp.bfloat16)
        d_gate[both, :] = jnp.where(
            own,
            back_activ * up_proj * sigmoid_gate * (1.0 + gate_pre * (1.0 - sigmoid_gate)),
            0.0,
        ).astype(jnp.bfloat16)
        d_up[both, :] = jnp.where(own, back_activ * silu_gate, 0.0).astype(jnp.bfloat16)
        part_b[both, :] = (
            contract(d_gate[both, :], w_gate[...], 1, 1)
            + contract(d_up[both, :], w_up[...], 1, 1)
        ).astype(jnp.bfloat16)
        remote(block(part_b, 2 * p + 1), sib_b.at[p], core_b, p, relative(1)).start()
        part_r[both, :] = contract(activ[both, :], w_down[...], 1, 0).astype(jnp.bfloat16)
        remote(block(part_r, 2 * p + 1), sib_r.at[p], core_r, p, relative(1)).start()
        return carry

    lax.fori_loop(0, 4, pair_step, 0)

    def fold(part, sib, core, land, hop):
        for p in (1, 2, 3, 0):
            remote(block(part, 2 * p + 1), sib.at[p], core, p, relative(1)).wait()
            rows = slice(2 * p * length, (2 * p + 1) * length)
            joined = part[rows, :].astype(jnp.float32) + sib[p].astype(jnp.float32)
            if p == 0:
                total[...] = joined
            else:
                part[rows, :] = joined.astype(jnp.bfloat16)
                remote(block(part, 2 * p), land.at[p - 1], hop, p, relative(2 * p)).start()

    def finish(part, land, hop, goal):
        value = goal[...]
        for p in (1, 2, 3):
            remote(block(part, 2 * p), land.at[p - 1], hop, p, relative(2 * p)).wait()
            value = value + land[p - 1].astype(jnp.float32)
        goal[...] = value

    fold(part_b, sib_b, core_b, land_b, link_b)
    back_ref[...] = total[...]
    fold(part_r, sib_r, core_r, land_r, link_r)
    result_ref[...] = total[...]

    half = width // 2

    def grad_step(h, carry):
        lanes = pl.ds(pl.multiple_of(h * TILE, TILE), TILE)
        left = rows_n[:, lanes]
        grads_ref[pl.ds(pl.multiple_of(h * TILE, TILE), TILE), :] = contract(
            left, d_gate[...], 0, 0
        ).astype(jnp.bfloat16)
        grads_ref[pl.ds(pl.multiple_of(width + h * TILE, TILE), TILE), :] = contract(
            left, d_up[...], 0, 0
        ).astype(jnp.bfloat16)
        down = contract(activ[...], rows_c[:, lanes], 0, 0).astype(jnp.bfloat16)
        for i in range(SLICE // TILE):
            grads_ref[
                pl.ds(pl.multiple_of(2 * width + h * TILE, TILE), TILE), i * TILE : (i + 1) * TILE
            ] = down[i * TILE : (i + 1) * TILE]
        return carry

    lax.fori_loop(0, width // TILE, grad_step, 0)
    finish(part_b, land_b, link_b, back_ref)
    finish(part_r, land_r, link_r, result_ref)
    for copy in sends:
        copy.wait_send()


def feed_forward(normed, cot_slots, gate_weight, up_weight, down_weight):
    length, width = normed.shape
    rows = 8 * length
    bf16, f32 = jnp.bfloat16, jnp.float32
    vmem = pl.BlockSpec(memory_space=pltpu.VMEM)
    hbm = pl.BlockSpec(memory_space=pl.ANY)
    pairs4 = [pltpu.SemaphoreType.DMA((4,)), pltpu.SemaphoreType.DMA((4,))]

    def body(*refs):
        plain, sems = refs[: 8 + 15], refs[8 + 15 :]
        local, rest = sems[0], sems[1:]
        grouped = [(rest[2 * i], rest[2 * i + 1]) for i in range(7)]
        ff_kernel(*plain, local, *grouped)

    return pl.pallas_call(
        body,
        out_shape=[
            jax.ShapeDtypeStruct((length, width), f32),
            jax.ShapeDtypeStruct((length, width), f32),
            jax.ShapeDtypeStruct((3 * width, SLICE), bf16),
        ],
        in_specs=[vmem, vmem, hbm, hbm, hbm],
        out_specs=[vmem, vmem, vmem],
        scratch_shapes=[
            pltpu.VMEM((rows, width), bf16),
            pltpu.VMEM((rows, width), bf16),
            pltpu.VMEM((width, SLICE), bf16),
            pltpu.VMEM((width, SLICE), bf16),
            pltpu.VMEM((SLICE, width), bf16),
            pltpu.VMEM((rows, SLICE), bf16),
            pltpu.VMEM((rows, SLICE), bf16),
            pltpu.VMEM((rows, SLICE), bf16),
            pltpu.VMEM((rows, width), bf16),
            pltpu.VMEM((rows, width), bf16),
            pltpu.VMEM((4, length, width), bf16),
            pltpu.VMEM((4, length, width), bf16),
            pltpu.VMEM((3, length, width), bf16),
            pltpu.VMEM((3, length, width), bf16),
            pltpu.VMEM((length, width), f32),
            pltpu.SemaphoreType.DMA((3,)),
        ]
        + pairs4 * 7,
        compiler_params=pltpu.CompilerParams(
            collective_id=1, has_side_effects=True, vmem_limit_bytes=56 * 1024 * 1024
        ),
        name="feed_forward",
    )(normed, cot_slots, gate_weight, up_weight, down_weight)


def sum_kernel(
    grads_ref,
    joined_ref,
    rest_ref,
    out_ref,
    own,
    land_u,
    land_m,
    total,
    mine,
    sib,
    across,
    beside,
    local,
    early,
    ring,
):
    count = own.shape[0] // CHUNK
    bulk = grads_ref.shape[0]
    first = bulk // CHUNK
    me = lax.axis_index("replica")
    pair = lax.axis_index("group")
    core, x, z = me % 2, lax.div(me, 2) % 2, lax.div(me, 4)
    quarter = me % 4
    beside_quarter = quarter + 2 * (1 - 2 * x)
    middle = (z == 1) | (z == 2)
    is_end = (z == 0) | (z == 3)
    near = {"replica": me + 4 * (1 - 2 * (z % 2))}
    far = {"replica": me + 4 * (1 - 2 * lax.div(z, 2))}
    sibling, neighbour, peer = relative(1), relative(2), relative(4)
    up, mid, down, side, out1, out2 = ring

    lines, wide = mine.shape[1], mine.shape[2]
    half = lines // 2
    depth = joined_ref.shape[0] // 2

    def halves(which):
        return pl.ds(pl.multiple_of(which * half, 16), half)

    def lanes(which):
        return pl.ds(pl.multiple_of(which * wide, TILE), wide)

    load = pltpu.make_async_copy(grads_ref, own.at[0:bulk], local.at[0])
    load.start()
    small_loads = []
    for g in range(2):
        rows = slice(g * depth, (g + 1) * depth)
        small_loads += [
            pltpu.make_async_copy(
                joined_ref.at[rows, lanes(core)], mine.at[g, 0:depth], local.at[1 + g]
            ),
            pltpu.make_async_copy(rest_ref.at[core], mine.at[g, depth:lines], local.at[3 + g]),
        ]
    for copy in small_loads:
        copy.start()
    barrier = greet([sibling, neighbour, peer, near])

    @pl.when(middle)
    def _():
        pl.semaphore_signal(barrier, inc=1, device_id=far, device_id_type=MESH_ID)

    pl.semaphore_wait(barrier, jnp.where(middle, 5, 4))

    swap0 = []
    for g in range(2):
        rows = slice(g * depth, (g + 1) * depth)
        swap0 += [
            remote(joined_ref.at[rows, lanes(1 - core)], sib.at[g, 0:depth], early, g, sibling),
            remote(rest_ref.at[1 - core], sib.at[g, depth:lines], early, 2 + g, sibling),
        ]
    for copy in swap0:
        copy.start()
    load.wait()

    def chunk(c):
        return pl.ds(pl.multiple_of(c * CHUNK, CHUNK), CHUNK)

    def up_copy(c):
        return remote(own.at[chunk(c)], land_u.at[chunk(c)], up, c, near)

    def mid_copy(c):
        return remote(own.at[chunk(c)], land_m.at[chunk(c)], mid, c, far)

    def down_copy(c):
        return remote(total.at[chunk(c)], total.at[chunk(c)], down, c, near)

    def side_copy(c):
        return remote(
            total.at[chunk(c)], out_ref.at[quarter].at[chunk(c)], side, c, neighbour
        )

    def side_arrival(c):
        return remote(
            total.at[chunk(c)], out_ref.at[beside_quarter].at[chunk(c)], side, c, neighbour
        )

    def out_copy(c):
        return remote(total.at[chunk(c)], out_ref.at[quarter].at[chunk(c)], out1, c, sibling)

    def pass_copy(c):
        place = out_ref.at[beside_quarter].at[chunk(c)]
        return remote(place, place, out2, c, sibling)

    def store(c):
        return pltpu.make_async_copy(
            total.at[chunk(c)], out_ref.at[quarter].at[chunk(c)], local.at[5 + c]
        )

    def hand_out(c):
        side_copy(c).start()
        out_copy(c).start()
        store(c).start()

    def add(goal, left, right, rows):
        goal[rows, :] = (
            left[rows, :].astype(jnp.float32) + right[rows, :].astype(jnp.float32)
        ).astype(jnp.bfloat16)

    def send_up(lo, hi):
        @pl.when(is_end)
        def _():
            def go(c, carry):
                up_copy(c).start()
                return carry

            lax.fori_loop(lo, hi, go, 0)

    skew1, skew2 = 3, 6

    def service(i, carry):
        a, b, d = i, i - skew1, i - skew2

        @pl.when(middle & (a < count))
        def _():
            up_copy(a).wait_recv()
            add(own, own, land_u, chunk(a))
            mid_copy(a).start()

        @pl.when((b >= 0) & (b < count))
        def _():
            @pl.when(middle)
            def _():
                mid_copy(b).wait_recv()
                add(total, own, land_m, chunk(b))
                down_copy(b).start()

            @pl.when(is_end)
            def _():
                down_copy(b).wait_recv()

            hand_out(b)

        @pl.when(d >= 0)
        def _():
            side_arrival(d).wait_recv()
            pass_copy(d).start()

        return carry

    send_up(0, first)
    for copy in small_loads + swap0:
        copy.wait()

    def add_small(r, carry):
        rows = pl.ds(pl.multiple_of(r * 48, 16), 48)
        for g in range(2):
            mine[g, rows, :] = (
                mine[g, rows, :].astype(jnp.float32) + sib[g, rows, :].astype(jnp.float32)
            ).astype(jnp.bfloat16)
        return carry

    lax.fori_loop(0, lines // 48, add_small, 0)

    def swap_copy(which):
        return remote(
            mine.at[1 - pair].at[halves(which)], across.at[halves(which)], early, 4 + which, peer
        )

    swap_copy(1 - x).start()
    swap_copy(x).start()
    lax.fori_loop(0, 14, service, 0)

    def add_across(which):
        def go(r, carry):
            rows = pl.ds(pl.multiple_of(which * half + r * 48, 16), 48)
            across[rows, :] = (
                across[rows, :].astype(jnp.float32) + mine[pair, rows, :].astype(jnp.float32)
            ).astype(jnp.bfloat16)
            return carry

        lax.fori_loop(0, half // 48, go, 0)

    swap_copy(1 - x).wait()
    add_across(1 - x)
    side_small = remote(across.at[halves(1 - x)], beside, early, 6, neighbour)
    side_small.start()
    lax.fori_loop(14, 28, service, 0)
    swap_copy(x).wait()
    side_small.wait()
    for s in range(half // 48):
        rows = pl.ds(pl.multiple_of(x * half + s * 48, 16), 48)
        value = (
            across[rows, :].astype(jnp.float32)
            + mine[pair, rows, :].astype(jnp.float32)
            + beside[s * 48 : (s + 1) * 48, :].astype(jnp.float32)
        ).astype(jnp.bfloat16)
        for t in range(wide // TILE):
            own[bulk + t * 48 : bulk + (t + 1) * 48, s * TILE : (s + 1) * TILE] = value[
                :, t * TILE : (t + 1) * TILE
            ]
    send_up(first, count)
    lax.fori_loop(28, count + skew2, service, 0)

    def drain(c, carry):
        @pl.when(is_end)
        def _():
            up_copy(c).wait_send()

        @pl.when(middle)
        def _():
            mid_copy(c).wait_send()
            down_copy(c).wait_send()

        side_copy(c).wait_send()
        out_copy(c).wait_send()
        out_copy(c).wait_recv()
        pass_copy(c).wait_send()
        pass_copy(c).wait_recv()
        store(c).wait()
        return carry

    lax.fori_loop(0, count, drain, 0)


def replica_sum(grads, joined, rest):
    bulk = grads.shape[0]
    wide = joined.shape[1] // 2
    lines = joined.shape[0] // 2 + rest.shape[1]
    rows = bulk + lines * wide // (2 * SLICE)
    count = rows // CHUNK
    bf16 = jnp.bfloat16
    hbm = pl.BlockSpec(memory_space=pl.ANY)

    def body(*refs):
        plain, sems = refs[:12], refs[12:]
        local, rest_sems = sems[0], sems[1:]
        grouped = [(rest_sems[2 * i], rest_sems[2 * i + 1]) for i in range(7)]
        sum_kernel(*plain, local, grouped[0], grouped[1:])

    return pl.pallas_call(
        body,
        out_shape=jax.ShapeDtypeStruct((4, rows, SLICE), bf16),
        in_specs=[hbm, hbm, hbm],
        out_specs=hbm,
        scratch_shapes=[pltpu.VMEM((rows, SLICE), bf16)] * 4
        + [
            pltpu.VMEM((2, lines, wide), bf16),
            pltpu.VMEM((2, lines, wide), bf16),
            pltpu.VMEM((lines, wide), bf16),
            pltpu.VMEM((lines // 2, wide), bf16),
            pltpu.SemaphoreType.DMA((5 + count,)),
            pltpu.SemaphoreType.DMA((7,)),
            pltpu.SemaphoreType.DMA((7,)),
        ]
        + [pltpu.SemaphoreType.DMA((count,))] * 12,
        compiler_params=pltpu.CompilerParams(
            collective_id=2, has_side_effects=True, vmem_limit_bytes=56 * 1024 * 1024
        ),
        name="replica_sum",
    )(grads, joined, rest)


def unpack_kernel(gate_in, up_in, down_in, small_in, gate, up, down, qkv, out, extra):
    f32 = jnp.float32
    for source, goal in ((gate_in, gate), (up_in, up)):
        for k in range(3):
            goal[:, k * SLICE : (k + 1) * SLICE] = source[k].astype(f32)
        goal[:, 3 * SLICE :] = source[3, :, TILE:].astype(f32)
    tiles = SLICE // TILE
    for k in range(4):
        for i in range(tiles):
            if k == 3 and i == 0:
                continue
            first = (k * tiles + i - k // 3) * TILE
            down[first : first + TILE, :] = down_in[k, :, i * TILE : (i + 1) * TILE].astype(f32)

    @pl.when(pl.program_id(0) == 0)
    def _():
        depth, split = qkv.shape
        lanes = small_in.shape[1] // 48
        for k in range(4):
            for t in range(lanes):
                for s in range(tiles):
                    value = small_in[
                        k, t * 48 : (t + 1) * 48, s * TILE : (s + 1) * TILE
                    ].astype(f32)
                    row, column = k // 2 * tiles * 48 + s * 48, (k % 2 * lanes + t) * TILE
                    keep = min(48, depth - row)
                    if column < split:
                        qkv[row : row + keep, column : column + TILE] = value[:keep]
                    else:
                        at = column - split
                        out[row : row + keep, at : at + TILE] = value[:keep]
                    if keep < 48:
                        extra[:, column : column + TILE] = value[keep:]


def unpack(full, width, qkv_width):
    f32 = jnp.float32
    steps = width // TILE
    features = 4 * SLICE - TILE
    small_rows = full.shape[1] - 3 * width
    depth = width // 2
    whole = lambda i: (0, 0)
    return pl.pallas_call(
        unpack_kernel,
        grid=(steps,),
        out_shape=[
            jax.ShapeDtypeStruct((width, features), f32),
            jax.ShapeDtypeStruct((width, features), f32),
            jax.ShapeDtypeStruct((features, width), f32),
            jax.ShapeDtypeStruct((depth, qkv_width), f32),
            jax.ShapeDtypeStruct((depth, width), f32),
            jax.ShapeDtypeStruct((SMALL_ROWS - depth, qkv_width + width), f32),
        ],
        in_specs=[
            pl.BlockSpec((4, TILE, SLICE), lambda i: (0, i, 0)),
            pl.BlockSpec((4, TILE, SLICE), lambda i: (0, steps + i, 0)),
            pl.BlockSpec((4, TILE, SLICE), lambda i: (0, 2 * steps + i, 0)),
            pl.BlockSpec((4, small_rows, SLICE), lambda i: (0, 3 * width // small_rows, 0)),
        ],
        out_specs=[
            pl.BlockSpec((TILE, features), lambda i: (i, 0)),
            pl.BlockSpec((TILE, features), lambda i: (i, 0)),
            pl.BlockSpec((features, TILE), lambda i: (0, i)),
            pl.BlockSpec((depth, qkv_width), whole),
            pl.BlockSpec((depth, width), whole),
            pl.BlockSpec((SMALL_ROWS - depth, qkv_width + width), whole),
        ],
        compiler_params=pltpu.CompilerParams(vmem_limit_bytes=56 * 1024 * 1024),
        name="unpack",
    )(full, full, full, full)


def fits(pairs, copies, tokens, segments, qkv, out, gate, down):
    return (
        pairs == 2
        and copies == 16
        and tokens.shape == (1, 144, 896)
        and qkv.shape == (448, 1152)
        and out.shape == (448, 896)
        and gate.shape == (896, 2432)
        and down.shape == (2432, 896)
    )


def sum_owned_fast(norm1, norm2, bias, qkv, out, grads):
    bf16 = jnp.bfloat16
    joined = jnp.concatenate([qkv.astype(bf16), out.astype(bf16)], axis=1)
    half = joined.shape[1] // 2
    depth = joined.shape[0] // 2
    extra = SMALL_ROWS - depth
    width = norm1.shape[0]
    gains = jnp.stack([norm1, norm2]).astype(bf16)
    gains = jnp.pad(gains, ((0, extra - 2), (0, half - width)))
    line = jnp.stack([bias[:half], jnp.pad(bias[half:], (0, 2 * half - bias.shape[0]))]).astype(bf16)
    line = jnp.pad(line, ((0, extra - 2), (0, 0)))
    full = replica_sum(grads, joined, jnp.stack([gains, line]))
    gate, up, down, qkv_sum, out_sum, rows = unpack(full, width, qkv.shape[1])
    group = lax.axis_index("group")

    def mine(v):
        return lax.dynamic_slice_in_dim(v, group * (v.shape[0] // 2), v.shape[0] // 2)

    bias_sum = jnp.concatenate([rows[0, half:], rows[1, half:]])[: bias.shape[0]]
    return (
        mine(rows[0, :width]),
        qkv_sum,
        mine(bias_sum),
        out_sum,
        mine(rows[1, :width]),
        gate,
        up,
        down,
    )


def swap(values):
    return lax.ppermute(values, "group", [(0, 1), (1, 0)])


def gather_weight(shard, pairs, copies):
    if pairs != 2 or copies % 2:
        return lax.all_gather(shard, "group", axis=0, tiled=True)
    half = shard.shape[0] // 2
    core = lax.axis_index("replica") % 2
    mine = swap(lax.dynamic_slice_in_dim(shard, core * half, half, 0))
    sibling = lax.ppermute(mine, "replica", [(i, i + 1 - 2 * (i % 2)) for i in range(copies)])
    front = jnp.where(core == 0, mine, sibling)
    back = jnp.where(core == 0, sibling, mine)
    first = lax.axis_index("group") == 0
    other = jnp.concatenate([front, back], axis=0)
    return jnp.concatenate(
        [jnp.where(first, shard, other), jnp.where(first, other, shard)], axis=0
    )


def gather_vectors(vectors, pairs):
    if pairs != 2:
        return [lax.all_gather(v, "group", axis=0, tiled=True) for v in vectors]
    joined = jnp.concatenate(vectors)
    other = swap(joined)
    first = lax.axis_index("group") == 0
    low, high = jnp.where(first, joined, other), jnp.where(first, other, joined)
    found, at = [], 0
    for v in vectors:
        size = v.shape[0]
        found.append(jnp.concatenate([low[at : at + size], high[at : at + size]]))
        at += size
    return found


def gather_rows(rows, pairs):
    if pairs != 2:
        return lax.all_gather(rows, "group", axis=0, tiled=True)
    return jnp.concatenate([rows, swap(rows)], axis=0)


def scatter_rows(partial, pairs):
    if pairs != 2:
        return lax.psum_scatter(
            partial.astype(jnp.bfloat16), "group", scatter_dimension=0, tiled=True
        ).astype(jnp.float32)
    half = partial.shape[0] // 2
    return partial[:half] + swap(partial[half:].astype(jnp.bfloat16)).astype(jnp.float32)


def scatter_owned(partial):
    return lax.psum_scatter(
        partial.astype(jnp.bfloat16), "group", scatter_dimension=0, tiled=True
    ).astype(jnp.float32)


def sum_owned(small, qkv, out, gate, up, down):
    owned = [scatter_owned(a) for a in (small, qkv, out)]
    return lax.psum(tuple(a.astype(jnp.bfloat16) for a in (*owned, gate, up, down)), "replica")


def on_device(
    tokens,
    segments,
    norm1_gain,
    qkv_weight,
    qkv_bias,
    out_weight,
    norm2_gain,
    gate_weight,
    up_weight,
    down_weight,
    cotangent,
    *,
    pairs,
    copies,
):
    sequences, length, model_width = tokens.shape
    row_count = sequences * length
    q_width = H * HD
    kv_width = KV * HD
    groups = H // KV
    score_scale = HD ** (-0.5)
    gain1_b, b_qkv, gain2_b = gather_vectors([norm1_gain, qkv_bias, norm2_gain], pairs)
    w_qkv = gather_weight(qkv_weight, pairs, copies)
    fast = fits(
        pairs, copies, tokens, segments, qkv_weight, out_weight, gate_weight, down_weight
    )
    w_out = gather_weight(out_weight, pairs, copies)
    cot_rows = cotangent.reshape(row_count, model_width)
    if fast:
        flips = [(i, i + 2 - 4 * (i // 2 % 2)) for i in range(copies)]
        cot_pair = jnp.stack([cot_rows, lax.ppermute(cot_rows, "replica", flips)])
        cot_slots = jnp.concatenate([cot_pair, swap(cot_pair)])
    else:
        back_all = gather_rows(cot_rows, pairs)
    allowed, cosine, sine = doc_layout(segments, HD)
    resid_in = tokens.reshape(row_count, model_width).astype(jnp.float32)
    inv_rms1 = inverse_rms(resid_in)
    gain1 = gain1_b.astype(jnp.float32)
    normed1 = (resid_in * inv_rms1 * gain1).astype(jnp.bfloat16)
    projected = matmul(normed1, w_qkv) + b_qkv.astype(jnp.float32)
    query = projected[:, :q_width].reshape(sequences, length, H, HD)
    keys_raw = projected[:, q_width : q_width + kv_width].reshape(sequences, length, KV, HD)
    values_raw = projected[:, q_width + kv_width :].reshape(sequences, length, KV, HD)
    query_b = (
        rotate(query, cosine, sine).astype(jnp.bfloat16).reshape(sequences, length, KV, groups, HD)
    )
    keys_b = rotate(keys_raw, cosine, sine).astype(jnp.bfloat16)
    values_b = values_raw.astype(jnp.bfloat16)
    scores = score_block(query_b, keys_b, allowed, score_scale)
    top_score = jnp.max(scores, axis=-1, keepdims=True)
    log_total = top_score + jnp.log(jnp.sum(jnp.exp(scores - top_score), axis=-1, keepdims=True))
    soft_b = jnp.exp(scores - log_total).astype(jnp.bfloat16)
    context = jnp.einsum("skgqp,spkd->sqkgd", soft_b, values_b, preferred_element_type=jnp.float32)
    context_b = context.astype(jnp.bfloat16).reshape(row_count, q_width)
    middle = resid_in + matmul(context_b, w_out)
    inv_rms2 = inverse_rms(middle)
    gain2 = gain2_b.astype(jnp.float32)
    normed2 = (middle * inv_rms2 * gain2).astype(jnp.bfloat16)
    back_rows = cotangent.reshape(row_count, model_width)
    if fast:
        added, back_normed2, grads = feed_forward(
            normed2, cot_slots, gate_weight, up_weight, down_weight
        )
        result = middle + added
    else:
        normed_all = gather_rows(normed2, pairs)
        gate_pre = matmul(normed_all, gate_weight)
        up_proj = matmul(normed_all, up_weight)
        sigmoid_gate = jax.nn.sigmoid(gate_pre)
        silu_gate = gate_pre * sigmoid_gate
        activ_b = (silu_gate * up_proj).astype(jnp.bfloat16)
        result = middle + scatter_rows(matmul(activ_b, down_weight), pairs)
        back_activ = times_transposed(back_all, down_weight)
        back_gate = (
            back_activ * up_proj * sigmoid_gate * (1.0 + gate_pre * (1.0 - sigmoid_gate))
        ).astype(jnp.bfloat16)
        back_up = (back_activ * silu_gate).astype(jnp.bfloat16)
        grad_down = outer_sum(activ_b, back_all)
        grad_gate = outer_sum(normed_all, back_gate)
        grad_up = outer_sum(normed_all, back_up)
        local_normed = times_transposed(back_gate, gate_weight) + times_transposed(back_up, up_weight)
        back_normed2 = scatter_rows(local_normed, pairs)
    back_norm2, grad_norm2_part = norm_backward(middle, inv_rms2, gain2, back_normed2)
    back_middle = back_rows.astype(jnp.float32) + back_norm2
    back_middle_b = back_middle.astype(jnp.bfloat16)
    grad_out_part = outer_sum(context_b, back_middle_b)
    back_context = times_transposed(back_middle_b, w_out).astype(jnp.bfloat16)
    back_context = back_context.reshape(sequences, length, KV, groups, HD)
    soft = jnp.exp(score_block(query_b, keys_b, allowed, score_scale) - log_total)
    soft_again = soft.astype(jnp.bfloat16)
    back_values = jnp.einsum(
        "skgqp,sqkgd->spkd", soft_again, back_context, preferred_element_type=jnp.float32
    )
    back_soft = jnp.einsum(
        "sqkgd,spkd->skgqp", back_context, values_b, preferred_element_type=jnp.float32
    )
    row_dot = jnp.sum(soft * back_soft, axis=-1, keepdims=True)
    back_scores = (soft * (back_soft - row_dot) * score_scale).astype(jnp.bfloat16)
    back_query = jnp.einsum(
        "skgqp,spkd->sqkgd", back_scores, keys_b, preferred_element_type=jnp.float32
    )
    back_keys = jnp.einsum(
        "skgqp,sqkgd->spkd", back_scores, query_b, preferred_element_type=jnp.float32
    )
    back_query = unrotate(back_query.reshape(sequences, length, H, HD), cosine, sine)
    back_keys = unrotate(back_keys, cosine, sine)
    back_proj = jnp.concatenate(
        [
            back_query.reshape(row_count, q_width),
            back_keys.reshape(row_count, kv_width),
            back_values.reshape(row_count, kv_width),
        ],
        axis=1,
    )
    grad_bias_part = jnp.sum(back_proj, axis=0)
    back_proj_b = back_proj.astype(jnp.bfloat16)
    grad_qkv_part = outer_sum(normed1, back_proj_b)
    back_normed1 = times_transposed(back_proj_b, w_qkv)
    back_norm1, grad_norm1_part = norm_backward(resid_in, inv_rms1, gain1, back_normed1)
    back_tokens = back_middle + back_norm1
    shape_out = (sequences, length, model_width)
    if fast:
        return (
            result.reshape(shape_out),
            back_tokens.reshape(shape_out),
            *sum_owned_fast(
                grad_norm1_part,
                grad_norm2_part,
                grad_bias_part,
                grad_qkv_part,
                grad_out_part,
                grads,
            ),
        )
    small = jnp.stack([v.reshape(pairs, -1) for v in (grad_norm1_part, grad_norm2_part)], axis=1)
    small = jnp.concatenate(
        [small.reshape(pairs, -1), grad_bias_part.reshape(pairs, -1)], axis=1
    ).reshape(-1)
    owned = sum_owned(
        small,
        grad_qkv_part,
        grad_out_part,
        grad_gate,
        grad_up,
        grad_down,
    )
    small, grad_qkv, grad_out, grad_gate, grad_up, grad_down = (
        a.astype(jnp.float32) for a in owned
    )
    gains = norm1_gain.shape[0]
    grad_norm1, grad_norm2, grad_bias = (
        small[:gains],
        small[gains : 2 * gains],
        small[2 * gains :],
    )
    return (
        result.reshape(shape_out),
        back_tokens.reshape(shape_out),
        grad_norm1,
        grad_qkv,
        grad_bias,
        grad_out,
        grad_norm2,
        grad_gate,
        grad_up,
        grad_down,
    )


def solution(mesh):
    in_specs = (
        P(("group", "replica"), None, None),
        P(("group", "replica"), None),
        P("group"),
        P("group", None),
        P("group"),
        P("group", None),
        P("group"),
        P(None, "group"),
        P(None, "group"),
        P("group", None),
        P(("group", "replica"), None, None),
    )
    out_specs = (
        P(("group", "replica"), None, None),
        P(("group", "replica"), None, None),
        P("group"),
        P("group", None),
        P("group"),
        P("group", None),
        P("group"),
        P(None, "group"),
        P(None, "group"),
        P("group", None),
    )
    program = functools.partial(
        on_device, pairs=mesh.shape["group"], copies=mesh.shape["replica"]
    )
    return jax.shard_map(
        program, mesh=mesh, in_specs=in_specs, out_specs=out_specs, check_vma=False
    )
```

```python
import functools

import jax
import jax.numpy as jnp
from jax import lax
from jax.experimental import pallas as pl
from jax.experimental.pallas import tpu as pltpu
from jax.sharding import PartitionSpec as P

H = 14
KV = 2
HD = 64


EPSILON = 1e-06
ROPE_BASE = 1000000.0
NEG_LARGE = -1e30


def doc_layout(segments, head_dim):
    length = segments.shape[1]
    places = jnp.arange(length, dtype=jnp.int32)
    same_doc = segments[:, :, None] == segments[:, None, :]
    earlier = places[None, None, :] < places[None, :, None]
    positions = jnp.sum(jnp.where(same_doc & earlier, 1.0, 0.0).astype(jnp.float32), axis=2)
    allowed = jnp.where(same_doc & (places[None, None, :] <= places[None, :, None]), 1, 0).astype(
        jnp.int32
    )
    half_dim = head_dim // 2
    frequency = ROPE_BASE ** (-2.0 * jnp.arange(half_dim, dtype=jnp.float32) / head_dim)
    angles = positions[:, :, None] * frequency[None, None, :]
    return (allowed, jnp.cos(angles)[:, :, None, :], jnp.sin(angles)[:, :, None, :])


def rotate(values, cosine, sine):
    half_dim = values.shape[-1] // 2
    front_half = values[..., :half_dim]
    back_half = values[..., half_dim:]
    return jnp.concatenate(
        [front_half * cosine - back_half * sine, back_half * cosine + front_half * sine], axis=-1
    )


def unrotate(gradients, cosine, sine):
    half_dim = gradients.shape[-1] // 2
    front_half = gradients[..., :half_dim]
    back_half = gradients[..., half_dim:]
    return jnp.concatenate(
        [front_half * cosine + back_half * sine, back_half * cosine - front_half * sine], axis=-1
    )


def inverse_rms(hidden):
    return lax.rsqrt(jnp.mean(hidden * hidden, axis=-1, keepdims=True) + EPSILON)


def norm_backward(hidden, inv_rms, gain_f, back_normed):
    weighted = back_normed * gain_f
    inner = jnp.mean(weighted * hidden, axis=-1, keepdims=True)
    back_hidden = inv_rms * weighted - hidden * (inv_rms * inv_rms * inv_rms) * inner
    back_gain = jnp.sum(back_normed * hidden * inv_rms, axis=0)
    return (back_hidden, back_gain)


def matmul(left, right):
    return jnp.dot(left, right, preferred_element_type=jnp.float32)


def outer_sum(left, right):
    return lax.dot_general(
        left, right, (((0,), (0,)), ((), ())), preferred_element_type=jnp.float32
    )


def times_transposed(left, right):
    return lax.dot_general(
        left, right, (((1,), (1,)), ((), ())), preferred_element_type=jnp.float32
    )


def score_block(query_b, keys_b, allowed, score_scale):
    scores = (
        jnp.einsum("sqkgd,spkd->skgqp", query_b, keys_b, preferred_element_type=jnp.float32)
        * score_scale
    )
    return jnp.where(allowed[:, None, None, :, :] > 0, scores, NEG_LARGE)


MESH_ID = pl.DeviceIdType.MESH
TILE = 128
SLICE = 640
CHUNK = 64
SMALL_ROWS = 480


def relative(delta):
    me = lax.axis_index("replica")
    pair = lax.axis_index("group")
    core, x = me % 2, lax.div(me, 2) % 2
    d_core, d_x, d_y = delta % 2, lax.div(delta, 2) % 2, lax.div(delta, 4) % 2
    shift = d_core * (1 - 2 * core) + 2 * d_x * (1 - 2 * x)
    return {"group": pair + d_y * (1 - 2 * pair), "replica": me + shift}


def greet(devices):
    barrier = pltpu.get_barrier_semaphore()
    for device in devices:
        pl.semaphore_signal(barrier, inc=1, device_id=device, device_id_type=MESH_ID)
    return barrier


def remote(src, dst, sems, where, device):
    return pltpu.make_async_remote_copy(
        src_ref=src,
        dst_ref=dst,
        send_sem=sems[0].at[where],
        recv_sem=sems[1].at[where],
        device_id=device,
        device_id_type=MESH_ID,
    )


def contract(left, right, left_dim, right_dim):
    return lax.dot_general(
        left,
        right,
        (((left_dim,), (right_dim,)), ((), ())),
        preferred_element_type=jnp.float32,
    )


def layer_kernel(
    normed_ref,
    cot_ref,
    gate_ref,
    up_ref,
    down_ref,
    middle_ref,
    gain1_ref,
    gain2_ref,
    query_ref,
    keys_ref,
    values_ref,
    log_ref,
    allowed_ref,
    cos_ref,
    sin_ref,
    context_ref,
    w_out_ref,
    w_qkv_ref,
    tokens_ref,
    result_ref,
    back_ref,
    out_ref,
    rows_n,
    rows_c,
    w_gate,
    w_up,
    w_down,
    activ,
    d_gate,
    d_up,
    part_b,
    part_r,
    sib_b,
    sib_r,
    land_b,
    land_r,
    own,
    land_u,
    land_m,
    total,
    mine,
    sib,
    across,
    beside,
    joined_ref,
    rest_ref,
    proj,
    stacked,
    normed1,
    share,
    local,
    link,
    core_n,
    core_c,
    core_b,
    core_r,
    link_b,
    link_r,
    early,
    *ring,
):
    f32, bf16 = jnp.float32, jnp.bfloat16
    count = own.shape[0] // CHUNK
    bulk = 3 * normed_ref.shape[1]
    first = bulk // CHUNK
    lines, wide = mine.shape[1], mine.shape[2]
    half = lines // 2
    depth = joined_ref.shape[0] // 2
    me = lax.axis_index("replica")
    pair = lax.axis_index("group")
    core, x, z = me % 2, lax.div(me, 2) % 2, lax.div(me, 4)
    quarter = me % 4
    beside_quarter = quarter + 2 * (1 - 2 * x)
    middle = (z == 1) | (z == 2)
    is_end = (z == 0) | (z == 3)
    near = {"replica": me + 4 * (1 - 2 * (z % 2))}
    far = {"replica": me + 4 * (1 - 2 * lax.div(z, 2))}
    sibling, neighbour, peer = relative(1), relative(2), relative(4)
    up, mid, down, side, out1, out2 = ring


    def halves(which):
        return pl.ds(pl.multiple_of(which * half, 16), half)

    def lanes(which):
        return pl.ds(pl.multiple_of(which * wide, TILE), wide)

    length, width = normed_ref.shape
    first_column = pl.multiple_of(TILE * (5 * quarter - lax.div(quarter, 3)), TILE)
    columns = pl.ds(first_column, SLICE)
    loads = [
        pltpu.make_async_copy(gate_ref.at[:, columns], w_gate, local.at[0]),
        pltpu.make_async_copy(up_ref.at[:, columns], w_up, local.at[1]),
        pltpu.make_async_copy(down_ref.at[columns, :], w_down, local.at[2]),
    ]
    rows_n[0:length] = normed_ref[...]
    for p in range(4):
        rows_c[2 * p * length : (2 * p + 1) * length] = cot_ref[p]
    barrier = greet([sibling, neighbour, peer, relative(6), near])

    @pl.when(middle)
    def _():
        pl.semaphore_signal(barrier, inc=1, device_id=far, device_id_type=MESH_ID)

    pl.semaphore_wait(barrier, jnp.where(middle, 6, 5))

    def block(ref, slot):
        return ref.at[pl.ds(pl.multiple_of(slot * length, 16), length)]

    sends = []
    for p in (1, 2, 3):
        copy = remote(block(rows_n, 0), block(rows_n, 2 * p), link, p, relative(2 * p))
        copy.start()
        sends.append(copy)

    def forward_n(p):
        return remote(
            block(rows_n, 2 * p), block(rows_n, 2 * p + 1), core_n, p, relative(1)
        )

    forward_n(0).start()
    for load in loads:
        load.start()
    shares = []
    for p in range(4):
        copy = remote(block(rows_c, 2 * p), block(rows_c, 2 * p + 1), core_c, p, relative(1))
        copy.start()
        shares.append(copy)
    for load in loads:
        load.wait()

    def pair_step(p, carry):
        @pl.when(p > 0)
        def _():
            arrived = remote(block(rows_n, 0), block(rows_n, 2 * p), link, p, relative(2 * p))
            arrived.wait_recv()
            forward_n(p).start()

        forward_n(p).wait()
        remote(block(rows_c, 2 * p), block(rows_c, 2 * p + 1), core_c, p, relative(1)).wait()
        both = pl.ds(pl.multiple_of(2 * p * length, 32), 2 * length)
        normed, cot = rows_n[both, :], rows_c[both, :]
        gate_pre = contract(normed, w_gate[...], 1, 0)
        up_proj = contract(normed, w_up[...], 1, 0)
        back_activ = contract(cot, w_down[...], 1, 1)
        sigmoid_gate = jax.nn.sigmoid(gate_pre)
        silu_gate = gate_pre * sigmoid_gate
        column = lax.broadcasted_iota(jnp.int32, gate_pre.shape, 1)
        own = column >= jnp.where(quarter == 3, TILE, 0)
        activ[both, :] = jnp.where(own, silu_gate * up_proj, 0.0).astype(jnp.bfloat16)
        d_gate[both, :] = jnp.where(
            own,
            back_activ * up_proj * sigmoid_gate * (1.0 + gate_pre * (1.0 - sigmoid_gate)),
            0.0,
        ).astype(jnp.bfloat16)
        d_up[both, :] = jnp.where(own, back_activ * silu_gate, 0.0).astype(jnp.bfloat16)
        part_b[both, :] = (
            contract(d_gate[both, :], w_gate[...], 1, 1)
            + contract(d_up[both, :], w_up[...], 1, 1)
        ).astype(jnp.bfloat16)
        remote(block(part_b, 2 * p + 1), sib_b.at[p], core_b, p, relative(1)).start()
        part_r[both, :] = contract(activ[both, :], w_down[...], 1, 0).astype(jnp.bfloat16)
        remote(block(part_r, 2 * p + 1), sib_r.at[p], core_r, p, relative(1)).start()
        return carry

    lax.fori_loop(0, 4, pair_step, 0)

    def fold(part, sib, core, land, hop):
        for p in (1, 2, 3, 0):
            remote(block(part, 2 * p + 1), sib.at[p], core, p, relative(1)).wait()
            rows = slice(2 * p * length, (2 * p + 1) * length)
            joined = part[rows, :].astype(jnp.float32) + sib[p].astype(jnp.float32)
            if p == 0:
                total[...] = joined
            else:
                part[rows, :] = joined.astype(jnp.bfloat16)
                remote(block(part, 2 * p), land.at[p - 1], hop, p, relative(2 * p)).start()

    def finish(part, land, hop, goal):
        value = goal[...]
        for p in (1, 2, 3):
            remote(block(part, 2 * p), land.at[p - 1], hop, p, relative(2 * p)).wait()
            value = value + land[p - 1].astype(jnp.float32)
        goal[...] = value

    def chunk(c):
        return pl.ds(pl.multiple_of(c * CHUNK, CHUNK), CHUNK)

    def up_copy(c):
        return remote(own.at[chunk(c)], land_u.at[chunk(c)], up, c, near)

    def mid_copy(c):
        return remote(own.at[chunk(c)], land_m.at[chunk(c)], mid, c, far)

    def down_copy(c):
        return remote(total.at[chunk(c)], total.at[chunk(c)], down, c, near)

    def side_copy(c):
        return remote(
            total.at[chunk(c)], out_ref.at[quarter].at[chunk(c)], side, c, neighbour
        )

    def side_arrival(c):
        return remote(
            total.at[chunk(c)], out_ref.at[beside_quarter].at[chunk(c)], side, c, neighbour
        )

    def out_copy(c):
        return remote(total.at[chunk(c)], out_ref.at[quarter].at[chunk(c)], out1, c, sibling)

    def pass_copy(c):
        place = out_ref.at[beside_quarter].at[chunk(c)]
        return remote(place, place, out2, c, sibling)

    def store(c):
        return pltpu.make_async_copy(
            total.at[chunk(c)], out_ref.at[quarter].at[chunk(c)], local.at[7 + c]
        )

    def hand_out(c):
        side_copy(c).start()
        out_copy(c).start()
        store(c).start()

    def add(goal, left, right, rows):
        goal[rows, :] = (
            left[rows, :].astype(jnp.float32) + right[rows, :].astype(jnp.float32)
        ).astype(jnp.bfloat16)

    def send_up(lo, hi):
        @pl.when(is_end)
        def _():
            def go(c, carry):
                up_copy(c).start()
                return carry

            lax.fori_loop(lo, hi, go, 0)

    skew1, skew2 = 3, 6

    def service(i, carry):
        a, b, d = i, i - skew1, i - skew2

        @pl.when(middle & (a < count))
        def _():
            up_copy(a).wait_recv()
            add(own, own, land_u, chunk(a))
            mid_copy(a).start()

        @pl.when((b >= 0) & (b < count))
        def _():
            @pl.when(middle)
            def _():
                mid_copy(b).wait_recv()
                add(total, own, land_m, chunk(b))
                down_copy(b).start()

            @pl.when(is_end)
            def _():
                down_copy(b).wait_recv()

            hand_out(b)

        @pl.when(d >= 0)
        def _():
            side_arrival(d).wait_recv()
            pass_copy(d).start()

        return carry

    def serve(lo, hi):
        lax.fori_loop(lo, hi, service, 0)

    def fold(part, sib, core, land, hop, goal):
        for p in (1, 2, 3, 0):
            remote(block(part, 2 * p + 1), sib.at[p], core, p, relative(1)).wait()
            rows = slice(2 * p * length, (2 * p + 1) * length)
            joined = part[rows, :].astype(f32) + sib[p].astype(f32)
            if p == 0:
                goal[...] = joined
            else:
                part[rows, :] = joined.astype(bf16)
                remote(block(part, 2 * p), land.at[p - 1], hop, p, relative(2 * p)).start()

    def finish(part, land, hop, goal):
        value = goal[...]
        for p in (1, 2, 3):
            remote(block(part, 2 * p), land.at[p - 1], hop, p, relative(2 * p)).wait()
            value = value + land[p - 1].astype(f32)
        return value

    fold(part_b, sib_b, core_b, land_b, link_b, share)

    def grad_step(h, carry):
        lane = pl.ds(pl.multiple_of(h * TILE, TILE), TILE)
        left = rows_n[:, lane]

        def place(which):
            return pl.ds(pl.multiple_of((3 * h + which) * TILE, TILE), TILE)

        own[place(0), :] = contract(left, d_gate[...], 0, 0).astype(bf16)
        own[place(1), :] = contract(left, d_up[...], 0, 0).astype(bf16)
        down = contract(activ[...], rows_c[:, lane], 0, 0).astype(bf16)
        for i in range(SLICE // TILE):
            own[place(2), i * TILE : (i + 1) * TILE] = down[i * TILE : (i + 1) * TILE]
        per = 3 * TILE // CHUNK
        send_up(h * per, (h + 1) * per)
        return carry

    lax.fori_loop(0, width // TILE, grad_step, 0)
    fold(part_r, sib_r, core_r, land_r, link_r, result_ref)
    back_normed = finish(part_b, land_b, link_b, share)
    serve(0, 2)

    def norm_back(hidden, inv, gain, back):
        weighted = back * gain
        inner = jnp.mean(weighted * hidden, axis=-1, keepdims=True)
        back_hidden = inv * weighted - hidden * (inv * inv * inv) * inner
        return back_hidden, jnp.sum(back * hidden * inv, axis=0, keepdims=True)

    hidden = middle_ref[...]
    back_hidden, sum2 = norm_back(hidden, inverse_rms(hidden), gain2_ref[...], back_normed)
    back_middle = rows_c[0:length, :].astype(f32) + back_hidden
    share[...] = back_middle
    back_middle_b = back_middle.astype(bf16)
    back_context = contract(back_middle_b, w_out_ref[...], 1, 1).astype(bf16)
    groups = H // KV
    for k in range(KV):
        for j in range(groups):
            at = (k * groups + j) * HD
            stacked[k, j * length : (j + 1) * length, :] = back_context[:, at : at + HD]
    joined_ref[:, proj.shape[1] :] = contract(context_ref[...], back_middle_b, 0, 0).astype(bf16)
    serve(2, 3)

    def unturn(value):
        swapped = jnp.concatenate([value[:, HD // 2 :], value[:, : HD // 2]], axis=1)
        return value * cos_ref[...] + swapped * sin_ref[...]

    score_scale = HD ** (-0.5)
    for k in range(KV):
        keys, values, query, back = keys_ref[k], values_ref[k], query_ref[k], stacked[k]
        mask = jnp.concatenate([allowed_ref[...]] * groups, axis=0) > 0
        scores = contract(query, keys, 1, 1) * score_scale
        soft = jnp.exp(jnp.where(mask, scores, NEG_LARGE) - log_ref[k])
        back_soft = contract(back, values, 1, 1)
        row_dot = jnp.sum(soft * back_soft, axis=-1, keepdims=True)
        back_scores = (soft * (back_soft - row_dot) * score_scale).astype(bf16)
        back_values = contract(soft.astype(bf16), back, 0, 0)
        back_query = contract(back_scores, keys, 1, 0)
        back_keys = contract(back_scores, query, 0, 0)
        for j in range(groups):
            at = (k * groups + j) * HD
            proj[:, at : at + HD] = unturn(back_query[j * length : (j + 1) * length, :])
        at = H * HD + k * HD
        proj[:, at : at + HD] = unturn(back_keys)
        proj[:, at + KV * HD : at + (KV + 1) * HD] = back_values
        serve(3 + 2 * k, 5 + 2 * k)

    sum_bias = jnp.sum(proj[...], axis=0, keepdims=True)
    proj_b = proj[...].astype(bf16)
    tokens = tokens_ref[...].astype(f32)
    inv1 = inverse_rms(tokens)
    normed1[...] = (tokens * inv1 * gain1_ref[...]).astype(bf16)
    joined_ref[:, : proj.shape[1]] = contract(normed1[...], proj_b, 0, 0).astype(bf16)
    serve(7, 8)
    back_normed1 = contract(proj_b, w_qkv_ref[...], 1, 1)
    back_first, sum1 = norm_back(tokens, inv1, gain1_ref[...], back_normed1)
    back_ref[...] = share[...] + back_first
    row = lax.broadcasted_iota(jnp.int32, rest_ref.shape[1:], 0)

    def lines_of(top, second):
        pads = [
            jnp.concatenate([v, jnp.zeros((1, wide - v.shape[1]), f32)], axis=1)
            if v.shape[1] < wide
            else v
            for v in (top, second)
        ]
        return jnp.where(row == 0, pads[0], jnp.where(row == 1, pads[1], 0.0)).astype(bf16)

    rest_ref[0] = lines_of(sum1, sum2)
    rest_ref[1] = lines_of(sum_bias[:, :wide], sum_bias[:, wide:])
    small_loads = []
    for g in range(2):
        rows = slice(g * depth, (g + 1) * depth)
        small_loads += [
            pltpu.make_async_copy(
                joined_ref.at[rows, lanes(core)], mine.at[g, 0:depth], local.at[3 + g]
            ),
            pltpu.make_async_copy(rest_ref.at[core], mine.at[g, depth:lines], local.at[5 + g]),
        ]
    for copy in small_loads:
        copy.start()
    swap0 = []
    for g in range(2):
        rows = slice(g * depth, (g + 1) * depth)
        swap0 += [
            remote(joined_ref.at[rows, lanes(1 - core)], sib.at[g, 0:depth], early, g, sibling),
            remote(rest_ref.at[1 - core], sib.at[g, depth:lines], early, 2 + g, sibling),
        ]
    for copy in swap0:
        copy.start()
    serve(8, 10)
    for copy in small_loads + swap0:
        copy.wait()

    def add_small(r, carry):
        rows = pl.ds(pl.multiple_of(r * 48, 16), 48)
        for g in range(2):
            mine[g, rows, :] = (
                mine[g, rows, :].astype(jnp.float32) + sib[g, rows, :].astype(jnp.float32)
            ).astype(jnp.bfloat16)
        return carry

    lax.fori_loop(0, lines // 48, add_small, 0)

    def swap_copy(which):
        return remote(
            mine.at[1 - pair].at[halves(which)], across.at[halves(which)], early, 4 + which, peer
        )

    swap_copy(1 - x).start()
    swap_copy(x).start()
    serve(10, 22)
    result_ref[...] = middle_ref[...] + finish(part_r, land_r, link_r, result_ref)


    def add_across(which):
        def go(r, carry):
            rows = pl.ds(pl.multiple_of(which * half + r * 48, 16), 48)
            across[rows, :] = (
                across[rows, :].astype(jnp.float32) + mine[pair, rows, :].astype(jnp.float32)
            ).astype(jnp.bfloat16)
            return carry

        lax.fori_loop(0, half // 48, go, 0)

    swap_copy(1 - x).wait()
    add_across(1 - x)
    side_small = remote(across.at[halves(1 - x)], beside, early, 6, neighbour)
    side_small.start()
    serve(22, 32)
    swap_copy(x).wait()
    side_small.wait()
    for s in range(half // 48):
        rows = pl.ds(pl.multiple_of(x * half + s * 48, 16), 48)
        value = (
            across[rows, :].astype(jnp.float32)
            + mine[pair, rows, :].astype(jnp.float32)
            + beside[s * 48 : (s + 1) * 48, :].astype(jnp.float32)
        ).astype(jnp.bfloat16)
        for t in range(wide // TILE):
            own[bulk + t * 48 : bulk + (t + 1) * 48, s * TILE : (s + 1) * TILE] = value[
                :, t * TILE : (t + 1) * TILE
            ]
    send_up(first, count)
    serve(32, count + skew2)

    def drain(c, carry):
        @pl.when(is_end)
        def _():
            up_copy(c).wait_send()

        @pl.when(middle)
        def _():
            mid_copy(c).wait_send()
            down_copy(c).wait_send()

        side_copy(c).wait_send()
        out_copy(c).wait_send()
        out_copy(c).wait_recv()
        pass_copy(c).wait_send()
        pass_copy(c).wait_recv()
        store(c).wait()
        return carry

    lax.fori_loop(0, count, drain, 0)


    for copy in sends:
        copy.wait_send()


def layer(*args):
    normed = args[0]
    length, width = normed.shape
    rows = 8 * length
    bf16, f32 = jnp.bfloat16, jnp.float32
    vmem = pl.BlockSpec(memory_space=pltpu.VMEM)
    hbm = pl.BlockSpec(memory_space=pl.ANY)
    w_qkv = args[17]
    wide = (w_qkv.shape[1] + width) // 2
    chain = 3 * width + SMALL_ROWS * wide // (2 * SLICE)
    count = chain // CHUNK
    buffers = [
        ((rows, width), bf16),
        ((rows, width), bf16),
        ((width, SLICE), bf16),
        ((width, SLICE), bf16),
        ((SLICE, width), bf16),
        ((rows, SLICE), bf16),
        ((rows, SLICE), bf16),
        ((rows, SLICE), bf16),
        ((rows, width), bf16),
        ((rows, width), bf16),
        ((4, length, width), bf16),
        ((4, length, width), bf16),
        ((3, length, width), bf16),
        ((3, length, width), bf16),
        ((chain, SLICE), bf16),
        ((chain, SLICE), bf16),
        ((chain, SLICE), bf16),
        ((chain, SLICE), bf16),
        ((2, SMALL_ROWS, wide), bf16),
        ((2, SMALL_ROWS, wide), bf16),
        ((SMALL_ROWS, wide), bf16),
        ((SMALL_ROWS // 2, wide), bf16),
        ((width, 2 * wide), bf16),
        ((2, SMALL_ROWS - width // 2, wide), bf16),
        ((length, w_qkv.shape[1]), f32),
        ((KV, H // KV * length, HD), bf16),
        ((length, width), bf16),
        ((length, width), f32),
    ]
    sizes = [4] * 7 + [7] + [count] * 6

    def body(*refs):
        plain = len(args) + 3 + len(buffers)
        local, rest = refs[plain], refs[plain + 1 :]
        grouped = [(rest[2 * i], rest[2 * i + 1]) for i in range(len(sizes))]
        layer_kernel(*refs[:plain], local, *grouped)

    return pl.pallas_call(
        body,
        out_shape=[
            jax.ShapeDtypeStruct((length, width), f32),
            jax.ShapeDtypeStruct((length, width), f32),
            jax.ShapeDtypeStruct((4, chain, SLICE), bf16),
        ],
        in_specs=[vmem, vmem, hbm, hbm, hbm] + [vmem] * (len(args) - 5),
        out_specs=[vmem, vmem, hbm],
        scratch_shapes=[pltpu.VMEM(shape, kind) for shape, kind in buffers]
        + [pltpu.SemaphoreType.DMA((7 + count,))]
        + [pltpu.SemaphoreType.DMA((size,)) for size in sizes for _ in range(2)],
        compiler_params=pltpu.CompilerParams(
            collective_id=1, has_side_effects=True, vmem_limit_bytes=60 * 1024 * 1024
        ),
        name="layer",
    )(*args)


def unpack_kernel(gate_in, up_in, down_in, small_in, gate, up, down, qkv, out, extra):
    f32 = jnp.float32
    for source, goal in ((gate_in, gate), (up_in, up)):
        for k in range(3):
            goal[:, k * SLICE : (k + 1) * SLICE] = source[k].astype(f32)
        goal[:, 3 * SLICE :] = source[3, :, TILE:].astype(f32)
    tiles = SLICE // TILE
    for k in range(4):
        for i in range(tiles):
            if k == 3 and i == 0:
                continue
            first = (k * tiles + i - k // 3) * TILE
            down[first : first + TILE, :] = down_in[k, :, i * TILE : (i + 1) * TILE].astype(f32)

    @pl.when(pl.program_id(0) == 0)
    def _():
        depth, split = qkv.shape
        lanes = small_in.shape[1] // 48
        for k in range(4):
            for t in range(lanes):
                for s in range(tiles):
                    value = small_in[
                        k, t * 48 : (t + 1) * 48, s * TILE : (s + 1) * TILE
                    ].astype(f32)
                    row, column = k // 2 * tiles * 48 + s * 48, (k % 2 * lanes + t) * TILE
                    keep = min(48, depth - row)
                    if column < split:
                        qkv[row : row + keep, column : column + TILE] = value[:keep]
                    else:
                        at = column - split
                        out[row : row + keep, at : at + TILE] = value[:keep]
                    if keep < 48:
                        extra[:, column : column + TILE] = value[keep:]


def unpack(full, width, qkv_width):
    f32 = jnp.float32
    steps = width // TILE
    features = 4 * SLICE - TILE
    small_rows = full.shape[1] - 3 * width
    depth = width // 2
    whole = lambda i: (0, 0)
    return pl.pallas_call(
        unpack_kernel,
        grid=(steps,),
        out_shape=[
            jax.ShapeDtypeStruct((width, features), f32),
            jax.ShapeDtypeStruct((width, features), f32),
            jax.ShapeDtypeStruct((features, width), f32),
            jax.ShapeDtypeStruct((depth, qkv_width), f32),
            jax.ShapeDtypeStruct((depth, width), f32),
            jax.ShapeDtypeStruct((SMALL_ROWS - depth, qkv_width + width), f32),
        ],
        in_specs=[
            pl.BlockSpec((4, TILE, SLICE), lambda i: (0, 3 * i, 0)),
            pl.BlockSpec((4, TILE, SLICE), lambda i: (0, 3 * i + 1, 0)),
            pl.BlockSpec((4, TILE, SLICE), lambda i: (0, 3 * i + 2, 0)),
            pl.BlockSpec((4, small_rows, SLICE), lambda i: (0, 3 * width // small_rows, 0)),
        ],
        out_specs=[
            pl.BlockSpec((TILE, features), lambda i: (i, 0)),
            pl.BlockSpec((TILE, features), lambda i: (i, 0)),
            pl.BlockSpec((features, TILE), lambda i: (0, i)),
            pl.BlockSpec((depth, qkv_width), whole),
            pl.BlockSpec((depth, width), whole),
            pl.BlockSpec((SMALL_ROWS - depth, qkv_width + width), whole),
        ],
        compiler_params=pltpu.CompilerParams(vmem_limit_bytes=56 * 1024 * 1024),
        name="unpack",
    )(full, full, full, full)


def fits(pairs, copies, tokens, segments, qkv, out, gate, down):
    return (
        pairs == 2
        and copies == 16
        and tokens.shape == (1, 144, 896)
        and qkv.shape == (448, 1152)
        and out.shape == (448, 896)
        and gate.shape == (896, 2432)
        and down.shape == (2432, 896)
    )


def gradients_of(full, width, qkv_width):
    gate, up, down, qkv_sum, out_sum, rows = unpack(full, width, qkv_width)
    half = rows.shape[1] // 2
    group = lax.axis_index("group")

    def mine(v):
        return lax.dynamic_slice_in_dim(v, group * (v.shape[0] // 2), v.shape[0] // 2)

    bias_sum = jnp.concatenate([rows[0, half:], rows[1, half:]])[:qkv_width]
    return (
        mine(rows[0, :width]),
        qkv_sum,
        mine(bias_sum),
        out_sum,
        mine(rows[1, :width]),
        gate,
        up,
        down,
    )


def swap(values):
    return lax.ppermute(values, "group", [(0, 1), (1, 0)])


def gather_weight(shard, pairs, copies):
    if pairs != 2 or copies % 2:
        return lax.all_gather(shard, "group", axis=0, tiled=True)
    half = shard.shape[0] // 2
    core = lax.axis_index("replica") % 2
    mine = swap(lax.dynamic_slice_in_dim(shard, core * half, half, 0))
    sibling = lax.ppermute(mine, "replica", [(i, i + 1 - 2 * (i % 2)) for i in range(copies)])
    front = jnp.where(core == 0, mine, sibling)
    back = jnp.where(core == 0, sibling, mine)
    first = lax.axis_index("group") == 0
    other = jnp.concatenate([front, back], axis=0)
    return jnp.concatenate(
        [jnp.where(first, shard, other), jnp.where(first, other, shard)], axis=0
    )


def gather_vectors(vectors, pairs):
    if pairs != 2:
        return [lax.all_gather(v, "group", axis=0, tiled=True) for v in vectors]
    joined = jnp.concatenate(vectors)
    other = swap(joined)
    first = lax.axis_index("group") == 0
    low, high = jnp.where(first, joined, other), jnp.where(first, other, joined)
    found, at = [], 0
    for v in vectors:
        size = v.shape[0]
        found.append(jnp.concatenate([low[at : at + size], high[at : at + size]]))
        at += size
    return found


def gather_rows(rows, pairs):
    if pairs != 2:
        return lax.all_gather(rows, "group", axis=0, tiled=True)
    return jnp.concatenate([rows, swap(rows)], axis=0)


def scatter_rows(partial, pairs):
    if pairs != 2:
        return lax.psum_scatter(
            partial.astype(jnp.bfloat16), "group", scatter_dimension=0, tiled=True
        ).astype(jnp.float32)
    half = partial.shape[0] // 2
    return partial[:half] + swap(partial[half:].astype(jnp.bfloat16)).astype(jnp.float32)


def scatter_owned(partial):
    return lax.psum_scatter(
        partial.astype(jnp.bfloat16), "group", scatter_dimension=0, tiled=True
    ).astype(jnp.float32)


def sum_owned(small, qkv, out, gate, up, down):
    owned = [scatter_owned(a) for a in (small, qkv, out)]
    return lax.psum(tuple(a.astype(jnp.bfloat16) for a in (*owned, gate, up, down)), "replica")


def on_device(
    tokens,
    segments,
    norm1_gain,
    qkv_weight,
    qkv_bias,
    out_weight,
    norm2_gain,
    gate_weight,
    up_weight,
    down_weight,
    cotangent,
    *,
    pairs,
    copies,
):
    sequences, length, model_width = tokens.shape
    row_count = sequences * length
    q_width = H * HD
    kv_width = KV * HD
    groups = H // KV
    score_scale = HD ** (-0.5)
    gain1_b, b_qkv, gain2_b = gather_vectors([norm1_gain, qkv_bias, norm2_gain], pairs)
    w_qkv = gather_weight(qkv_weight, pairs, copies)
    fast = fits(
        pairs, copies, tokens, segments, qkv_weight, out_weight, gate_weight, down_weight
    )
    w_out = gather_weight(out_weight, pairs, copies)
    cot_rows = cotangent.reshape(row_count, model_width)
    if fast:
        flips = [(i, i + 2 - 4 * (i // 2 % 2)) for i in range(copies)]
        cot_pair = jnp.stack([cot_rows, lax.ppermute(cot_rows, "replica", flips)])
        cot_slots = jnp.concatenate([cot_pair, swap(cot_pair)])
    else:
        back_all = gather_rows(cot_rows, pairs)
    allowed, cosine, sine = doc_layout(segments, HD)
    resid_in = tokens.reshape(row_count, model_width).astype(jnp.float32)
    inv_rms1 = inverse_rms(resid_in)
    gain1 = gain1_b.astype(jnp.float32)
    normed1 = (resid_in * inv_rms1 * gain1).astype(jnp.bfloat16)
    projected = matmul(normed1, w_qkv) + b_qkv.astype(jnp.float32)
    query = projected[:, :q_width].reshape(sequences, length, H, HD)
    keys_raw = projected[:, q_width : q_width + kv_width].reshape(sequences, length, KV, HD)
    values_raw = projected[:, q_width + kv_width :].reshape(sequences, length, KV, HD)
    query_b = (
        rotate(query, cosine, sine).astype(jnp.bfloat16).reshape(sequences, length, KV, groups, HD)
    )
    keys_b = rotate(keys_raw, cosine, sine).astype(jnp.bfloat16)
    values_b = values_raw.astype(jnp.bfloat16)
    scores = score_block(query_b, keys_b, allowed, score_scale)
    top_score = jnp.max(scores, axis=-1, keepdims=True)
    log_total = top_score + jnp.log(jnp.sum(jnp.exp(scores - top_score), axis=-1, keepdims=True))
    soft_b = jnp.exp(scores - log_total).astype(jnp.bfloat16)
    context = jnp.einsum("skgqp,spkd->sqkgd", soft_b, values_b, preferred_element_type=jnp.float32)
    context_b = context.astype(jnp.bfloat16).reshape(row_count, q_width)
    middle = resid_in + matmul(context_b, w_out)
    inv_rms2 = inverse_rms(middle)
    gain2 = gain2_b.astype(jnp.float32)
    normed2 = (middle * inv_rms2 * gain2).astype(jnp.bfloat16)
    back_rows = cotangent.reshape(row_count, model_width)
    if fast:
        shape_out = (sequences, length, model_width)
        stack = query_b[0].transpose(1, 2, 0, 3).reshape(KV, groups * length, HD)
        turn = jnp.concatenate([cosine[0, :, 0, :]] * 2, axis=1)
        unturn = jnp.concatenate([sine[0, :, 0, :], -sine[0, :, 0, :]], axis=1)
        result, back_tokens, full = layer(
            normed2,
            cot_slots,
            gate_weight,
            up_weight,
            down_weight,
            middle,
            gain1[None],
            gain2[None],
            stack,
            keys_b[0].transpose(1, 0, 2),
            values_b[0].transpose(1, 0, 2),
            log_total[0].reshape(KV, groups * length, 1),
            allowed[0],
            turn,
            unturn,
            context_b,
            w_out,
            w_qkv,
            tokens.reshape(row_count, model_width),
        )
        return (
            result.reshape(shape_out),
            back_tokens.reshape(shape_out),
            *gradients_of(full, model_width, w_qkv.shape[1]),
        )
    normed_all = gather_rows(normed2, pairs)
    gate_pre = matmul(normed_all, gate_weight)
    up_proj = matmul(normed_all, up_weight)
    sigmoid_gate = jax.nn.sigmoid(gate_pre)
    silu_gate = gate_pre * sigmoid_gate
    activ_b = (silu_gate * up_proj).astype(jnp.bfloat16)
    result = middle + scatter_rows(matmul(activ_b, down_weight), pairs)
    back_activ = times_transposed(back_all, down_weight)
    back_gate = (
        back_activ * up_proj * sigmoid_gate * (1.0 + gate_pre * (1.0 - sigmoid_gate))
    ).astype(jnp.bfloat16)
    back_up = (back_activ * silu_gate).astype(jnp.bfloat16)
    grad_down = outer_sum(activ_b, back_all)
    grad_gate = outer_sum(normed_all, back_gate)
    grad_up = outer_sum(normed_all, back_up)
    local_normed = times_transposed(back_gate, gate_weight) + times_transposed(back_up, up_weight)
    back_normed2 = scatter_rows(local_normed, pairs)
    back_norm2, grad_norm2_part = norm_backward(middle, inv_rms2, gain2, back_normed2)
    back_middle = back_rows.astype(jnp.float32) + back_norm2
    back_middle_b = back_middle.astype(jnp.bfloat16)
    grad_out_part = outer_sum(context_b, back_middle_b)
    back_context = times_transposed(back_middle_b, w_out).astype(jnp.bfloat16)
    back_context = back_context.reshape(sequences, length, KV, groups, HD)
    soft = jnp.exp(score_block(query_b, keys_b, allowed, score_scale) - log_total)
    soft_again = soft.astype(jnp.bfloat16)
    back_values = jnp.einsum(
        "skgqp,sqkgd->spkd", soft_again, back_context, preferred_element_type=jnp.float32
    )
    back_soft = jnp.einsum(
        "sqkgd,spkd->skgqp", back_context, values_b, preferred_element_type=jnp.float32
    )
    row_dot = jnp.sum(soft * back_soft, axis=-1, keepdims=True)
    back_scores = (soft * (back_soft - row_dot) * score_scale).astype(jnp.bfloat16)
    back_query = jnp.einsum(
        "skgqp,spkd->sqkgd", back_scores, keys_b, preferred_element_type=jnp.float32
    )
    back_keys = jnp.einsum(
        "skgqp,sqkgd->spkd", back_scores, query_b, preferred_element_type=jnp.float32
    )
    back_query = unrotate(back_query.reshape(sequences, length, H, HD), cosine, sine)
    back_keys = unrotate(back_keys, cosine, sine)
    back_proj = jnp.concatenate(
        [
            back_query.reshape(row_count, q_width),
            back_keys.reshape(row_count, kv_width),
            back_values.reshape(row_count, kv_width),
        ],
        axis=1,
    )
    grad_bias_part = jnp.sum(back_proj, axis=0)
    back_proj_b = back_proj.astype(jnp.bfloat16)
    grad_qkv_part = outer_sum(normed1, back_proj_b)
    back_normed1 = times_transposed(back_proj_b, w_qkv)
    back_norm1, grad_norm1_part = norm_backward(resid_in, inv_rms1, gain1, back_normed1)
    back_tokens = back_middle + back_norm1
    small = jnp.stack([v.reshape(pairs, -1) for v in (grad_norm1_part, grad_norm2_part)], axis=1)
    small = jnp.concatenate(
        [small.reshape(pairs, -1), grad_bias_part.reshape(pairs, -1)], axis=1
    ).reshape(-1)
    owned = sum_owned(
        small,
        grad_qkv_part,
        grad_out_part,
        grad_gate,
        grad_up,
        grad_down,
    )
    small, grad_qkv, grad_out, grad_gate, grad_up, grad_down = (
        a.astype(jnp.float32) for a in owned
    )
    gains = norm1_gain.shape[0]
    grad_norm1, grad_norm2, grad_bias = (
        small[:gains],
        small[gains : 2 * gains],
        small[2 * gains :],
    )
    shape_out = (sequences, length, model_width)
    return (
        result.reshape(shape_out),
        back_tokens.reshape(shape_out),
        grad_norm1,
        grad_qkv,
        grad_bias,
        grad_out,
        grad_norm2,
        grad_gate,
        grad_up,
        grad_down,
    )


def solution(mesh):
    in_specs = (
        P(("group", "replica"), None, None),
        P(("group", "replica"), None),
        P("group"),
        P("group", None),
        P("group"),
        P("group", None),
        P("group"),
        P(None, "group"),
        P(None, "group"),
        P("group", None),
        P(("group", "replica"), None, None),
    )
    out_specs = (
        P(("group", "replica"), None, None),
        P(("group", "replica"), None, None),
        P("group"),
        P("group", None),
        P("group"),
        P("group", None),
        P("group"),
        P(None, "group"),
        P(None, "group"),
        P("group", None),
    )
    program = functools.partial(
        on_device, pairs=mesh.shape["group"], copies=mesh.shape["replica"]
    )
    return jax.shard_map(
        program, mesh=mesh, in_specs=in_specs, out_specs=out_specs, check_vma=False
    )
```

```python
import functools

import jax
import jax.numpy as jnp
from jax import lax
from jax.experimental import pallas as pl
from jax.experimental.pallas import tpu as pltpu
from jax.sharding import PartitionSpec as P

H = 14
KV = 2
HD = 64


EPSILON = 1e-06
ROPE_BASE = 1000000.0
NEG_LARGE = -1e30


def doc_layout(segments, head_dim):
    length = segments.shape[1]
    places = jnp.arange(length, dtype=jnp.int32)
    same_doc = segments[:, :, None] == segments[:, None, :]
    earlier = places[None, None, :] < places[None, :, None]
    positions = jnp.sum(jnp.where(same_doc & earlier, 1.0, 0.0).astype(jnp.float32), axis=2)
    allowed = jnp.where(same_doc & (places[None, None, :] <= places[None, :, None]), 1, 0).astype(
        jnp.int32
    )
    half_dim = head_dim // 2
    frequency = ROPE_BASE ** (-2.0 * jnp.arange(half_dim, dtype=jnp.float32) / head_dim)
    angles = positions[:, :, None] * frequency[None, None, :]
    return (allowed, jnp.cos(angles)[:, :, None, :], jnp.sin(angles)[:, :, None, :])


def rotate(values, cosine, sine):
    half_dim = values.shape[-1] // 2
    front_half = values[..., :half_dim]
    back_half = values[..., half_dim:]
    return jnp.concatenate(
        [front_half * cosine - back_half * sine, back_half * cosine + front_half * sine], axis=-1
    )


def unrotate(gradients, cosine, sine):
    half_dim = gradients.shape[-1] // 2
    front_half = gradients[..., :half_dim]
    back_half = gradients[..., half_dim:]
    return jnp.concatenate(
        [front_half * cosine + back_half * sine, back_half * cosine - front_half * sine], axis=-1
    )


def inverse_rms(hidden):
    return lax.rsqrt(jnp.mean(hidden * hidden, axis=-1, keepdims=True) + EPSILON)


def norm_backward(hidden, inv_rms, gain_f, back_normed):
    weighted = back_normed * gain_f
    inner = jnp.mean(weighted * hidden, axis=-1, keepdims=True)
    back_hidden = inv_rms * weighted - hidden * (inv_rms * inv_rms * inv_rms) * inner
    back_gain = jnp.sum(back_normed * hidden * inv_rms, axis=0)
    return (back_hidden, back_gain)


def matmul(left, right):
    return jnp.dot(left, right, preferred_element_type=jnp.float32)


def outer_sum(left, right):
    return lax.dot_general(
        left, right, (((0,), (0,)), ((), ())), preferred_element_type=jnp.float32
    )


def times_transposed(left, right):
    return lax.dot_general(
        left, right, (((1,), (1,)), ((), ())), preferred_element_type=jnp.float32
    )


def score_block(query_b, keys_b, allowed, score_scale):
    scores = (
        jnp.einsum("sqkgd,spkd->skgqp", query_b, keys_b, preferred_element_type=jnp.float32)
        * score_scale
    )
    return jnp.where(allowed[:, None, None, :, :] > 0, scores, NEG_LARGE)


MESH_ID = pl.DeviceIdType.MESH
TILE = 128
SLICE = 640
CHUNK = 64
SMALL_ROWS = 480


def relative(delta):
    me = lax.axis_index("replica")
    pair = lax.axis_index("group")
    core, x = me % 2, lax.div(me, 2) % 2
    d_core, d_x, d_y = delta % 2, lax.div(delta, 2) % 2, lax.div(delta, 4) % 2
    shift = d_core * (1 - 2 * core) + 2 * d_x * (1 - 2 * x)
    return {"group": pair + d_y * (1 - 2 * pair), "replica": me + shift}


def greet(devices):
    barrier = pltpu.get_barrier_semaphore()
    for device in devices:
        pl.semaphore_signal(barrier, inc=1, device_id=device, device_id_type=MESH_ID)
    return barrier


def remote(src, dst, sems, where, device):
    return pltpu.make_async_remote_copy(
        src_ref=src,
        dst_ref=dst,
        send_sem=sems[0].at[where],
        recv_sem=sems[1].at[where],
        device_id=device,
        device_id_type=MESH_ID,
    )


def contract(left, right, left_dim, right_dim):
    return lax.dot_general(
        left,
        right,
        (((left_dim,), (right_dim,)), ((), ())),
        preferred_element_type=jnp.float32,
    )


def layer_kernel(
    tokens_ref,
    seg_column,
    seg_row,
    frequency,
    vector_ref,
    cot_ref,
    qkv_ref,
    out_weight_ref,
    gate_ref,
    up_ref,
    down_ref,
    result_ref,
    back_ref,
    out_ref,
    rows_n,
    rows_c,
    w_gate,
    w_up,
    w_down,
    activ,
    d_gate,
    d_up,
    part_b,
    part_r,
    sib_b,
    sib_r,
    land_b,
    land_r,
    own,
    land_u,
    land_m,
    total,
    mine,
    sib,
    across,
    beside,
    joined_ref,
    rest_ref,
    proj,
    stacked,
    normed1,
    share,
    w_qkv_ref,
    w_out_ref,
    vectors,
    query_ref,
    keys_ref,
    values_ref,
    log_ref,
    allowed_ref,
    cos_ref,
    sin_ref,
    context_ref,
    middle_ref,
    gain1_ref,
    gain2_ref,
    local,
    link,
    core_n,
    core_c,
    core_b,
    core_r,
    link_b,
    link_r,
    early,
    up,
    mid,
    down,
    side,
    out1,
    out2,
    link_c,
    weights_y,
    weights_x,
    weights_1,
    weights_2,
):
    f32, bf16 = jnp.float32, jnp.bfloat16
    count = own.shape[0] // CHUNK
    length, width = tokens_ref.shape
    bulk = 3 * width
    first = bulk // CHUNK
    lines, wide = mine.shape[1], mine.shape[2]
    half = lines // 2
    depth = joined_ref.shape[0] // 2
    me = lax.axis_index("replica")
    pair = lax.axis_index("group")
    core, x, z = me % 2, lax.div(me, 2) % 2, lax.div(me, 4)
    quarter = me % 4
    beside_quarter = quarter + 2 * (1 - 2 * x)
    middle = (z == 1) | (z == 2)
    is_end = (z == 0) | (z == 3)
    near = {"replica": me + 4 * (1 - 2 * (z % 2))}
    far = {"replica": me + 4 * (1 - 2 * lax.div(z, 2))}
    sibling, neighbour, peer = relative(1), relative(2), relative(4)


    def halves(which):
        return pl.ds(pl.multiple_of(which * half, 16), half)

    def lanes(which):
        return pl.ds(pl.multiple_of(which * wide, TILE), wide)

    first_column = pl.multiple_of(TILE * (5 * quarter - lax.div(quarter, 3)), TILE)
    columns = pl.ds(first_column, SLICE)
    loads = [
        pltpu.make_async_copy(gate_ref.at[:, columns], w_gate, local.at[0]),
        pltpu.make_async_copy(up_ref.at[:, columns], w_up, local.at[1]),
        pltpu.make_async_copy(down_ref.at[columns, :], w_down, local.at[2]),
    ]
    shard = width // 2
    w_loads = [
        pltpu.make_async_copy(
            qkv_ref, w_qkv_ref.at[pl.ds(pl.multiple_of(pair * shard, 64), shard)], local.at[3]
        ),
        pltpu.make_async_copy(
            out_weight_ref, w_out_ref.at[pl.ds(pl.multiple_of(pair * shard, 64), shard)], local.at[4]
        ),
    ]
    for load in w_loads:
        load.start()
    rows_c[0:length] = cot_ref[...]
    barrier = greet([sibling, neighbour, peer, relative(6), near])

    @pl.when(middle)
    def _():
        pl.semaphore_signal(barrier, inc=1, device_id=far, device_id_type=MESH_ID)

    pl.semaphore_wait(barrier, jnp.where(middle, 6, 5))

    def block(ref, slot):
        return ref.at[pl.ds(pl.multiple_of(slot * length, 16), length)]

    part = shard // 4
    cuts = ((0, 48), (48, part - 48))
    vector_copy = remote(vector_ref, vectors, early, 7, peer)
    vector_copy.start()

    def quarter_rows(which, fourth, cut):
        first = which * shard + fourth * part + cuts[cut][0]
        return pl.ds(pl.multiple_of(first, 16), cuts[cut][1])

    moved = [(qkv_ref, w_qkv_ref, 0), (out_weight_ref, w_out_ref, 1)]

    def weight_y(w, cut):
        source, goal, _ = moved[w]
        rows = pl.ds(pl.multiple_of(quarter * part + cuts[cut][0], 16), cuts[cut][1])
        return remote(
            source.at[rows], goal.at[quarter_rows(pair, quarter, cut)], weights_y, 2 * w + cut, peer
        )

    def weight_y_in(w, cut):
        goal = moved[w][1].at[quarter_rows(1 - pair, quarter, cut)]
        return remote(goal, goal, weights_y, 2 * w + cut, peer)

    def weight_pass(w, cut, fourth, sems, device):
        goal = moved[w][1].at[quarter_rows(1 - pair, fourth, cut)]
        return remote(goal, goal, sems, 2 * w + cut, device)

    order = [(w, cut) for w in range(2) for cut in range(2)]
    for w, cut in order:
        weight_y(w, cut).start()
    sends = []
    for p in (1, 2, 3):
        copy = remote(block(rows_c, 0), block(rows_c, 2 * p), link_c, p, relative(2 * p))
        copy.start()
        sends.append(copy)

    def forward_n(p):
        return remote(block(rows_n, 2 * p), block(rows_n, 2 * p + 1), core_n, p, sibling)

    def forward_c(p):
        return remote(block(rows_c, 2 * p), block(rows_c, 2 * p + 1), core_c, p, sibling)

    forward_c(0).start()
    for load in loads:
        load.start()
    same = seg_column[...] == seg_row[...]
    asked = lax.broadcasted_iota(jnp.int32, same.shape, 0)
    seen = lax.broadcasted_iota(jnp.int32, same.shape, 1)
    allowed_ref[...] = jnp.where(same & (seen <= asked), 1, 0)
    positions = jnp.sum(jnp.where(same & (seen < asked), 1.0, 0.0), axis=1, keepdims=True)
    angles = positions * frequency[...]
    cos_ref[...] = jnp.cos(angles)
    column = lax.broadcasted_iota(jnp.int32, angles.shape, 1)
    sine = jnp.sin(angles)
    sin_ref[...] = jnp.where(column < HD // 2, sine, -sine)
    tokens = tokens_ref[...].astype(f32)
    inv1 = inverse_rms(tokens)
    vector_copy.wait()
    mine_v, other_v = vector_ref[0:1, :], vectors[0:1, :]
    low_v = jnp.where(pair == 0, mine_v, other_v)
    high_v = jnp.where(pair == 0, other_v, mine_v)
    bias_at = 2 * shard
    gain1_ref[...] = jnp.concatenate([low_v[:, :shard], high_v[:, :shard]], axis=1)
    gain2_ref[...] = jnp.concatenate(
        [low_v[:, shard:bias_at], high_v[:, shard:bias_at]], axis=1
    )
    bias = jnp.concatenate(
        [low_v[:, bias_at : bias_at + proj.shape[1] // 2], high_v[:, bias_at : bias_at + proj.shape[1] // 2]],
        axis=1,
    )
    normed1[...] = (tokens * inv1 * gain1_ref[...]).astype(bf16)
    for load in w_loads:
        load.wait()

    def relay(w):
        for cut in range(2):
            weight_y_in(w, cut).wait_recv()
            weight_pass(w, cut, quarter, weights_x, neighbour).start()
            weight_pass(w, cut, quarter, weights_1, sibling).start()

    def relay_x(w):
        for cut in range(2):
            weight_pass(w, cut, beside_quarter, weights_x, neighbour).wait_recv()
            weight_pass(w, cut, beside_quarter, weights_2, sibling).start()

    def settle(w):
        for cut in range(2):
            weight_y(w, cut).wait_send()
            weight_pass(w, cut, quarter, weights_x, neighbour).wait_send()
            weight_pass(w, cut, quarter, weights_1, sibling).wait()
            weight_pass(w, cut, beside_quarter, weights_2, sibling).wait()

    relay(0)
    relay_x(0)
    settle(0)
    projected = contract(normed1[...], w_qkv_ref[...], 1, 0) + bias
    proj[...] = projected
    relay(1)
    groups = H // KV
    score_scale = HD ** (-0.5)

    def turned(at):
        value = proj[:, at : at + HD]
        swapped = jnp.concatenate([value[:, HD // 2 :], value[:, : HD // 2]], axis=1)
        return (value * cos_ref[...] - swapped * sin_ref[...]).astype(bf16)

    for k in range(KV):
        for j in range(groups):
            query_ref[k, j * length : (j + 1) * length, :] = turned((k * groups + j) * HD)
        at = H * HD + k * HD
        keys_ref[k] = turned(at)
        values_ref[k] = proj[:, at + KV * HD : at + (KV + 1) * HD].astype(bf16)
        mask = jnp.concatenate([allowed_ref[...]] * groups, axis=0) > 0
        scores = contract(query_ref[k], keys_ref[k], 1, 1) * score_scale
        scores = jnp.where(mask, scores, NEG_LARGE)
        top = jnp.max(scores, axis=-1, keepdims=True)
        log_total = top + jnp.log(jnp.sum(jnp.exp(scores - top), axis=-1, keepdims=True))
        log_ref[k] = log_total
        soft = jnp.exp(scores - log_total).astype(bf16)
        context = contract(soft, values_ref[k], 1, 0).astype(bf16)
        for j in range(groups):
            at = (k * groups + j) * HD
            context_ref[:, at : at + HD] = context[j * length : (j + 1) * length, :]
        if k == 0:
            relay_x(1)
    settle(1)
    middle_value = tokens + contract(context_ref[...], w_out_ref[...], 1, 0)
    middle_ref[...] = middle_value
    rows_n[0:length] = (middle_value * inverse_rms(middle_value) * gain2_ref[...]).astype(bf16)
    for p in (1, 2, 3):
        copy = remote(block(rows_n, 0), block(rows_n, 2 * p), link, p, relative(2 * p))
        copy.start()
        sends.append(copy)
    forward_n(0).start()
    for load in loads:
        load.wait()

    def pair_step(p, carry):
        def arrive(q):
            remote(block(rows_n, 0), block(rows_n, 2 * q), link, q, relative(2 * q)).wait_recv()
            forward_n(q).start()

        @pl.when(p == 1)
        def _():
            arrive(1)
            arrive(2)

        @pl.when(p == 2)
        def _():
            arrive(3)

        @pl.when(p < 3)
        def _():
            q = p + 1
            remote(block(rows_c, 0), block(rows_c, 2 * q), link_c, q, relative(2 * q)).wait_recv()
            forward_c(q).start()

        forward_n(p).wait()
        forward_c(p).wait()
        both = pl.ds(pl.multiple_of(2 * p * length, 32), 2 * length)
        normed, cot = rows_n[both, :], rows_c[both, :]
        gate_pre = contract(normed, w_gate[...], 1, 0)
        up_proj = contract(normed, w_up[...], 1, 0)
        back_activ = contract(cot, w_down[...], 1, 1)
        sigmoid_gate = jax.nn.sigmoid(gate_pre)
        silu_gate = gate_pre * sigmoid_gate
        column = lax.broadcasted_iota(jnp.int32, gate_pre.shape, 1)
        own = column >= jnp.where(quarter == 3, TILE, 0)
        activ[both, :] = jnp.where(own, silu_gate * up_proj, 0.0).astype(jnp.bfloat16)
        d_gate[both, :] = jnp.where(
            own,
            back_activ * up_proj * sigmoid_gate * (1.0 + gate_pre * (1.0 - sigmoid_gate)),
            0.0,
        ).astype(jnp.bfloat16)
        d_up[both, :] = jnp.where(own, back_activ * silu_gate, 0.0).astype(jnp.bfloat16)
        part_b[both, :] = (
            contract(d_gate[both, :], w_gate[...], 1, 1)
            + contract(d_up[both, :], w_up[...], 1, 1)
        ).astype(jnp.bfloat16)
        remote(block(part_b, 2 * p + 1), sib_b.at[p], core_b, p, relative(1)).start()
        part_r[both, :] = contract(activ[both, :], w_down[...], 1, 0).astype(jnp.bfloat16)
        remote(block(part_r, 2 * p + 1), sib_r.at[p], core_r, p, relative(1)).start()
        return carry

    lax.fori_loop(0, 4, pair_step, 0)

    def fold(part, sib, core, land, hop):
        for p in (1, 2, 3, 0):
            remote(block(part, 2 * p + 1), sib.at[p], core, p, relative(1)).wait()
            rows = slice(2 * p * length, (2 * p + 1) * length)
            joined = part[rows, :].astype(jnp.float32) + sib[p].astype(jnp.float32)
            if p == 0:
                total[...] = joined
            else:
                part[rows, :] = joined.astype(jnp.bfloat16)
                remote(block(part, 2 * p), land.at[p - 1], hop, p, relative(2 * p)).start()

    def finish(part, land, hop, goal):
        value = goal[...]
        for p in (1, 2, 3):
            remote(block(part, 2 * p), land.at[p - 1], hop, p, relative(2 * p)).wait()
            value = value + land[p - 1].astype(jnp.float32)
        goal[...] = value

    def chunk(c):
        return pl.ds(pl.multiple_of(c * CHUNK, CHUNK), CHUNK)

    def up_copy(c):
        return remote(own.at[chunk(c)], land_u.at[chunk(c)], up, c, near)

    def mid_copy(c):
        return remote(own.at[chunk(c)], land_m.at[chunk(c)], mid, c, far)

    def down_copy(c):
        return remote(total.at[chunk(c)], total.at[chunk(c)], down, c, near)

    def side_copy(c):
        return remote(
            total.at[chunk(c)], out_ref.at[quarter].at[chunk(c)], side, c, neighbour
        )

    def side_arrival(c):
        return remote(
            total.at[chunk(c)], out_ref.at[beside_quarter].at[chunk(c)], side, c, neighbour
        )

    def out_copy(c):
        return remote(total.at[chunk(c)], out_ref.at[quarter].at[chunk(c)], out1, c, sibling)

    def pass_copy(c):
        place = out_ref.at[beside_quarter].at[chunk(c)]
        return remote(place, place, out2, c, sibling)

    def store(c):
        return pltpu.make_async_copy(
            total.at[chunk(c)], out_ref.at[quarter].at[chunk(c)], local.at[7 + c]
        )

    def hand_out(c):
        side_copy(c).start()
        out_copy(c).start()
        store(c).start()

    def add(goal, left, right, rows):
        goal[rows, :] = (
            left[rows, :].astype(jnp.float32) + right[rows, :].astype(jnp.float32)
        ).astype(jnp.bfloat16)

    def send_up(lo, hi):
        @pl.when(is_end)
        def _():
            def go(c, carry):
                up_copy(c).start()
                return carry

            lax.fori_loop(lo, hi, go, 0)

    skew1, skew2 = 3, 6

    def service(i, carry):
        a, b, d = i, i - skew1, i - skew2

        @pl.when(middle & (a < count))
        def _():
            up_copy(a).wait_recv()
            add(own, own, land_u, chunk(a))
            mid_copy(a).start()

        @pl.when((b >= 0) & (b < count))
        def _():
            @pl.when(middle)
            def _():
                mid_copy(b).wait_recv()
                add(total, own, land_m, chunk(b))
                down_copy(b).start()

            @pl.when(is_end)
            def _():
                down_copy(b).wait_recv()

            hand_out(b)

        @pl.when(d >= 0)
        def _():
            side_arrival(d).wait_recv()
            pass_copy(d).start()

        return carry

    def serve(lo, hi):
        lax.fori_loop(lo, hi, service, 0)

    def fold(part, sib, core, land, hop, goal):
        for p in (1, 2, 3, 0):
            remote(block(part, 2 * p + 1), sib.at[p], core, p, relative(1)).wait()
            rows = slice(2 * p * length, (2 * p + 1) * length)
            joined = part[rows, :].astype(f32) + sib[p].astype(f32)
            if p == 0:
                goal[...] = joined
            else:
                part[rows, :] = joined.astype(bf16)
                remote(block(part, 2 * p), land.at[p - 1], hop, p, relative(2 * p)).start()

    def finish(part, land, hop, goal):
        value = goal[...]
        for p in (1, 2, 3):
            remote(block(part, 2 * p), land.at[p - 1], hop, p, relative(2 * p)).wait()
            value = value + land[p - 1].astype(f32)
        return value

    fold(part_b, sib_b, core_b, land_b, link_b, share)

    def grad_step(h, carry):
        lane = pl.ds(pl.multiple_of(h * TILE, TILE), TILE)
        left = rows_n[:, lane]

        def place(which):
            return pl.ds(pl.multiple_of((3 * h + which) * TILE, TILE), TILE)

        own[place(0), :] = contract(left, d_gate[...], 0, 0).astype(bf16)
        own[place(1), :] = contract(left, d_up[...], 0, 0).astype(bf16)
        down = contract(activ[...], rows_c[:, lane], 0, 0).astype(bf16)
        for i in range(SLICE // TILE):
            own[place(2), i * TILE : (i + 1) * TILE] = down[i * TILE : (i + 1) * TILE]
        per = 3 * TILE // CHUNK
        send_up(h * per, (h + 1) * per)
        return carry

    lax.fori_loop(0, width // TILE, grad_step, 0)
    fold(part_r, sib_r, core_r, land_r, link_r, result_ref)
    back_normed = finish(part_b, land_b, link_b, share)
    serve(0, 2)

    def norm_back(hidden, inv, gain, back):
        weighted = back * gain
        inner = jnp.mean(weighted * hidden, axis=-1, keepdims=True)
        back_hidden = inv * weighted - hidden * (inv * inv * inv) * inner
        return back_hidden, jnp.sum(back * hidden * inv, axis=0, keepdims=True)

    hidden = middle_ref[...]
    back_hidden, sum2 = norm_back(hidden, inverse_rms(hidden), gain2_ref[...], back_normed)
    back_middle = rows_c[0:length, :].astype(f32) + back_hidden
    share[...] = back_middle
    back_middle_b = back_middle.astype(bf16)
    back_context = contract(back_middle_b, w_out_ref[...], 1, 1).astype(bf16)
    for k in range(KV):
        for j in range(groups):
            at = (k * groups + j) * HD
            stacked[k, j * length : (j + 1) * length, :] = back_context[:, at : at + HD]
    joined_ref[:, proj.shape[1] :] = contract(context_ref[...], back_middle_b, 0, 0).astype(bf16)
    serve(2, 3)

    def unturn(value):
        swapped = jnp.concatenate([value[:, HD // 2 :], value[:, : HD // 2]], axis=1)
        return value * cos_ref[...] + swapped * sin_ref[...]

    for k in range(KV):
        keys, values, query, back = keys_ref[k], values_ref[k], query_ref[k], stacked[k]
        mask = jnp.concatenate([allowed_ref[...]] * groups, axis=0) > 0
        scores = contract(query, keys, 1, 1) * score_scale
        soft = jnp.exp(jnp.where(mask, scores, NEG_LARGE) - log_ref[k])
        back_soft = contract(back, values, 1, 1)
        row_dot = jnp.sum(soft * back_soft, axis=-1, keepdims=True)
        back_scores = (soft * (back_soft - row_dot) * score_scale).astype(bf16)
        back_values = contract(soft.astype(bf16), back, 0, 0)
        back_query = contract(back_scores, keys, 1, 0)
        back_keys = contract(back_scores, query, 0, 0)
        for j in range(groups):
            at = (k * groups + j) * HD
            proj[:, at : at + HD] = unturn(back_query[j * length : (j + 1) * length, :])
        at = H * HD + k * HD
        proj[:, at : at + HD] = unturn(back_keys)
        proj[:, at + KV * HD : at + (KV + 1) * HD] = back_values
        serve(3 + 2 * k, 5 + 2 * k)

    sum_bias = jnp.sum(proj[...], axis=0, keepdims=True)
    proj_b = proj[...].astype(bf16)
    tokens = tokens_ref[...].astype(f32)
    inv1 = inverse_rms(tokens)
    joined_ref[:, : proj.shape[1]] = contract(normed1[...], proj_b, 0, 0).astype(bf16)
    serve(7, 8)
    back_normed1 = contract(proj_b, w_qkv_ref[...], 1, 1)
    back_first, sum1 = norm_back(tokens, inv1, gain1_ref[...], back_normed1)
    back_ref[...] = share[...] + back_first
    row = lax.broadcasted_iota(jnp.int32, rest_ref.shape[1:], 0)

    def lines_of(top, second):
        pads = [
            jnp.concatenate([v, jnp.zeros((1, wide - v.shape[1]), f32)], axis=1)
            if v.shape[1] < wide
            else v
            for v in (top, second)
        ]
        return jnp.where(row == 0, pads[0], jnp.where(row == 1, pads[1], 0.0)).astype(bf16)

    rest_ref[0] = lines_of(sum1, sum2)
    rest_ref[1] = lines_of(sum_bias[:, :wide], sum_bias[:, wide:])
    small_loads = []
    for g in range(2):
        rows = slice(g * depth, (g + 1) * depth)
        small_loads += [
            pltpu.make_async_copy(
                joined_ref.at[rows, lanes(core)], mine.at[g, 0:depth], local.at[3 + g]
            ),
            pltpu.make_async_copy(rest_ref.at[core], mine.at[g, depth:lines], local.at[5 + g]),
        ]
    for copy in small_loads:
        copy.start()
    swap0 = []
    for g in range(2):
        rows = slice(g * depth, (g + 1) * depth)
        swap0 += [
            remote(joined_ref.at[rows, lanes(1 - core)], sib.at[g, 0:depth], early, g, sibling),
            remote(rest_ref.at[1 - core], sib.at[g, depth:lines], early, 2 + g, sibling),
        ]
    for copy in swap0:
        copy.start()
    serve(8, 10)
    for copy in small_loads + swap0:
        copy.wait()

    def add_small(r, carry):
        rows = pl.ds(pl.multiple_of(r * 48, 16), 48)
        for g in range(2):
            mine[g, rows, :] = (
                mine[g, rows, :].astype(jnp.float32) + sib[g, rows, :].astype(jnp.float32)
            ).astype(jnp.bfloat16)
        return carry

    lax.fori_loop(0, lines // 48, add_small, 0)

    def swap_copy(which):
        return remote(
            mine.at[1 - pair].at[halves(which)], across.at[halves(which)], early, 4 + which, peer
        )

    swap_copy(1 - x).start()
    swap_copy(x).start()
    serve(10, 22)
    result_ref[...] = middle_ref[...] + finish(part_r, land_r, link_r, result_ref)


    def add_across(which):
        def go(r, carry):
            rows = pl.ds(pl.multiple_of(which * half + r * 48, 16), 48)
            across[rows, :] = (
                across[rows, :].astype(jnp.float32) + mine[pair, rows, :].astype(jnp.float32)
            ).astype(jnp.bfloat16)
            return carry

        lax.fori_loop(0, half // 48, go, 0)

    swap_copy(1 - x).wait()
    add_across(1 - x)
    side_small = remote(across.at[halves(1 - x)], beside, early, 6, neighbour)
    side_small.start()
    serve(22, 32)
    swap_copy(x).wait()
    side_small.wait()
    for s in range(half // 48):
        rows = pl.ds(pl.multiple_of(x * half + s * 48, 16), 48)
        value = (
            across[rows, :].astype(jnp.float32)
            + mine[pair, rows, :].astype(jnp.float32)
            + beside[s * 48 : (s + 1) * 48, :].astype(jnp.float32)
        ).astype(jnp.bfloat16)
        for t in range(wide // TILE):
            own[bulk + t * 48 : bulk + (t + 1) * 48, s * TILE : (s + 1) * TILE] = value[
                :, t * TILE : (t + 1) * TILE
            ]
    send_up(first, count)
    serve(32, count + skew2)

    def drain(c, carry):
        @pl.when(is_end)
        def _():
            up_copy(c).wait_send()

        @pl.when(middle)
        def _():
            mid_copy(c).wait_send()
            down_copy(c).wait_send()

        side_copy(c).wait_send()
        out_copy(c).wait_send()
        out_copy(c).wait_recv()
        pass_copy(c).wait_send()
        pass_copy(c).wait_recv()
        store(c).wait()
        return carry

    lax.fori_loop(0, count, drain, 0)


    for copy in sends:
        copy.wait_send()


def layer(*args):
    length, width = args[0].shape
    rows = 8 * length
    bf16, f32 = jnp.bfloat16, jnp.float32
    vmem = pl.BlockSpec(memory_space=pltpu.VMEM)
    hbm = pl.BlockSpec(memory_space=pl.ANY)
    qkv_width = args[6].shape[1]
    wide = (qkv_width + width) // 2
    chain = 3 * width + SMALL_ROWS * wide // (2 * SLICE)
    count = chain // CHUNK
    stack = (KV, H // KV * length)
    buffers = [
        ((rows, width), bf16),
        ((rows, width), bf16),
        ((width, SLICE), bf16),
        ((width, SLICE), bf16),
        ((SLICE, width), bf16),
        ((rows, SLICE), bf16),
        ((rows, SLICE), bf16),
        ((rows, SLICE), bf16),
        ((rows, width), bf16),
        ((rows, width), bf16),
        ((4, length, width), bf16),
        ((4, length, width), bf16),
        ((3, length, width), bf16),
        ((3, length, width), bf16),
        ((chain, SLICE), bf16),
        ((chain, SLICE), bf16),
        ((chain, SLICE), bf16),
        ((chain, SLICE), bf16),
        ((2, SMALL_ROWS, wide), bf16),
        ((2, SMALL_ROWS, wide), bf16),
        ((SMALL_ROWS, wide), bf16),
        ((SMALL_ROWS // 2, wide), bf16),
        ((width, 2 * wide), bf16),
        ((2, SMALL_ROWS - width // 2, wide), bf16),
        ((length, qkv_width), f32),
        ((KV, H // KV * length, HD), bf16),
        ((length, width), bf16),
        ((length, width), f32),
        ((width, qkv_width), bf16),
        ((width, width), bf16),
        (args[4].shape, f32),
        ((*stack, HD), bf16),
        ((KV, length, HD), bf16),
        ((KV, length, HD), bf16),
        ((*stack, 1), f32),
        ((length, length), jnp.int32),
        ((length, HD), f32),
        ((length, HD), f32),
        ((length, width), bf16),
        ((length, width), f32),
        ((1, width), f32),
        ((1, width), f32),
    ]
    sizes = [4] * 7 + [8] + [count] * 6 + [4] * 5

    def body(*refs):
        plain = len(args) + 3 + len(buffers)
        local, rest = refs[plain], refs[plain + 1 :]
        grouped = [(rest[2 * i], rest[2 * i + 1]) for i in range(len(sizes))]
        layer_kernel(*refs[:plain], local, *grouped)

    return pl.pallas_call(
        body,
        out_shape=[
            jax.ShapeDtypeStruct((length, width), f32),
            jax.ShapeDtypeStruct((length, width), f32),
            jax.ShapeDtypeStruct((4, chain, SLICE), bf16),
        ],
        in_specs=[vmem] * 6 + [hbm] * 5,
        out_specs=[vmem, vmem, hbm],
        scratch_shapes=[pltpu.VMEM(shape, kind) for shape, kind in buffers]
        + [pltpu.SemaphoreType.DMA((7 + count,))]
        + [pltpu.SemaphoreType.DMA((size,)) for size in sizes for _ in range(2)],
        compiler_params=pltpu.CompilerParams(
            collective_id=1, has_side_effects=True, vmem_limit_bytes=60 * 1024 * 1024
        ),
        name="layer",
    )(*args)


def unpack_kernel(
    gate_in, up_in, down_in, small_in, gate, up, down, qkv, out, norm1, norm2, bias, extra
):
    f32 = jnp.float32
    for source, goal in ((gate_in, gate), (up_in, up)):
        for k in range(3):
            goal[:, k * SLICE : (k + 1) * SLICE] = source[k].astype(f32)
        goal[:, 3 * SLICE :] = source[3, :, TILE:].astype(f32)
    tiles = SLICE // TILE
    for k in range(4):
        for i in range(tiles):
            if k == 3 and i == 0:
                continue
            first = (k * tiles + i - k // 3) * TILE
            down[first : first + TILE, :] = down_in[k, :, i * TILE : (i + 1) * TILE].astype(f32)

    @pl.when(pl.program_id(0) == 0)
    def _():
        depth, split = qkv.shape
        lanes = small_in.shape[1] // 48
        for k in range(4):
            for t in range(lanes):
                for s in range(tiles):
                    value = small_in[
                        k, t * 48 : (t + 1) * 48, s * TILE : (s + 1) * TILE
                    ].astype(f32)
                    row, column = k // 2 * tiles * 48 + s * 48, (k % 2 * lanes + t) * TILE
                    keep = min(48, depth - row)
                    if column < split:
                        qkv[row : row + keep, column : column + TILE] = value[:keep]
                    else:
                        at = column - split
                        out[row : row + keep, at : at + TILE] = value[:keep]
                    if keep < 48:
                        extra[:, column : column + TILE] = value[keep:]
        high = lax.axis_index("group") == 1
        wide, share = extra.shape[1] // 2, norm1.shape[1]
        for row, goal in ((0, norm1), (1, norm2)):
            line = extra[row : row + 1, : 2 * share]
            goal[...] = jnp.where(high, line[:, share:], line[:, :share])
        most = bias.shape[1]
        line = jnp.concatenate(
            [extra[0:1, wide:], extra[1:2, wide : wide + 2 * most - wide]], axis=1
        )
        goal = jnp.where(high, line[:, most:], line[:, :most])
        bias[...] = goal


def unpack(full, width, qkv_width):
    f32 = jnp.float32
    steps = width // TILE
    features = 4 * SLICE - TILE
    small_rows = full.shape[1] - 3 * width
    depth = width // 2
    whole = lambda i: (0, 0)
    return pl.pallas_call(
        unpack_kernel,
        grid=(steps,),
        out_shape=[
            jax.ShapeDtypeStruct((width, features), f32),
            jax.ShapeDtypeStruct((width, features), f32),
            jax.ShapeDtypeStruct((features, width), f32),
            jax.ShapeDtypeStruct((depth, qkv_width), f32),
            jax.ShapeDtypeStruct((depth, width), f32),
            jax.ShapeDtypeStruct((1, depth), f32),
            jax.ShapeDtypeStruct((1, depth), f32),
            jax.ShapeDtypeStruct((1, qkv_width // 2), f32),
        ],
        in_specs=[
            pl.BlockSpec((4, TILE, SLICE), lambda i: (0, 3 * i, 0)),
            pl.BlockSpec((4, TILE, SLICE), lambda i: (0, 3 * i + 1, 0)),
            pl.BlockSpec((4, TILE, SLICE), lambda i: (0, 3 * i + 2, 0)),
            pl.BlockSpec((4, small_rows, SLICE), lambda i: (0, 3 * width // small_rows, 0)),
        ],
        out_specs=[
            pl.BlockSpec((TILE, features), lambda i: (i, 0)),
            pl.BlockSpec((TILE, features), lambda i: (i, 0)),
            pl.BlockSpec((features, TILE), lambda i: (0, i)),
            pl.BlockSpec((depth, qkv_width), whole),
            pl.BlockSpec((depth, width), whole),
            pl.BlockSpec((1, depth), whole),
            pl.BlockSpec((1, depth), whole),
            pl.BlockSpec((1, qkv_width // 2), whole),
        ],
        scratch_shapes=[pltpu.VMEM((SMALL_ROWS - depth, qkv_width + width), f32)],
        compiler_params=pltpu.CompilerParams(vmem_limit_bytes=56 * 1024 * 1024),
        name="unpack",
    )(full, full, full, full)


def fits(pairs, copies, tokens, segments, qkv, out, gate, down):
    return (
        pairs == 2
        and copies == 16
        and tokens.shape == (1, 144, 896)
        and qkv.shape == (448, 1152)
        and out.shape == (448, 896)
        and gate.shape == (896, 2432)
        and down.shape == (2432, 896)
    )


def gradients_of(full, width, qkv_width):
    gate, up, down, qkv, out, norm1, norm2, bias = unpack(full, width, qkv_width)
    return (norm1[0], qkv, bias[0], out, norm2[0], gate, up, down)


def swap(values):
    return lax.ppermute(values, "group", [(0, 1), (1, 0)])


def gather_weight(shard, pairs, copies):
    if pairs != 2 or copies % 2:
        return lax.all_gather(shard, "group", axis=0, tiled=True)
    half = shard.shape[0] // 2
    core = lax.axis_index("replica") % 2
    mine = swap(lax.dynamic_slice_in_dim(shard, core * half, half, 0))
    sibling = lax.ppermute(mine, "replica", [(i, i + 1 - 2 * (i % 2)) for i in range(copies)])
    front = jnp.where(core == 0, mine, sibling)
    back = jnp.where(core == 0, sibling, mine)
    first = lax.axis_index("group") == 0
    other = jnp.concatenate([front, back], axis=0)
    return jnp.concatenate(
        [jnp.where(first, shard, other), jnp.where(first, other, shard)], axis=0
    )


def gather_vectors(vectors, pairs):
    if pairs != 2:
        return [lax.all_gather(v, "group", axis=0, tiled=True) for v in vectors]
    joined = jnp.concatenate(vectors)
    other = swap(joined)
    first = lax.axis_index("group") == 0
    low, high = jnp.where(first, joined, other), jnp.where(first, other, joined)
    found, at = [], 0
    for v in vectors:
        size = v.shape[0]
        found.append(jnp.concatenate([low[at : at + size], high[at : at + size]]))
        at += size
    return found


def gather_rows(rows, pairs):
    if pairs != 2:
        return lax.all_gather(rows, "group", axis=0, tiled=True)
    return jnp.concatenate([rows, swap(rows)], axis=0)


def scatter_rows(partial, pairs):
    if pairs != 2:
        return lax.psum_scatter(
            partial.astype(jnp.bfloat16), "group", scatter_dimension=0, tiled=True
        ).astype(jnp.float32)
    half = partial.shape[0] // 2
    return partial[:half] + swap(partial[half:].astype(jnp.bfloat16)).astype(jnp.float32)


def scatter_owned(partial):
    return lax.psum_scatter(
        partial.astype(jnp.bfloat16), "group", scatter_dimension=0, tiled=True
    ).astype(jnp.float32)


def sum_owned(small, qkv, out, gate, up, down):
    owned = [scatter_owned(a) for a in (small, qkv, out)]
    return lax.psum(tuple(a.astype(jnp.bfloat16) for a in (*owned, gate, up, down)), "replica")


def on_device(
    tokens,
    segments,
    norm1_gain,
    qkv_weight,
    qkv_bias,
    out_weight,
    norm2_gain,
    gate_weight,
    up_weight,
    down_weight,
    cotangent,
    *,
    pairs,
    copies,
):
    sequences, length, model_width = tokens.shape
    row_count = sequences * length
    q_width = H * HD
    kv_width = KV * HD
    groups = H // KV
    score_scale = HD ** (-0.5)
    if fits(pairs, copies, tokens, segments, qkv_weight, out_weight, gate_weight, down_weight):
        shape_out = (sequences, length, model_width)
        vector = jnp.concatenate([norm1_gain, norm2_gain, qkv_bias]).astype(jnp.float32)
        vector = jnp.broadcast_to(jnp.pad(vector, (0, -vector.shape[0] % 128)), (8, 1536))
        half_dim = HD // 2
        frequency = ROPE_BASE ** (-2.0 * jnp.arange(half_dim, dtype=jnp.float32) / HD)
        result, back_tokens, full = layer(
            tokens.reshape(row_count, model_width),
            segments.reshape(length, 1),
            segments.reshape(1, length),
            jnp.concatenate([frequency, frequency])[None],
            vector,
            cotangent.reshape(row_count, model_width),
            qkv_weight,
            out_weight,
            gate_weight,
            up_weight,
            down_weight,
        )
        return (
            result.reshape(shape_out),
            back_tokens.reshape(shape_out),
            *gradients_of(full, model_width, qkv_weight.shape[1]),
        )
    gain1_b, b_qkv, gain2_b = gather_vectors([norm1_gain, qkv_bias, norm2_gain], pairs)
    w_qkv = gather_weight(qkv_weight, pairs, copies)
    w_out = gather_weight(out_weight, pairs, copies)
    back_all = gather_rows(cotangent.reshape(row_count, model_width), pairs)
    allowed, cosine, sine = doc_layout(segments, HD)
    resid_in = tokens.reshape(row_count, model_width).astype(jnp.float32)
    inv_rms1 = inverse_rms(resid_in)
    gain1 = gain1_b.astype(jnp.float32)
    normed1 = (resid_in * inv_rms1 * gain1).astype(jnp.bfloat16)
    projected = matmul(normed1, w_qkv) + b_qkv.astype(jnp.float32)
    query = projected[:, :q_width].reshape(sequences, length, H, HD)
    keys_raw = projected[:, q_width : q_width + kv_width].reshape(sequences, length, KV, HD)
    values_raw = projected[:, q_width + kv_width :].reshape(sequences, length, KV, HD)
    query_b = (
        rotate(query, cosine, sine).astype(jnp.bfloat16).reshape(sequences, length, KV, groups, HD)
    )
    keys_b = rotate(keys_raw, cosine, sine).astype(jnp.bfloat16)
    values_b = values_raw.astype(jnp.bfloat16)
    scores = score_block(query_b, keys_b, allowed, score_scale)
    top_score = jnp.max(scores, axis=-1, keepdims=True)
    log_total = top_score + jnp.log(jnp.sum(jnp.exp(scores - top_score), axis=-1, keepdims=True))
    soft_b = jnp.exp(scores - log_total).astype(jnp.bfloat16)
    context = jnp.einsum("skgqp,spkd->sqkgd", soft_b, values_b, preferred_element_type=jnp.float32)
    context_b = context.astype(jnp.bfloat16).reshape(row_count, q_width)
    middle = resid_in + matmul(context_b, w_out)
    inv_rms2 = inverse_rms(middle)
    gain2 = gain2_b.astype(jnp.float32)
    normed2 = (middle * inv_rms2 * gain2).astype(jnp.bfloat16)
    back_rows = cotangent.reshape(row_count, model_width)
    normed_all = gather_rows(normed2, pairs)
    gate_pre = matmul(normed_all, gate_weight)
    up_proj = matmul(normed_all, up_weight)
    sigmoid_gate = jax.nn.sigmoid(gate_pre)
    silu_gate = gate_pre * sigmoid_gate
    activ_b = (silu_gate * up_proj).astype(jnp.bfloat16)
    result = middle + scatter_rows(matmul(activ_b, down_weight), pairs)
    back_activ = times_transposed(back_all, down_weight)
    back_gate = (
        back_activ * up_proj * sigmoid_gate * (1.0 + gate_pre * (1.0 - sigmoid_gate))
    ).astype(jnp.bfloat16)
    back_up = (back_activ * silu_gate).astype(jnp.bfloat16)
    grad_down = outer_sum(activ_b, back_all)
    grad_gate = outer_sum(normed_all, back_gate)
    grad_up = outer_sum(normed_all, back_up)
    local_normed = times_transposed(back_gate, gate_weight) + times_transposed(back_up, up_weight)
    back_normed2 = scatter_rows(local_normed, pairs)
    back_norm2, grad_norm2_part = norm_backward(middle, inv_rms2, gain2, back_normed2)
    back_middle = back_rows.astype(jnp.float32) + back_norm2
    back_middle_b = back_middle.astype(jnp.bfloat16)
    grad_out_part = outer_sum(context_b, back_middle_b)
    back_context = times_transposed(back_middle_b, w_out).astype(jnp.bfloat16)
    back_context = back_context.reshape(sequences, length, KV, groups, HD)
    soft = jnp.exp(score_block(query_b, keys_b, allowed, score_scale) - log_total)
    soft_again = soft.astype(jnp.bfloat16)
    back_values = jnp.einsum(
        "skgqp,sqkgd->spkd", soft_again, back_context, preferred_element_type=jnp.float32
    )
    back_soft = jnp.einsum(
        "sqkgd,spkd->skgqp", back_context, values_b, preferred_element_type=jnp.float32
    )
    row_dot = jnp.sum(soft * back_soft, axis=-1, keepdims=True)
    back_scores = (soft * (back_soft - row_dot) * score_scale).astype(jnp.bfloat16)
    back_query = jnp.einsum(
        "skgqp,spkd->sqkgd", back_scores, keys_b, preferred_element_type=jnp.float32
    )
    back_keys = jnp.einsum(
        "skgqp,sqkgd->spkd", back_scores, query_b, preferred_element_type=jnp.float32
    )
    back_query = unrotate(back_query.reshape(sequences, length, H, HD), cosine, sine)
    back_keys = unrotate(back_keys, cosine, sine)
    back_proj = jnp.concatenate(
        [
            back_query.reshape(row_count, q_width),
            back_keys.reshape(row_count, kv_width),
            back_values.reshape(row_count, kv_width),
        ],
        axis=1,
    )
    grad_bias_part = jnp.sum(back_proj, axis=0)
    back_proj_b = back_proj.astype(jnp.bfloat16)
    grad_qkv_part = outer_sum(normed1, back_proj_b)
    back_normed1 = times_transposed(back_proj_b, w_qkv)
    back_norm1, grad_norm1_part = norm_backward(resid_in, inv_rms1, gain1, back_normed1)
    back_tokens = back_middle + back_norm1
    small = jnp.stack([v.reshape(pairs, -1) for v in (grad_norm1_part, grad_norm2_part)], axis=1)
    small = jnp.concatenate(
        [small.reshape(pairs, -1), grad_bias_part.reshape(pairs, -1)], axis=1
    ).reshape(-1)
    owned = sum_owned(
        small,
        grad_qkv_part,
        grad_out_part,
        grad_gate,
        grad_up,
        grad_down,
    )
    small, grad_qkv, grad_out, grad_gate, grad_up, grad_down = (
        a.astype(jnp.float32) for a in owned
    )
    gains = norm1_gain.shape[0]
    grad_norm1, grad_norm2, grad_bias = (
        small[:gains],
        small[gains : 2 * gains],
        small[2 * gains :],
    )
    shape_out = (sequences, length, model_width)
    return (
        result.reshape(shape_out),
        back_tokens.reshape(shape_out),
        grad_norm1,
        grad_qkv,
        grad_bias,
        grad_out,
        grad_norm2,
        grad_gate,
        grad_up,
        grad_down,
    )


def solution(mesh):
    in_specs = (
        P(("group", "replica"), None, None),
        P(("group", "replica"), None),
        P("group"),
        P("group", None),
        P("group"),
        P("group", None),
        P("group"),
        P(None, "group"),
        P(None, "group"),
        P("group", None),
        P(("group", "replica"), None, None),
    )
    out_specs = (
        P(("group", "replica"), None, None),
        P(("group", "replica"), None, None),
        P("group"),
        P("group", None),
        P("group"),
        P("group", None),
        P("group"),
        P(None, "group"),
        P(None, "group"),
        P("group", None),
    )
    program = functools.partial(
        on_device, pairs=mesh.shape["group"], copies=mesh.shape["replica"]
    )
    return jax.shard_map(
        program, mesh=mesh, in_specs=in_specs, out_specs=out_specs, check_vma=False
    )
```

```python
import functools

import jax
import jax.numpy as jnp
from jax import lax
from jax.experimental import pallas as pl
from jax.experimental.pallas import tpu as pltpu
from jax.sharding import PartitionSpec as P

H = 14
KV = 2
HD = 64


EPSILON = 1e-06
ROPE_BASE = 1000000.0
NEG_LARGE = -1e30


def doc_layout(segments, head_dim):
    length = segments.shape[1]
    places = jnp.arange(length, dtype=jnp.int32)
    same_doc = segments[:, :, None] == segments[:, None, :]
    earlier = places[None, None, :] < places[None, :, None]
    positions = jnp.sum(jnp.where(same_doc & earlier, 1.0, 0.0).astype(jnp.float32), axis=2)
    allowed = jnp.where(same_doc & (places[None, None, :] <= places[None, :, None]), 1, 0).astype(
        jnp.int32
    )
    half_dim = head_dim // 2
    frequency = ROPE_BASE ** (-2.0 * jnp.arange(half_dim, dtype=jnp.float32) / head_dim)
    angles = positions[:, :, None] * frequency[None, None, :]
    return (allowed, jnp.cos(angles)[:, :, None, :], jnp.sin(angles)[:, :, None, :])


def rotate(values, cosine, sine):
    half_dim = values.shape[-1] // 2
    front_half = values[..., :half_dim]
    back_half = values[..., half_dim:]
    return jnp.concatenate(
        [front_half * cosine - back_half * sine, back_half * cosine + front_half * sine], axis=-1
    )


def unrotate(gradients, cosine, sine):
    half_dim = gradients.shape[-1] // 2
    front_half = gradients[..., :half_dim]
    back_half = gradients[..., half_dim:]
    return jnp.concatenate(
        [front_half * cosine + back_half * sine, back_half * cosine - front_half * sine], axis=-1
    )


def inverse_rms(hidden):
    return lax.rsqrt(jnp.mean(hidden * hidden, axis=-1, keepdims=True) + EPSILON)


def norm_backward(hidden, inv_rms, gain_f, back_normed):
    weighted = back_normed * gain_f
    inner = jnp.mean(weighted * hidden, axis=-1, keepdims=True)
    back_hidden = inv_rms * weighted - hidden * (inv_rms * inv_rms * inv_rms) * inner
    back_gain = jnp.sum(back_normed * hidden * inv_rms, axis=0)
    return (back_hidden, back_gain)


def matmul(left, right):
    return jnp.dot(left, right, preferred_element_type=jnp.float32)


def outer_sum(left, right):
    return lax.dot_general(
        left, right, (((0,), (0,)), ((), ())), preferred_element_type=jnp.float32
    )


def times_transposed(left, right):
    return lax.dot_general(
        left, right, (((1,), (1,)), ((), ())), preferred_element_type=jnp.float32
    )


def score_block(query_b, keys_b, allowed, score_scale):
    scores = (
        jnp.einsum("sqkgd,spkd->skgqp", query_b, keys_b, preferred_element_type=jnp.float32)
        * score_scale
    )
    return jnp.where(allowed[:, None, None, :, :] > 0, scores, NEG_LARGE)


MESH_ID = pl.DeviceIdType.MESH
TILE = 128
SLICE = 640
CHUNK = 64
SMALL_ROWS = 480


def relative(delta):
    me = lax.axis_index("replica")
    pair = lax.axis_index("group")
    core, x = me % 2, lax.div(me, 2) % 2
    d_core, d_x, d_y = delta % 2, lax.div(delta, 2) % 2, lax.div(delta, 4) % 2
    shift = d_core * (1 - 2 * core) + 2 * d_x * (1 - 2 * x)
    return {"group": pair + d_y * (1 - 2 * pair), "replica": me + shift}


def greet(devices):
    barrier = pltpu.get_barrier_semaphore()
    for device in devices:
        pl.semaphore_signal(barrier, inc=1, device_id=device, device_id_type=MESH_ID)
    return barrier


def remote(src, dst, sems, where, device):
    return pltpu.make_async_remote_copy(
        src_ref=src,
        dst_ref=dst,
        send_sem=sems[0].at[where],
        recv_sem=sems[1].at[where],
        device_id=device,
        device_id_type=MESH_ID,
    )


def contract(left, right, left_dim, right_dim):
    return lax.dot_general(
        left,
        right,
        (((left_dim,), (right_dim,)), ((), ())),
        preferred_element_type=jnp.float32,
    )


def layer_kernel(
    tokens_ref,
    seg_row,
    frequency,
    gain1_in,
    gain2_in,
    bias_in,
    cot_ref,
    qkv_ref,
    out_weight_ref,
    gate_ref,
    up_ref,
    down_ref,
    result_ref,
    back_ref,
    out_ref,
    rows_n,
    rows_c,
    w_gate,
    w_up,
    w_down,
    activ,
    d_gate,
    d_up,
    part_b,
    part_r,
    sib_b,
    sib_r,
    land_b,
    land_r,
    own,
    land_u,
    land_m,
    total,
    mine,
    sib,
    across,
    beside,
    joined_ref,
    rest_ref,
    proj,
    stacked,
    normed1,
    share,
    w_qkv_ref,
    w_out_ref,
    vector_ref,
    vectors,
    query_ref,
    keys_ref,
    values_ref,
    log_ref,
    allowed_ref,
    cos_ref,
    sin_ref,
    context_ref,
    middle_ref,
    gain1_ref,
    gain2_ref,
    local,
    hop_sem,
    link,
    core_n,
    core_c,
    core_b,
    core_r,
    link_b,
    link_r,
    early,
    up,
    mid,
    down,
    side,
    out1,
    out2,
    link_c,
    weights_y,
    weights_x,
    weights_1,
    weights_2,
):
    f32, bf16 = jnp.float32, jnp.bfloat16
    count = own.shape[0] // CHUNK
    length, width = tokens_ref.shape
    bulk = 3 * width
    first = bulk // CHUNK
    lines, wide = mine.shape[1], mine.shape[2]
    half = lines // 2
    depth = joined_ref.shape[0] // 2
    me = lax.axis_index("replica")
    pair = lax.axis_index("group")
    core, x, z = me % 2, lax.div(me, 2) % 2, lax.div(me, 4)
    quarter = me % 4
    beside_quarter = quarter + 2 * (1 - 2 * x)
    middle = (z == 1) | (z == 2)
    is_end = (z == 0) | (z == 3)
    near = {"replica": me + 4 * (1 - 2 * (z % 2))}
    far = {"replica": me + 4 * (1 - 2 * lax.div(z, 2))}
    sibling, neighbour, peer = relative(1), relative(2), relative(4)


    def halves(which):
        return pl.ds(pl.multiple_of(which * half, 16), half)

    def lanes(which):
        return pl.ds(pl.multiple_of(which * wide, TILE), wide)

    first_column = pl.multiple_of(TILE * (5 * quarter - lax.div(quarter, 3)), TILE)
    columns = pl.ds(first_column, SLICE)
    loads = [
        pltpu.make_async_copy(gate_ref.at[:, columns], w_gate, local.at[0]),
        pltpu.make_async_copy(up_ref.at[:, columns], w_up, local.at[1]),
        pltpu.make_async_copy(down_ref.at[columns, :], w_down, local.at[2]),
    ]
    shard = width // 2
    w_loads = [
        pltpu.make_async_copy(
            qkv_ref, w_qkv_ref.at[pl.ds(pl.multiple_of(pair * shard, 64), shard)], local.at[3]
        ),
        pltpu.make_async_copy(
            out_weight_ref, w_out_ref.at[pl.ds(pl.multiple_of(pair * shard, 64), shard)], local.at[4]
        ),
    ]
    for load in w_loads:
        load.start()
    rows_c[0:length] = cot_ref[...]
    vector_ref[0:1, 0:shard] = gain1_in[...].astype(f32)
    vector_ref[0:1, 512 : 512 + shard] = gain2_in[...].astype(f32)
    vector_ref[0:1, 1024 : 1024 + bias_in.shape[1]] = bias_in[...].astype(f32)
    barrier = greet([sibling, neighbour, peer, relative(6), near])

    @pl.when(middle)
    def _():
        pl.semaphore_signal(barrier, inc=1, device_id=far, device_id_type=MESH_ID)

    pl.semaphore_wait(barrier, jnp.where(middle, 6, 5))

    def block(ref, slot):
        return ref.at[pl.ds(pl.multiple_of(slot * length, 16), length)]

    part = shard // 4
    cuts = ((0, 48), (48, part - 48))
    vector_copy = remote(vector_ref, vectors, early, 7, peer)
    vector_copy.start()

    def quarter_rows(which, fourth, cut):
        first = which * shard + fourth * part + cuts[cut][0]
        return pl.ds(pl.multiple_of(first, 16), cuts[cut][1])

    moved = [(qkv_ref, w_qkv_ref, 0), (out_weight_ref, w_out_ref, 1)]

    def weight_y(w, cut):
        source, goal, _ = moved[w]
        rows = pl.ds(pl.multiple_of(quarter * part + cuts[cut][0], 16), cuts[cut][1])
        return remote(
            source.at[rows], goal.at[quarter_rows(pair, quarter, cut)], weights_y, 2 * w + cut, peer
        )

    def weight_y_in(w, cut):
        goal = moved[w][1].at[quarter_rows(1 - pair, quarter, cut)]
        return remote(goal, goal, weights_y, 2 * w + cut, peer)

    def weight_pass(w, cut, fourth, sems, device):
        goal = moved[w][1].at[quarter_rows(1 - pair, fourth, cut)]
        return remote(goal, goal, sems, 2 * w + cut, device)

    order = [(w, cut) for w in range(2) for cut in range(2)]
    for w, cut in order:
        weight_y(w, cut).start()
    sends = []

    def send_cot(p):
        copy = remote(block(rows_c, 0), block(rows_c, 2 * p), link_c, p, relative(2 * p))
        copy.start()
        sends.append(copy)

    send_cot(1)

    def forward_n(p):
        return remote(block(rows_n, 2 * p), block(rows_n, 2 * p + 1), core_n, p, sibling)

    def forward_c(p):
        return remote(block(rows_c, 2 * p), block(rows_c, 2 * p + 1), core_c, p, sibling)

    forward_c(0).start()
    for load in loads:
        load.start()
    asked = lax.broadcasted_iota(jnp.int32, (length, length), 0)
    seen = lax.broadcasted_iota(jnp.int32, (length, length), 1)
    seg_column = jnp.sum(jnp.where(asked == seen, seg_row[...], 0), axis=1, keepdims=True)
    same = seg_column == seg_row[...]
    allowed_ref[...] = jnp.where(same & (seen <= asked), 1, 0)
    positions = jnp.sum(jnp.where(same & (seen < asked), 1.0, 0.0), axis=1, keepdims=True)
    angles = positions * frequency[...]
    cos_ref[...] = jnp.cos(angles)
    column = lax.broadcasted_iota(jnp.int32, angles.shape, 1)
    sine = jnp.sin(angles)
    sin_ref[...] = jnp.where(column < HD // 2, sine, -sine)
    tokens = tokens_ref[...].astype(f32)
    inv1 = inverse_rms(tokens)
    vector_copy.wait()
    mine_v, other_v = vector_ref[0:1, :], vectors[0:1, :]
    low_v = jnp.where(pair == 0, mine_v, other_v)
    high_v = jnp.where(pair == 0, other_v, mine_v)
    gain1_ref[...] = jnp.concatenate([low_v[:, :shard], high_v[:, :shard]], axis=1)
    gain2_ref[...] = jnp.concatenate(
        [low_v[:, 512 : 512 + shard], high_v[:, 512 : 512 + shard]], axis=1
    )
    bias_at = 1024
    bias = jnp.concatenate(
        [low_v[:, bias_at : bias_at + proj.shape[1] // 2], high_v[:, bias_at : bias_at + proj.shape[1] // 2]],
        axis=1,
    )
    normed1[...] = (tokens * inv1 * gain1_ref[...]).astype(bf16)
    for load in w_loads:
        load.wait()

    def relay(w):
        for cut in range(2):
            weight_y_in(w, cut).wait_recv()
            weight_pass(w, cut, quarter, weights_x, neighbour).start()
            weight_pass(w, cut, quarter, weights_1, sibling).start()

    def relay_x(w):
        for cut in range(2):
            weight_pass(w, cut, beside_quarter, weights_x, neighbour).wait_recv()
            weight_pass(w, cut, beside_quarter, weights_2, sibling).start()

    def settle(w):
        for cut in range(2):
            weight_y(w, cut).wait_send()
            weight_pass(w, cut, quarter, weights_x, neighbour).wait_send()
            weight_pass(w, cut, quarter, weights_1, sibling).wait()
            weight_pass(w, cut, beside_quarter, weights_2, sibling).wait()

    relay(0)
    send_cot(2)
    relay_x(0)
    settle(0)
    projected = contract(normed1[...], w_qkv_ref[...], 1, 0) + bias
    proj[...] = projected
    relay(1)
    send_cot(3)
    groups = H // KV
    score_scale = HD ** (-0.5)

    def turned(at):
        value = proj[:, at : at + HD]
        swapped = jnp.concatenate([value[:, HD // 2 :], value[:, : HD // 2]], axis=1)
        return (value * cos_ref[...] - swapped * sin_ref[...]).astype(bf16)

    for k in range(KV):
        for j in range(groups):
            query_ref[k, j * length : (j + 1) * length, :] = turned((k * groups + j) * HD)
        at = H * HD + k * HD
        keys_ref[k] = turned(at)
        values_ref[k] = proj[:, at + KV * HD : at + (KV + 1) * HD].astype(bf16)
        mask = jnp.concatenate([allowed_ref[...]] * groups, axis=0) > 0
        scores = contract(query_ref[k], keys_ref[k], 1, 1) * score_scale
        scores = jnp.where(mask, scores, NEG_LARGE)
        top = jnp.max(scores, axis=-1, keepdims=True)
        log_total = top + jnp.log(jnp.sum(jnp.exp(scores - top), axis=-1, keepdims=True))
        log_ref[k] = log_total
        soft = jnp.exp(scores - log_total).astype(bf16)
        context = contract(soft, values_ref[k], 1, 0).astype(bf16)
        for j in range(groups):
            at = (k * groups + j) * HD
            context_ref[:, at : at + HD] = context[j * length : (j + 1) * length, :]
        if k == 0:
            relay_x(1)
    settle(1)
    middle_value = tokens + contract(context_ref[...], w_out_ref[...], 1, 0)
    middle_ref[...] = middle_value
    rows_n[0:length] = (middle_value * inverse_rms(middle_value) * gain2_ref[...]).astype(bf16)
    for p in (1, 2, 3):
        copy = remote(block(rows_n, 0), block(rows_n, 2 * p), link, p, relative(2 * p))
        copy.start()
        sends.append(copy)
    forward_n(0).start()
    for load in loads:
        load.wait()

    def fold(part, sib, core, land, hop, q):
        remote(block(part, 2 * q + 1), sib.at[q], core, q, sibling).wait()
        rows = pl.ds(pl.multiple_of(2 * q * length, 16), length)
        part[rows, :] = (part[rows, :].astype(f32) + sib[q].astype(f32)).astype(bf16)
        remote(block(part, 2 * q), land.at[q - 1], hop, q, relative(2 * q)).start()

    def fold_own(part, sib, core):
        remote(block(part, 1), sib.at[0], core, 0, sibling).wait()
        return part[0:length, :].astype(f32) + sib[0].astype(f32)

    def pair_step(p, carry):
        def arrive(q):
            remote(block(rows_n, 0), block(rows_n, 2 * q), link, q, relative(2 * q)).wait_recv()
            forward_n(q).start()

        @pl.when(p == 1)
        def _():
            arrive(1)
            arrive(2)

        @pl.when(p == 2)
        def _():
            arrive(3)

        @pl.when(p < 3)
        def _():
            q = p + 1
            remote(block(rows_c, 0), block(rows_c, 2 * q), link_c, q, relative(2 * q)).wait_recv()
            forward_c(q).start()

        forward_n(p).wait()
        forward_c(p).wait()
        both = pl.ds(pl.multiple_of(2 * p * length, 32), 2 * length)
        normed, cot = rows_n[both, :], rows_c[both, :]
        gate_pre = contract(normed, w_gate[...], 1, 0)
        up_proj = contract(normed, w_up[...], 1, 0)
        back_activ = contract(cot, w_down[...], 1, 1)
        sigmoid_gate = jax.nn.sigmoid(gate_pre)
        silu_gate = gate_pre * sigmoid_gate
        column = lax.broadcasted_iota(jnp.int32, gate_pre.shape, 1)
        own = column >= jnp.where(quarter == 3, TILE, 0)
        activ[both, :] = jnp.where(own, silu_gate * up_proj, 0.0).astype(jnp.bfloat16)
        d_gate[both, :] = jnp.where(
            own,
            back_activ * up_proj * sigmoid_gate * (1.0 + gate_pre * (1.0 - sigmoid_gate)),
            0.0,
        ).astype(jnp.bfloat16)
        d_up[both, :] = jnp.where(own, back_activ * silu_gate, 0.0).astype(jnp.bfloat16)
        part_b[both, :] = (
            contract(d_gate[both, :], w_gate[...], 1, 1)
            + contract(d_up[both, :], w_up[...], 1, 1)
        ).astype(jnp.bfloat16)
        remote(block(part_b, 2 * p + 1), sib_b.at[p], core_b, p, relative(1)).start()
        part_r[both, :] = contract(activ[both, :], w_down[...], 1, 0).astype(jnp.bfloat16)
        remote(block(part_r, 2 * p + 1), sib_r.at[p], core_r, p, relative(1)).start()

        @pl.when(p >= 2)
        def _():
            fold(part_b, sib_b, core_b, land_b, link_b, p - 1)
            fold(part_r, sib_r, core_r, land_r, link_r, p - 1)

        return carry

    lax.fori_loop(0, 4, pair_step, 0)

    def chunk(c):
        return pl.ds(pl.multiple_of(c * CHUNK, CHUNK), CHUNK)

    def up_copy(c):
        return remote(own.at[chunk(c)], land_u.at[chunk(c)], up, c, near)

    def mid_copy(c):
        return remote(own.at[chunk(c)], land_m.at[chunk(c)], mid, c, far)

    def down_copy(c):
        return remote(total.at[chunk(c)], total.at[chunk(c)], down, c, near)

    def side_copy(c):
        return remote(
            total.at[chunk(c)], out_ref.at[quarter].at[chunk(c)], side, c, neighbour
        )

    def side_arrival(c):
        return remote(
            total.at[chunk(c)], out_ref.at[beside_quarter].at[chunk(c)], side, c, neighbour
        )

    def out_copy(c):
        return remote(total.at[chunk(c)], out_ref.at[quarter].at[chunk(c)], out1, c, sibling)

    def pass_copy(c):
        place = out_ref.at[beside_quarter].at[chunk(c)]
        return remote(place, place, out2, c, sibling)

    def store(c):
        return pltpu.make_async_copy(
            total.at[chunk(c)], out_ref.at[quarter].at[chunk(c)], local.at[7 + c]
        )

    def crosses(c):
        kind = c % 8
        return ((kind != 1) & (kind != 5)) | ((kind == 1) & is_end) | ((kind == 5) & middle)

    def relays(c):
        return (((c % 8) == 1) & is_end) | (((c % 8) == 5) & middle)

    def relay_copy(c):
        place = out_ref.at[beside_quarter].at[chunk(c)]
        return remote(place, place, (hop_sem, side[1]), c, near)

    def hand_out(c):
        @pl.when(crosses(c))
        def _():
            side_copy(c).start()

        out_copy(c).start()
        store(c).start()

    def add(goal, left, right, rows):
        goal[rows, :] = (
            left[rows, :].astype(jnp.float32) + right[rows, :].astype(jnp.float32)
        ).astype(jnp.bfloat16)

    def send_up(lo, hi):
        @pl.when(is_end)
        def _():
            def go(c, carry):
                up_copy(c).start()
                return carry

            lax.fori_loop(lo, hi, go, 0)

    skew1, skew2, skew3 = 3, 6, 12

    def service(i, carry):
        a, b, d, e = i, i - skew1, i - skew2, i - skew3

        @pl.when(middle & (a < count))
        def _():
            up_copy(a).wait_recv()
            add(own, own, land_u, chunk(a))
            mid_copy(a).start()

        @pl.when((b >= 0) & (b < count))
        def _():
            @pl.when(middle)
            def _():
                mid_copy(b).wait_recv()
                add(total, own, land_m, chunk(b))
                down_copy(b).start()

            @pl.when(is_end)
            def _():
                down_copy(b).wait_recv()

            hand_out(b)

        @pl.when((d >= 0) & (d < count) & crosses(d))
        def _():
            side_arrival(d).wait_recv()
            pass_copy(d).start()

            @pl.when(relays(d))
            def _():
                relay_copy(d).start()

        @pl.when((e >= 0) & jnp.logical_not(crosses(e)))
        def _():
            side_arrival(e).wait_recv()
            pass_copy(e).start()

        return carry

    def serve(lo, hi):
        lax.fori_loop(lo, hi, service, 0)

    def finish(part, land, hop, goal):
        value = goal[...]
        for p in (1, 2, 3):
            remote(block(part, 2 * p), land.at[p - 1], hop, p, relative(2 * p)).wait()
            value = value + land[p - 1].astype(f32)
        return value

    fold(part_b, sib_b, core_b, land_b, link_b, 3)
    share[...] = fold_own(part_b, sib_b, core_b)
    fold(part_r, sib_r, core_r, land_r, link_r, 3)
    result_ref[...] = fold_own(part_r, sib_r, core_r)

    def grad_step(h, carry):
        lane = pl.ds(pl.multiple_of(h * TILE, TILE), TILE)
        left = rows_n[:, lane]

        def place(which):
            return pl.ds(pl.multiple_of((3 * h + which) * TILE, TILE), TILE)

        own[place(0), :] = contract(left, d_gate[...], 0, 0).astype(bf16)
        own[place(1), :] = contract(left, d_up[...], 0, 0).astype(bf16)
        down = contract(activ[...], rows_c[:, lane], 0, 0).astype(bf16)
        for i in range(SLICE // TILE):
            own[place(2), i * TILE : (i + 1) * TILE] = down[i * TILE : (i + 1) * TILE]
        per = 3 * TILE // CHUNK
        send_up(h * per, (h + 1) * per)
        return carry

    lax.fori_loop(0, width // TILE, grad_step, 0)
    serve(0, 2)
    back_normed = finish(part_b, land_b, link_b, share)
    serve(2, 4)

    def norm_back(hidden, inv, gain, back):
        weighted = back * gain
        inner = jnp.mean(weighted * hidden, axis=-1, keepdims=True)
        back_hidden = inv * weighted - hidden * (inv * inv * inv) * inner
        return back_hidden, jnp.sum(back * hidden * inv, axis=0, keepdims=True)

    hidden = middle_ref[...]
    back_hidden, sum2 = norm_back(hidden, inverse_rms(hidden), gain2_ref[...], back_normed)
    back_middle = rows_c[0:length, :].astype(f32) + back_hidden
    share[...] = back_middle
    back_middle_b = back_middle.astype(bf16)
    back_context = contract(back_middle_b, w_out_ref[...], 1, 1).astype(bf16)
    for k in range(KV):
        for j in range(groups):
            at = (k * groups + j) * HD
            stacked[k, j * length : (j + 1) * length, :] = back_context[:, at : at + HD]
    joined_ref[:, proj.shape[1] :] = contract(context_ref[...], back_middle_b, 0, 0).astype(bf16)
    serve(4, 5)

    def unturn(value):
        swapped = jnp.concatenate([value[:, HD // 2 :], value[:, : HD // 2]], axis=1)
        return value * cos_ref[...] + swapped * sin_ref[...]

    for k in range(KV):
        keys, values, query, back = keys_ref[k], values_ref[k], query_ref[k], stacked[k]
        mask = jnp.concatenate([allowed_ref[...]] * groups, axis=0) > 0
        scores = contract(query, keys, 1, 1) * score_scale
        soft = jnp.exp(jnp.where(mask, scores, NEG_LARGE) - log_ref[k])
        back_soft = contract(back, values, 1, 1)
        row_dot = jnp.sum(soft * back_soft, axis=-1, keepdims=True)
        back_scores = (soft * (back_soft - row_dot) * score_scale).astype(bf16)
        back_values = contract(soft.astype(bf16), back, 0, 0)
        back_query = contract(back_scores, keys, 1, 0)
        back_keys = contract(back_scores, query, 0, 0)
        for j in range(groups):
            at = (k * groups + j) * HD
            proj[:, at : at + HD] = unturn(back_query[j * length : (j + 1) * length, :])
        at = H * HD + k * HD
        proj[:, at : at + HD] = unturn(back_keys)
        proj[:, at + KV * HD : at + (KV + 1) * HD] = back_values
        serve(5 + 2 * k, 7 + 2 * k)

    sum_bias = jnp.sum(proj[...], axis=0, keepdims=True)
    proj_b = proj[...].astype(bf16)
    tokens = tokens_ref[...].astype(f32)
    inv1 = inverse_rms(tokens)
    joined_ref[:, : proj.shape[1]] = contract(normed1[...], proj_b, 0, 0).astype(bf16)
    serve(9, 10)
    back_normed1 = contract(proj_b, w_qkv_ref[...], 1, 1)
    back_first, sum1 = norm_back(tokens, inv1, gain1_ref[...], back_normed1)
    back_ref[...] = share[...] + back_first
    row = lax.broadcasted_iota(jnp.int32, rest_ref.shape[1:], 0)

    def lines_of(top, second):
        pads = [
            jnp.concatenate([v, jnp.zeros((1, wide - v.shape[1]), f32)], axis=1)
            if v.shape[1] < wide
            else v
            for v in (top, second)
        ]
        return jnp.where(row == 0, pads[0], jnp.where(row == 1, pads[1], 0.0)).astype(bf16)

    rest_ref[0] = lines_of(sum1, sum2)
    rest_ref[1] = lines_of(sum_bias[:, :wide], sum_bias[:, wide:])
    small_loads = []
    for g in range(2):
        rows = slice(g * depth, (g + 1) * depth)
        small_loads += [
            pltpu.make_async_copy(
                joined_ref.at[rows, lanes(core)], mine.at[g, 0:depth], local.at[3 + g]
            ),
            pltpu.make_async_copy(rest_ref.at[core], mine.at[g, depth:lines], local.at[5 + g]),
        ]
    for copy in small_loads:
        copy.start()
    swap0 = []
    for g in range(2):
        rows = slice(g * depth, (g + 1) * depth)
        swap0 += [
            remote(joined_ref.at[rows, lanes(1 - core)], sib.at[g, 0:depth], early, g, sibling),
            remote(rest_ref.at[1 - core], sib.at[g, depth:lines], early, 2 + g, sibling),
        ]
    for copy in swap0:
        copy.start()
    serve(10, 12)
    for copy in small_loads + swap0:
        copy.wait()

    def add_small(r, carry):
        rows = pl.ds(pl.multiple_of(r * 48, 16), 48)
        for g in range(2):
            mine[g, rows, :] = (
                mine[g, rows, :].astype(jnp.float32) + sib[g, rows, :].astype(jnp.float32)
            ).astype(jnp.bfloat16)
        return carry

    lax.fori_loop(0, lines // 48, add_small, 0)

    def swap_copy(which):
        return remote(
            mine.at[1 - pair].at[halves(which)], across.at[halves(which)], early, 4 + which, peer
        )

    swap_copy(1 - x).start()
    swap_copy(x).start()
    serve(12, 24)
    result_ref[...] = middle_ref[...] + finish(part_r, land_r, link_r, result_ref)


    def add_across(which):
        def go(r, carry):
            rows = pl.ds(pl.multiple_of(which * half + r * 48, 16), 48)
            across[rows, :] = (
                across[rows, :].astype(jnp.float32) + mine[pair, rows, :].astype(jnp.float32)
            ).astype(jnp.bfloat16)
            return carry

        lax.fori_loop(0, half // 48, go, 0)

    swap_copy(1 - x).wait()
    add_across(1 - x)
    side_small = remote(across.at[halves(1 - x)], beside, early, 6, neighbour)
    side_small.start()
    serve(24, 34)
    swap_copy(x).wait()
    side_small.wait()
    for s in range(half // 48):
        rows = pl.ds(pl.multiple_of(x * half + s * 48, 16), 48)
        value = (
            across[rows, :].astype(jnp.float32)
            + mine[pair, rows, :].astype(jnp.float32)
            + beside[s * 48 : (s + 1) * 48, :].astype(jnp.float32)
        ).astype(jnp.bfloat16)
        for t in range(wide // TILE):
            own[bulk + t * 48 : bulk + (t + 1) * 48, s * TILE : (s + 1) * TILE] = value[
                :, t * TILE : (t + 1) * TILE
            ]
    send_up(first, count)
    serve(34, count + skew3)

    def drain(c, carry):
        @pl.when(is_end)
        def _():
            up_copy(c).wait_send()

        @pl.when(middle)
        def _():
            mid_copy(c).wait_send()
            down_copy(c).wait_send()

        @pl.when(crosses(c))
        def _():
            side_copy(c).wait_send()

        @pl.when(relays(c))
        def _():
            relay_copy(c).wait_send()

        out_copy(c).wait_send()
        out_copy(c).wait_recv()
        pass_copy(c).wait_send()
        pass_copy(c).wait_recv()
        store(c).wait()
        return carry

    lax.fori_loop(0, count, drain, 0)


    for copy in sends:
        copy.wait_send()


def layer(*args):
    length, width = args[0].shape
    rows = 8 * length
    bf16, f32 = jnp.bfloat16, jnp.float32
    vmem = pl.BlockSpec(memory_space=pltpu.VMEM)
    hbm = pl.BlockSpec(memory_space=pl.ANY)
    qkv_width = args[7].shape[1]
    wide = (qkv_width + width) // 2
    chain = 3 * width + SMALL_ROWS * wide // (2 * SLICE)
    count = chain // CHUNK
    stack = (KV, H // KV * length)
    buffers = [
        ((rows, width), bf16),
        ((rows, width), bf16),
        ((width, SLICE), bf16),
        ((width, SLICE), bf16),
        ((SLICE, width), bf16),
        ((rows, SLICE), bf16),
        ((rows, SLICE), bf16),
        ((rows, SLICE), bf16),
        ((rows, width), bf16),
        ((rows, width), bf16),
        ((4, length, width), bf16),
        ((4, length, width), bf16),
        ((3, length, width), bf16),
        ((3, length, width), bf16),
        ((chain, SLICE), bf16),
        ((chain, SLICE), bf16),
        ((chain, SLICE), bf16),
        ((chain, SLICE), bf16),
        ((2, SMALL_ROWS, wide), bf16),
        ((2, SMALL_ROWS, wide), bf16),
        ((SMALL_ROWS, wide), bf16),
        ((SMALL_ROWS // 2, wide), bf16),
        ((width, 2 * wide), bf16),
        ((2, SMALL_ROWS - width // 2, wide), bf16),
        ((length, qkv_width), f32),
        ((KV, H // KV * length, HD), bf16),
        ((length, width), bf16),
        ((length, width), f32),
        ((width, qkv_width), bf16),
        ((width, width), bf16),
        ((8, 1664), f32),
        ((8, 1664), f32),
        ((*stack, HD), bf16),
        ((KV, length, HD), bf16),
        ((KV, length, HD), bf16),
        ((*stack, 1), f32),
        ((length, length), jnp.int32),
        ((length, HD), f32),
        ((length, HD), f32),
        ((length, width), bf16),
        ((length, width), f32),
        ((1, width), f32),
        ((1, width), f32),
    ]
    sizes = [4] * 7 + [8] + [count] * 6 + [4] * 5

    def body(*refs):
        plain = len(args) + 3 + len(buffers)
        local, hop, rest = refs[plain], refs[plain + 1], refs[plain + 2 :]
        grouped = [(rest[2 * i], rest[2 * i + 1]) for i in range(len(sizes))]
        layer_kernel(*refs[:plain], local, hop, *grouped)

    return pl.pallas_call(
        body,
        out_shape=[
            jax.ShapeDtypeStruct((length, width), f32),
            jax.ShapeDtypeStruct((length, width), f32),
            jax.ShapeDtypeStruct((4, chain, SLICE), bf16),
        ],
        in_specs=[vmem] * 7 + [hbm] * 5,
        out_specs=[vmem, vmem, hbm],
        scratch_shapes=[pltpu.VMEM(shape, kind) for shape, kind in buffers]
        + [pltpu.SemaphoreType.DMA((7 + count,)), pltpu.SemaphoreType.DMA((count,))]
        + [pltpu.SemaphoreType.DMA((size,)) for size in sizes for _ in range(2)],
        compiler_params=pltpu.CompilerParams(
            collective_id=1, has_side_effects=True, vmem_limit_bytes=60 * 1024 * 1024
        ),
        name="layer",
    )(*args)


def unpack_kernel(
    gate_in, up_in, down_in, small_in, gate, up, down, qkv, out, norm1, norm2, bias, extra
):
    f32 = jnp.float32
    for source, goal in ((gate_in, gate), (up_in, up)):
        for k in range(3):
            goal[:, k * SLICE : (k + 1) * SLICE] = source[k].astype(f32)
        goal[:, 3 * SLICE :] = source[3, :, TILE:].astype(f32)
    tiles = SLICE // TILE
    for k in range(4):
        for i in range(tiles):
            if k == 3 and i == 0:
                continue
            first = (k * tiles + i - k // 3) * TILE
            down[first : first + TILE, :] = down_in[k, :, i * TILE : (i + 1) * TILE].astype(f32)

    @pl.when(pl.program_id(0) == 0)
    def _():
        depth, split = qkv.shape
        lanes = small_in.shape[1] // 48
        for k in range(4):
            for t in range(lanes):
                for s in range(tiles):
                    value = small_in[
                        k, t * 48 : (t + 1) * 48, s * TILE : (s + 1) * TILE
                    ].astype(f32)
                    row, column = k // 2 * tiles * 48 + s * 48, (k % 2 * lanes + t) * TILE
                    keep = min(48, depth - row)
                    if column < split:
                        qkv[row : row + keep, column : column + TILE] = value[:keep]
                    else:
                        at = column - split
                        out[row : row + keep, at : at + TILE] = value[:keep]
                    if keep < 48:
                        extra[:, column : column + TILE] = value[keep:]
        high = lax.axis_index("group") == 1
        wide, share = extra.shape[1] // 2, norm1.shape[1]
        for row, goal in ((0, norm1), (1, norm2)):
            line = extra[row : row + 1, : 2 * share]
            goal[...] = jnp.where(high, line[:, share:], line[:, :share])
        most = bias.shape[1]
        line = jnp.concatenate(
            [extra[0:1, wide:], extra[1:2, wide : wide + 2 * most - wide]], axis=1
        )
        goal = jnp.where(high, line[:, most:], line[:, :most])
        bias[...] = goal


def unpack(full, width, qkv_width):
    f32 = jnp.float32
    steps = width // TILE
    features = 4 * SLICE - TILE
    small_rows = full.shape[1] - 3 * width
    depth = width // 2
    whole = lambda i: (0, 0)
    return pl.pallas_call(
        unpack_kernel,
        grid=(steps,),
        out_shape=[
            jax.ShapeDtypeStruct((width, features), f32),
            jax.ShapeDtypeStruct((width, features), f32),
            jax.ShapeDtypeStruct((features, width), f32),
            jax.ShapeDtypeStruct((depth, qkv_width), f32),
            jax.ShapeDtypeStruct((depth, width), f32),
            jax.ShapeDtypeStruct((1, depth), f32),
            jax.ShapeDtypeStruct((1, depth), f32),
            jax.ShapeDtypeStruct((1, qkv_width // 2), f32),
        ],
        in_specs=[
            pl.BlockSpec((4, TILE, SLICE), lambda i: (0, 3 * i, 0)),
            pl.BlockSpec((4, TILE, SLICE), lambda i: (0, 3 * i + 1, 0)),
            pl.BlockSpec((4, TILE, SLICE), lambda i: (0, 3 * i + 2, 0)),
            pl.BlockSpec((4, small_rows, SLICE), lambda i: (0, 3 * width // small_rows, 0)),
        ],
        out_specs=[
            pl.BlockSpec((TILE, features), lambda i: (i, 0)),
            pl.BlockSpec((TILE, features), lambda i: (i, 0)),
            pl.BlockSpec((features, TILE), lambda i: (0, i)),
            pl.BlockSpec((depth, qkv_width), whole),
            pl.BlockSpec((depth, width), whole),
            pl.BlockSpec((1, depth), whole),
            pl.BlockSpec((1, depth), whole),
            pl.BlockSpec((1, qkv_width // 2), whole),
        ],
        scratch_shapes=[pltpu.VMEM((SMALL_ROWS - depth, qkv_width + width), f32)],
        compiler_params=pltpu.CompilerParams(vmem_limit_bytes=56 * 1024 * 1024),
        name="unpack",
    )(full, full, full, full)


def fits(pairs, copies, tokens, segments, qkv, out, gate, down):
    return (
        pairs == 2
        and copies == 16
        and tokens.shape == (1, 144, 896)
        and qkv.shape == (448, 1152)
        and out.shape == (448, 896)
        and gate.shape == (896, 2432)
        and down.shape == (2432, 896)
    )


def gradients_of(full, width, qkv_width):
    gate, up, down, qkv, out, norm1, norm2, bias = unpack(full, width, qkv_width)
    return (norm1[0], qkv, bias[0], out, norm2[0], gate, up, down)


def swap(values):
    return lax.ppermute(values, "group", [(0, 1), (1, 0)])


def gather_weight(shard, pairs, copies):
    if pairs != 2 or copies % 2:
        return lax.all_gather(shard, "group", axis=0, tiled=True)
    half = shard.shape[0] // 2
    core = lax.axis_index("replica") % 2
    mine = swap(lax.dynamic_slice_in_dim(shard, core * half, half, 0))
    sibling = lax.ppermute(mine, "replica", [(i, i + 1 - 2 * (i % 2)) for i in range(copies)])
    front = jnp.where(core == 0, mine, sibling)
    back = jnp.where(core == 0, sibling, mine)
    first = lax.axis_index("group") == 0
    other = jnp.concatenate([front, back], axis=0)
    return jnp.concatenate(
        [jnp.where(first, shard, other), jnp.where(first, other, shard)], axis=0
    )


def gather_vectors(vectors, pairs):
    if pairs != 2:
        return [lax.all_gather(v, "group", axis=0, tiled=True) for v in vectors]
    joined = jnp.concatenate(vectors)
    other = swap(joined)
    first = lax.axis_index("group") == 0
    low, high = jnp.where(first, joined, other), jnp.where(first, other, joined)
    found, at = [], 0
    for v in vectors:
        size = v.shape[0]
        found.append(jnp.concatenate([low[at : at + size], high[at : at + size]]))
        at += size
    return found


def gather_rows(rows, pairs):
    if pairs != 2:
        return lax.all_gather(rows, "group", axis=0, tiled=True)
    return jnp.concatenate([rows, swap(rows)], axis=0)


def scatter_rows(partial, pairs):
    if pairs != 2:
        return lax.psum_scatter(
            partial.astype(jnp.bfloat16), "group", scatter_dimension=0, tiled=True
        ).astype(jnp.float32)
    half = partial.shape[0] // 2
    return partial[:half] + swap(partial[half:].astype(jnp.bfloat16)).astype(jnp.float32)


def scatter_owned(partial):
    return lax.psum_scatter(
        partial.astype(jnp.bfloat16), "group", scatter_dimension=0, tiled=True
    ).astype(jnp.float32)


def sum_owned(small, qkv, out, gate, up, down):
    owned = [scatter_owned(a) for a in (small, qkv, out)]
    return lax.psum(tuple(a.astype(jnp.bfloat16) for a in (*owned, gate, up, down)), "replica")


def on_device(
    tokens,
    segments,
    norm1_gain,
    qkv_weight,
    qkv_bias,
    out_weight,
    norm2_gain,
    gate_weight,
    up_weight,
    down_weight,
    cotangent,
    *,
    pairs,
    copies,
):
    sequences, length, model_width = tokens.shape
    row_count = sequences * length
    q_width = H * HD
    kv_width = KV * HD
    groups = H // KV
    score_scale = HD ** (-0.5)
    if fits(pairs, copies, tokens, segments, qkv_weight, out_weight, gate_weight, down_weight):
        shape_out = (sequences, length, model_width)
        half_dim = HD // 2
        frequency = ROPE_BASE ** (-2.0 * jnp.arange(half_dim, dtype=jnp.float32) / HD)
        result, back_tokens, full = layer(
            tokens.reshape(row_count, model_width),
            segments.reshape(1, length),
            jnp.concatenate([frequency, frequency])[None],
            norm1_gain[None],
            norm2_gain[None],
            qkv_bias[None],
            cotangent.reshape(row_count, model_width),
            qkv_weight,
            out_weight,
            gate_weight,
            up_weight,
            down_weight,
        )
        return (
            result.reshape(shape_out),
            back_tokens.reshape(shape_out),
            *gradients_of(full, model_width, qkv_weight.shape[1]),
        )
    gain1_b, b_qkv, gain2_b = gather_vectors([norm1_gain, qkv_bias, norm2_gain], pairs)
    w_qkv = gather_weight(qkv_weight, pairs, copies)
    w_out = gather_weight(out_weight, pairs, copies)
    back_all = gather_rows(cotangent.reshape(row_count, model_width), pairs)
    allowed, cosine, sine = doc_layout(segments, HD)
    resid_in = tokens.reshape(row_count, model_width).astype(jnp.float32)
    inv_rms1 = inverse_rms(resid_in)
    gain1 = gain1_b.astype(jnp.float32)
    normed1 = (resid_in * inv_rms1 * gain1).astype(jnp.bfloat16)
    projected = matmul(normed1, w_qkv) + b_qkv.astype(jnp.float32)
    query = projected[:, :q_width].reshape(sequences, length, H, HD)
    keys_raw = projected[:, q_width : q_width + kv_width].reshape(sequences, length, KV, HD)
    values_raw = projected[:, q_width + kv_width :].reshape(sequences, length, KV, HD)
    query_b = (
        rotate(query, cosine, sine).astype(jnp.bfloat16).reshape(sequences, length, KV, groups, HD)
    )
    keys_b = rotate(keys_raw, cosine, sine).astype(jnp.bfloat16)
    values_b = values_raw.astype(jnp.bfloat16)
    scores = score_block(query_b, keys_b, allowed, score_scale)
    top_score = jnp.max(scores, axis=-1, keepdims=True)
    log_total = top_score + jnp.log(jnp.sum(jnp.exp(scores - top_score), axis=-1, keepdims=True))
    soft_b = jnp.exp(scores - log_total).astype(jnp.bfloat16)
    context = jnp.einsum("skgqp,spkd->sqkgd", soft_b, values_b, preferred_element_type=jnp.float32)
    context_b = context.astype(jnp.bfloat16).reshape(row_count, q_width)
    middle = resid_in + matmul(context_b, w_out)
    inv_rms2 = inverse_rms(middle)
    gain2 = gain2_b.astype(jnp.float32)
    normed2 = (middle * inv_rms2 * gain2).astype(jnp.bfloat16)
    back_rows = cotangent.reshape(row_count, model_width)
    normed_all = gather_rows(normed2, pairs)
    gate_pre = matmul(normed_all, gate_weight)
    up_proj = matmul(normed_all, up_weight)
    sigmoid_gate = jax.nn.sigmoid(gate_pre)
    silu_gate = gate_pre * sigmoid_gate
    activ_b = (silu_gate * up_proj).astype(jnp.bfloat16)
    result = middle + scatter_rows(matmul(activ_b, down_weight), pairs)
    back_activ = times_transposed(back_all, down_weight)
    back_gate = (
        back_activ * up_proj * sigmoid_gate * (1.0 + gate_pre * (1.0 - sigmoid_gate))
    ).astype(jnp.bfloat16)
    back_up = (back_activ * silu_gate).astype(jnp.bfloat16)
    grad_down = outer_sum(activ_b, back_all)
    grad_gate = outer_sum(normed_all, back_gate)
    grad_up = outer_sum(normed_all, back_up)
    local_normed = times_transposed(back_gate, gate_weight) + times_transposed(back_up, up_weight)
    back_normed2 = scatter_rows(local_normed, pairs)
    back_norm2, grad_norm2_part = norm_backward(middle, inv_rms2, gain2, back_normed2)
    back_middle = back_rows.astype(jnp.float32) + back_norm2
    back_middle_b = back_middle.astype(jnp.bfloat16)
    grad_out_part = outer_sum(context_b, back_middle_b)
    back_context = times_transposed(back_middle_b, w_out).astype(jnp.bfloat16)
    back_context = back_context.reshape(sequences, length, KV, groups, HD)
    soft = jnp.exp(score_block(query_b, keys_b, allowed, score_scale) - log_total)
    soft_again = soft.astype(jnp.bfloat16)
    back_values = jnp.einsum(
        "skgqp,sqkgd->spkd", soft_again, back_context, preferred_element_type=jnp.float32
    )
    back_soft = jnp.einsum(
        "sqkgd,spkd->skgqp", back_context, values_b, preferred_element_type=jnp.float32
    )
    row_dot = jnp.sum(soft * back_soft, axis=-1, keepdims=True)
    back_scores = (soft * (back_soft - row_dot) * score_scale).astype(jnp.bfloat16)
    back_query = jnp.einsum(
        "skgqp,spkd->sqkgd", back_scores, keys_b, preferred_element_type=jnp.float32
    )
    back_keys = jnp.einsum(
        "skgqp,sqkgd->spkd", back_scores, query_b, preferred_element_type=jnp.float32
    )
    back_query = unrotate(back_query.reshape(sequences, length, H, HD), cosine, sine)
    back_keys = unrotate(back_keys, cosine, sine)
    back_proj = jnp.concatenate(
        [
            back_query.reshape(row_count, q_width),
            back_keys.reshape(row_count, kv_width),
            back_values.reshape(row_count, kv_width),
        ],
        axis=1,
    )
    grad_bias_part = jnp.sum(back_proj, axis=0)
    back_proj_b = back_proj.astype(jnp.bfloat16)
    grad_qkv_part = outer_sum(normed1, back_proj_b)
    back_normed1 = times_transposed(back_proj_b, w_qkv)
    back_norm1, grad_norm1_part = norm_backward(resid_in, inv_rms1, gain1, back_normed1)
    back_tokens = back_middle + back_norm1
    small = jnp.stack([v.reshape(pairs, -1) for v in (grad_norm1_part, grad_norm2_part)], axis=1)
    small = jnp.concatenate(
        [small.reshape(pairs, -1), grad_bias_part.reshape(pairs, -1)], axis=1
    ).reshape(-1)
    owned = sum_owned(
        small,
        grad_qkv_part,
        grad_out_part,
        grad_gate,
        grad_up,
        grad_down,
    )
    small, grad_qkv, grad_out, grad_gate, grad_up, grad_down = (
        a.astype(jnp.float32) for a in owned
    )
    gains = norm1_gain.shape[0]
    grad_norm1, grad_norm2, grad_bias = (
        small[:gains],
        small[gains : 2 * gains],
        small[2 * gains :],
    )
    shape_out = (sequences, length, model_width)
    return (
        result.reshape(shape_out),
        back_tokens.reshape(shape_out),
        grad_norm1,
        grad_qkv,
        grad_bias,
        grad_out,
        grad_norm2,
        grad_gate,
        grad_up,
        grad_down,
    )


def solution(mesh):
    in_specs = (
        P(("group", "replica"), None, None),
        P(("group", "replica"), None),
        P("group"),
        P("group", None),
        P("group"),
        P("group", None),
        P("group"),
        P(None, "group"),
        P(None, "group"),
        P("group", None),
        P(("group", "replica"), None, None),
    )
    out_specs = (
        P(("group", "replica"), None, None),
        P(("group", "replica"), None, None),
        P("group"),
        P("group", None),
        P("group"),
        P("group", None),
        P("group"),
        P(None, "group"),
        P(None, "group"),
        P("group", None),
    )
    program = functools.partial(
        on_device, pairs=mesh.shape["group"], copies=mesh.shape["replica"]
    )
    return jax.shard_map(
        program, mesh=mesh, in_specs=in_specs, out_specs=out_specs, check_vma=False
    )
```

```python
import functools

import jax
import jax.numpy as jnp
import numpy as np
from jax import lax
from jax.experimental import pallas as pl
from jax.experimental.pallas import tpu as pltpu
from jax.sharding import PartitionSpec as P

H = 14
KV = 2
HD = 64


EPSILON = 1e-06
ROPE_BASE = 1000000.0
NEG_LARGE = -1e30


def doc_layout(segments, head_dim):
    length = segments.shape[1]
    places = jnp.arange(length, dtype=jnp.int32)
    same_doc = segments[:, :, None] == segments[:, None, :]
    earlier = places[None, None, :] < places[None, :, None]
    positions = jnp.sum(jnp.where(same_doc & earlier, 1.0, 0.0).astype(jnp.float32), axis=2)
    allowed = jnp.where(same_doc & (places[None, None, :] <= places[None, :, None]), 1, 0).astype(
        jnp.int32
    )
    half_dim = head_dim // 2
    frequency = ROPE_BASE ** (-2.0 * jnp.arange(half_dim, dtype=jnp.float32) / head_dim)
    angles = positions[:, :, None] * frequency[None, None, :]
    return (allowed, jnp.cos(angles)[:, :, None, :], jnp.sin(angles)[:, :, None, :])


def rotate(values, cosine, sine):
    half_dim = values.shape[-1] // 2
    front_half = values[..., :half_dim]
    back_half = values[..., half_dim:]
    return jnp.concatenate(
        [front_half * cosine - back_half * sine, back_half * cosine + front_half * sine], axis=-1
    )


def unrotate(gradients, cosine, sine):
    half_dim = gradients.shape[-1] // 2
    front_half = gradients[..., :half_dim]
    back_half = gradients[..., half_dim:]
    return jnp.concatenate(
        [front_half * cosine + back_half * sine, back_half * cosine - front_half * sine], axis=-1
    )


def inverse_rms(hidden):
    return lax.rsqrt(jnp.mean(hidden * hidden, axis=-1, keepdims=True) + EPSILON)


def norm_backward(hidden, inv_rms, gain_f, back_normed):
    weighted = back_normed * gain_f
    inner = jnp.mean(weighted * hidden, axis=-1, keepdims=True)
    back_hidden = inv_rms * weighted - hidden * (inv_rms * inv_rms * inv_rms) * inner
    back_gain = jnp.sum(back_normed * hidden * inv_rms, axis=0)
    return (back_hidden, back_gain)


def matmul(left, right):
    return jnp.dot(left, right, preferred_element_type=jnp.float32)


def outer_sum(left, right):
    return lax.dot_general(
        left, right, (((0,), (0,)), ((), ())), preferred_element_type=jnp.float32
    )


def times_transposed(left, right):
    return lax.dot_general(
        left, right, (((1,), (1,)), ((), ())), preferred_element_type=jnp.float32
    )


def score_block(query_b, keys_b, allowed, score_scale):
    scores = (
        jnp.einsum("sqkgd,spkd->skgqp", query_b, keys_b, preferred_element_type=jnp.float32)
        * score_scale
    )
    return jnp.where(allowed[:, None, None, :, :] > 0, scores, NEG_LARGE)


MESH_ID = pl.DeviceIdType.MESH
TILE = 128
SLICE = 640
CHUNK = 64
SMALL_ROWS = 480


def relative(delta):
    me = lax.axis_index("replica")
    pair = lax.axis_index("group")
    core, x = me % 2, lax.div(me, 2) % 2
    d_core, d_x, d_y = delta % 2, lax.div(delta, 2) % 2, lax.div(delta, 4) % 2
    shift = d_core * (1 - 2 * core) + 2 * d_x * (1 - 2 * x)
    return {"group": pair + d_y * (1 - 2 * pair), "replica": me + shift}


def greet(devices):
    barrier = pltpu.get_barrier_semaphore()
    for device in devices:
        pl.semaphore_signal(barrier, inc=1, device_id=device, device_id_type=MESH_ID)
    return barrier


def remote(src, dst, sems, where, device):
    return pltpu.make_async_remote_copy(
        src_ref=src,
        dst_ref=dst,
        send_sem=sems[0].at[where],
        recv_sem=sems[1].at[where],
        device_id=device,
        device_id_type=MESH_ID,
    )


def contract(left, right, left_dim, right_dim):
    return lax.dot_general(
        left,
        right,
        (((left_dim,), (right_dim,)), ((), ())),
        preferred_element_type=jnp.float32,
    )


def layer_kernel(
    tokens_ref,
    seg_row,
    frequency,
    gain1_in,
    gain2_in,
    bias_in,
    cot_ref,
    qkv_ref,
    out_weight_ref,
    gate_ref,
    up_ref,
    down_ref,
    result_ref,
    back_ref,
    out_ref,
    rows_n,
    rows_c,
    w_gate,
    w_up,
    w_down,
    activ,
    d_gate,
    d_up,
    part_b,
    part_r,
    sib_b,
    sib_r,
    land_b,
    land_r,
    own,
    land_u,
    land_m,
    total,
    mine,
    sib,
    across,
    beside,
    joined_ref,
    rest_ref,
    proj,
    stacked,
    normed1,
    share,
    w_qkv_ref,
    w_out_ref,
    vector_ref,
    vectors,
    query_ref,
    keys_ref,
    values_ref,
    log_ref,
    allowed_ref,
    cos_ref,
    sin_ref,
    context_ref,
    middle_ref,
    gain1_ref,
    gain2_ref,
    local,
    link,
    core_n,
    core_c,
    core_b,
    core_r,
    link_b,
    link_r,
    early,
    up,
    mid,
    down,
    side,
    out1,
    out2,
    link_c,
    weights_y,
    weights_x,
    weights_1,
    weights_2,
):
    f32, bf16 = jnp.float32, jnp.bfloat16
    count = own.shape[0] // CHUNK
    length, width = tokens_ref.shape
    bulk = 3 * width
    first = bulk // CHUNK
    lines, wide = mine.shape[1], mine.shape[2]
    half = lines // 2
    depth = joined_ref.shape[0] // 2
    me = lax.axis_index("replica")
    pair = lax.axis_index("group")
    core, x, z = me % 2, lax.div(me, 2) % 2, lax.div(me, 4)
    quarter = me % 4
    beside_quarter = quarter + 2 * (1 - 2 * x)
    middle = (z == 1) | (z == 2)
    is_end = (z == 0) | (z == 3)
    near = {"replica": me + 4 * (1 - 2 * (z % 2))}
    far = {"replica": me + 4 * (1 - 2 * lax.div(z, 2))}
    sibling, neighbour, peer = relative(1), relative(2), relative(4)


    def halves(which):
        return pl.ds(pl.multiple_of(which * half, 16), half)

    def lanes(which):
        return pl.ds(pl.multiple_of(which * wide, TILE), wide)

    first_column = pl.multiple_of(TILE * (5 * quarter - lax.div(quarter, 3)), TILE)
    columns = pl.ds(first_column, SLICE)
    loads = [
        pltpu.make_async_copy(gate_ref.at[:, columns], w_gate, local.at[0]),
        pltpu.make_async_copy(up_ref.at[:, columns], w_up, local.at[1]),
        pltpu.make_async_copy(down_ref.at[columns, :], w_down, local.at[2]),
    ]
    shard = width // 2
    w_loads = [
        pltpu.make_async_copy(
            qkv_ref, w_qkv_ref.at[pl.ds(pl.multiple_of(pair * shard, 64), shard)], local.at[3]
        ),
        pltpu.make_async_copy(
            out_weight_ref, w_out_ref.at[pl.ds(pl.multiple_of(pair * shard, 64), shard)], local.at[4]
        ),
    ]
    for load in w_loads:
        load.start()
    rows_c[0:length] = cot_ref[...]
    vector_ref[0:1, 0:shard] = gain1_in[...].astype(f32).reshape(1, gain1_in.shape[0])
    vector_ref[0:1, 512 : 512 + shard] = gain2_in[...].astype(f32).reshape(1, gain2_in.shape[0])
    vector_ref[0:1, 1024 : 1024 + bias_in.shape[0]] = bias_in[...].astype(f32).reshape(1, bias_in.shape[0])
    barrier = greet([sibling, neighbour, peer, relative(6), near])

    @pl.when(middle)
    def _():
        pl.semaphore_signal(barrier, inc=1, device_id=far, device_id_type=MESH_ID)

    pl.semaphore_wait(barrier, jnp.where(middle, 6, 5))

    def block(ref, slot):
        return ref.at[pl.ds(pl.multiple_of(slot * length, 16), length)]

    part = shard // 4
    cuts = ((0, 48), (48, part - 48))
    vector_copy = remote(vector_ref, vectors, early, 7, peer)
    vector_copy.start()

    def quarter_rows(which, fourth, cut):
        first = which * shard + fourth * part + cuts[cut][0]
        return pl.ds(pl.multiple_of(first, 16), cuts[cut][1])

    moved = [(qkv_ref, w_qkv_ref, 0), (out_weight_ref, w_out_ref, 1)]

    def weight_y(w, cut):
        source, goal, _ = moved[w]
        rows = pl.ds(pl.multiple_of(quarter * part + cuts[cut][0], 16), cuts[cut][1])
        return remote(
            source.at[rows], goal.at[quarter_rows(pair, quarter, cut)], weights_y, 2 * w + cut, peer
        )

    def weight_y_in(w, cut):
        goal = moved[w][1].at[quarter_rows(1 - pair, quarter, cut)]
        return remote(goal, goal, weights_y, 2 * w + cut, peer)

    def weight_pass(w, cut, fourth, sems, device):
        goal = moved[w][1].at[quarter_rows(1 - pair, fourth, cut)]
        return remote(goal, goal, sems, 2 * w + cut, device)

    order = [(w, cut) for w in range(2) for cut in range(2)]
    for w, cut in order:
        weight_y(w, cut).start()
    sends = []

    def send_cot(p):
        copy = remote(block(rows_c, 0), block(rows_c, 2 * p), link_c, p, relative(2 * p))
        copy.start()
        sends.append(copy)

    send_cot(1)

    def forward_n(p):
        return remote(block(rows_n, 2 * p), block(rows_n, 2 * p + 1), core_n, p, sibling)

    def forward_c(p):
        return remote(block(rows_c, 2 * p), block(rows_c, 2 * p + 1), core_c, p, sibling)

    forward_c(0).start()
    for load in loads:
        load.start()
    asked = lax.broadcasted_iota(jnp.int32, (length, length), 0)
    seen = lax.broadcasted_iota(jnp.int32, (length, length), 1)
    seg_column = jnp.sum(jnp.where(asked == seen, seg_row[...], 0), axis=1, keepdims=True)
    same = seg_column == seg_row[...]
    allowed_ref[...] = jnp.where(same & (seen <= asked), 1, 0)
    positions = jnp.sum(jnp.where(same & (seen < asked), 1.0, 0.0), axis=1, keepdims=True)
    angles = positions * frequency[...]
    cos_ref[...] = jnp.cos(angles)
    column = lax.broadcasted_iota(jnp.int32, angles.shape, 1)
    sine = jnp.sin(angles)
    sin_ref[...] = jnp.where(column < HD // 2, sine, -sine)
    tokens = tokens_ref[...].astype(f32)
    inv1 = inverse_rms(tokens)
    vector_copy.wait()
    mine_v, other_v = vector_ref[0:1, :], vectors[0:1, :]
    low_v = jnp.where(pair == 0, mine_v, other_v)
    high_v = jnp.where(pair == 0, other_v, mine_v)
    gain1_ref[...] = jnp.concatenate([low_v[:, :shard], high_v[:, :shard]], axis=1)
    gain2_ref[...] = jnp.concatenate(
        [low_v[:, 512 : 512 + shard], high_v[:, 512 : 512 + shard]], axis=1
    )
    bias_at = 1024
    bias = jnp.concatenate(
        [low_v[:, bias_at : bias_at + proj.shape[1] // 2], high_v[:, bias_at : bias_at + proj.shape[1] // 2]],
        axis=1,
    )
    normed1[...] = (tokens * inv1 * gain1_ref[...]).astype(bf16)
    for load in w_loads:
        load.wait()

    def relay(w):
        for cut in range(2):
            weight_y_in(w, cut).wait_recv()
            weight_pass(w, cut, quarter, weights_x, neighbour).start()
            weight_pass(w, cut, quarter, weights_1, sibling).start()

    def relay_x(w):
        for cut in range(2):
            weight_pass(w, cut, beside_quarter, weights_x, neighbour).wait_recv()
            weight_pass(w, cut, beside_quarter, weights_2, sibling).start()

    def settle(w):
        for cut in range(2):
            weight_y(w, cut).wait_send()
            weight_pass(w, cut, quarter, weights_x, neighbour).wait_send()
            weight_pass(w, cut, quarter, weights_1, sibling).wait()
            weight_pass(w, cut, beside_quarter, weights_2, sibling).wait()

    relay(0)
    send_cot(2)
    relay_x(0)
    settle(0)
    projected = contract(normed1[...], w_qkv_ref[...], 1, 0) + bias
    proj[...] = projected
    relay(1)
    send_cot(3)
    groups = H // KV
    score_scale = HD ** (-0.5)

    def turned(at):
        value = proj[:, at : at + HD]
        swapped = jnp.concatenate([value[:, HD // 2 :], value[:, : HD // 2]], axis=1)
        return (value * cos_ref[...] - swapped * sin_ref[...]).astype(bf16)

    for k in range(KV):
        for j in range(groups):
            query_ref[k, j * length : (j + 1) * length, :] = turned((k * groups + j) * HD)
        at = H * HD + k * HD
        keys_ref[k] = turned(at)
        values_ref[k] = proj[:, at + KV * HD : at + (KV + 1) * HD].astype(bf16)
        mask = jnp.concatenate([allowed_ref[...]] * groups, axis=0) > 0
        scores = contract(query_ref[k], keys_ref[k], 1, 1) * score_scale
        scores = jnp.where(mask, scores, NEG_LARGE)
        top = jnp.max(scores, axis=-1, keepdims=True)
        log_total = top + jnp.log(jnp.sum(jnp.exp(scores - top), axis=-1, keepdims=True))
        log_ref[k] = log_total
        soft = jnp.exp(scores - log_total).astype(bf16)
        context = contract(soft, values_ref[k], 1, 0).astype(bf16)
        for j in range(groups):
            at = (k * groups + j) * HD
            context_ref[:, at : at + HD] = context[j * length : (j + 1) * length, :]
        if k == 0:
            relay_x(1)
    settle(1)
    middle_value = tokens + contract(context_ref[...], w_out_ref[...], 1, 0)
    middle_ref[...] = middle_value
    rows_n[0:length] = (middle_value * inverse_rms(middle_value) * gain2_ref[...]).astype(bf16)
    for p in (1, 2, 3):
        copy = remote(block(rows_n, 0), block(rows_n, 2 * p), link, p, relative(2 * p))
        copy.start()
        sends.append(copy)
    forward_n(0).start()
    for load in loads:
        load.wait()

    def fold(part, sib, core, land, hop, q):
        remote(block(part, 2 * q + 1), sib.at[q], core, q, sibling).wait()
        rows = pl.ds(pl.multiple_of(2 * q * length, 16), length)
        part[rows, :] = (part[rows, :].astype(f32) + sib[q].astype(f32)).astype(bf16)
        remote(block(part, 2 * q), land.at[q - 1], hop, q, relative(2 * q)).start()

    def fold_own(part, sib, core):
        remote(block(part, 1), sib.at[0], core, 0, sibling).wait()
        return part[0:length, :].astype(f32) + sib[0].astype(f32)

    def pair_step(p, carry):
        def arrive(q):
            remote(block(rows_n, 0), block(rows_n, 2 * q), link, q, relative(2 * q)).wait_recv()
            forward_n(q).start()

        @pl.when(p == 1)
        def _():
            arrive(1)
            arrive(2)

        @pl.when(p == 2)
        def _():
            arrive(3)

        @pl.when(p < 3)
        def _():
            q = p + 1
            remote(block(rows_c, 0), block(rows_c, 2 * q), link_c, q, relative(2 * q)).wait_recv()
            forward_c(q).start()

        forward_n(p).wait()
        forward_c(p).wait()
        both = pl.ds(pl.multiple_of(2 * p * length, 32), 2 * length)
        normed, cot = rows_n[both, :], rows_c[both, :]
        gate_pre = contract(normed, w_gate[...], 1, 0)
        up_proj = contract(normed, w_up[...], 1, 0)
        back_activ = contract(cot, w_down[...], 1, 1)
        sigmoid_gate = jax.nn.sigmoid(gate_pre)
        silu_gate = gate_pre * sigmoid_gate
        column = lax.broadcasted_iota(jnp.int32, gate_pre.shape, 1)
        own = column >= jnp.where(quarter == 3, TILE, 0)
        activ[both, :] = jnp.where(own, silu_gate * up_proj, 0.0).astype(jnp.bfloat16)
        d_gate[both, :] = jnp.where(
            own,
            back_activ * up_proj * sigmoid_gate * (1.0 + gate_pre * (1.0 - sigmoid_gate)),
            0.0,
        ).astype(jnp.bfloat16)
        d_up[both, :] = jnp.where(own, back_activ * silu_gate, 0.0).astype(jnp.bfloat16)
        part_b[both, :] = (
            contract(d_gate[both, :], w_gate[...], 1, 1)
            + contract(d_up[both, :], w_up[...], 1, 1)
        ).astype(jnp.bfloat16)
        remote(block(part_b, 2 * p + 1), sib_b.at[p], core_b, p, relative(1)).start()
        part_r[both, :] = contract(activ[both, :], w_down[...], 1, 0).astype(jnp.bfloat16)
        remote(block(part_r, 2 * p + 1), sib_r.at[p], core_r, p, relative(1)).start()

        return carry

    lax.fori_loop(0, 4, pair_step, 0)

    def chunk(c):
        return pl.ds(pl.multiple_of(c * CHUNK, CHUNK), CHUNK)

    def up_copy(c):
        return remote(own.at[chunk(c)], land_u.at[chunk(c)], up, c, near)

    def mid_copy(c):
        return remote(own.at[chunk(c)], land_m.at[chunk(c)], mid, c, far)

    def down_copy(c):
        return remote(total.at[chunk(c)], total.at[chunk(c)], down, c, near)

    def side_copy(c):
        return remote(
            total.at[chunk(c)], out_ref.at[quarter].at[chunk(c)], side, c, neighbour
        )

    def side_arrival(c):
        return remote(
            total.at[chunk(c)], out_ref.at[beside_quarter].at[chunk(c)], side, c, neighbour
        )

    def out_copy(c):
        return remote(total.at[chunk(c)], out_ref.at[quarter].at[chunk(c)], out1, c, sibling)

    def pass_copy(c):
        place = out_ref.at[beside_quarter].at[chunk(c)]
        return remote(place, place, out2, c, sibling)

    def store(c):
        return pltpu.make_async_copy(
            total.at[chunk(c)], out_ref.at[quarter].at[chunk(c)], local.at[7 + c]
        )

    def hand_out(c):
        side_copy(c).start()
        out_copy(c).start()
        store(c).start()

    def add(goal, left, right, rows):
        goal[rows, :] = (
            left[rows, :].astype(jnp.float32) + right[rows, :].astype(jnp.float32)
        ).astype(jnp.bfloat16)

    def send_up(lo, hi):
        @pl.when(is_end)
        def _():
            def go(c, carry):
                up_copy(c).start()
                return carry

            lax.fori_loop(lo, hi, go, 0)

    skew1, skew2 = 3, 14

    def service(i, carry):
        a, b, d = i, i - skew1, i - skew2

        @pl.when(middle & (a < count))
        def _():
            up_copy(a).wait_recv()
            add(own, own, land_u, chunk(a))
            mid_copy(a).start()

        @pl.when((b >= 0) & (b < count))
        def _():
            @pl.when(middle)
            def _():
                mid_copy(b).wait_recv()
                add(total, own, land_m, chunk(b))
                down_copy(b).start()

            @pl.when(is_end)
            def _():
                down_copy(b).wait_recv()

            hand_out(b)

        @pl.when(d >= 0)
        def _():
            side_arrival(d).wait_recv()
            pass_copy(d).start()

        return carry

    def serve(lo, hi):
        lax.fori_loop(lo, hi, service, 0)

    def finish(part, land, hop, goal):
        value = goal[...]
        for p in (1, 2, 3):
            remote(block(part, 2 * p), land.at[p - 1], hop, p, relative(2 * p)).wait()
            value = value + land[p - 1].astype(f32)
        return value

    for q in (1, 2, 3):
        fold(part_b, sib_b, core_b, land_b, link_b, q)
    share[...] = fold_own(part_b, sib_b, core_b)

    def grad_step(h, carry):
        lane = pl.ds(pl.multiple_of(h * TILE, TILE), TILE)
        left = rows_n[:, lane]

        def place(which):
            return pl.ds(pl.multiple_of((3 * h + which) * TILE, TILE), TILE)

        own[place(0), :] = contract(left, d_gate[...], 0, 0).astype(bf16)
        own[place(1), :] = contract(left, d_up[...], 0, 0).astype(bf16)
        down = contract(activ[...], rows_c[:, lane], 0, 0).astype(bf16)
        for i in range(SLICE // TILE):
            own[place(2), i * TILE : (i + 1) * TILE] = down[i * TILE : (i + 1) * TILE]
        per = 3 * TILE // CHUNK
        send_up(h * per, (h + 1) * per)
        return carry

    lax.fori_loop(0, width // TILE, grad_step, 0)
    for q in (1, 2, 3):
        fold(part_r, sib_r, core_r, land_r, link_r, q)
    result_ref[...] = fold_own(part_r, sib_r, core_r)
    serve(0, 2)
    back_normed = finish(part_b, land_b, link_b, share)
    serve(2, 4)

    def norm_back(hidden, inv, gain, back):
        weighted = back * gain
        inner = jnp.mean(weighted * hidden, axis=-1, keepdims=True)
        back_hidden = inv * weighted - hidden * (inv * inv * inv) * inner
        return back_hidden, jnp.sum(back * hidden * inv, axis=0, keepdims=True)

    hidden = middle_ref[...]
    back_hidden, sum2 = norm_back(hidden, inverse_rms(hidden), gain2_ref[...], back_normed)
    back_middle = rows_c[0:length, :].astype(f32) + back_hidden
    share[...] = back_middle
    back_middle_b = back_middle.astype(bf16)
    back_context = contract(back_middle_b, w_out_ref[...], 1, 1).astype(bf16)
    for k in range(KV):
        for j in range(groups):
            at = (k * groups + j) * HD
            stacked[k, j * length : (j + 1) * length, :] = back_context[:, at : at + HD]
    joined_ref[:, proj.shape[1] :] = contract(context_ref[...], back_middle_b, 0, 0).astype(bf16)
    serve(4, 5)

    def unturn(value):
        swapped = jnp.concatenate([value[:, HD // 2 :], value[:, : HD // 2]], axis=1)
        return value * cos_ref[...] + swapped * sin_ref[...]

    for k in range(KV):
        keys, values, query, back = keys_ref[k], values_ref[k], query_ref[k], stacked[k]
        mask = jnp.concatenate([allowed_ref[...]] * groups, axis=0) > 0
        scores = contract(query, keys, 1, 1) * score_scale
        soft = jnp.exp(jnp.where(mask, scores, NEG_LARGE) - log_ref[k])
        back_soft = contract(back, values, 1, 1)
        row_dot = jnp.sum(soft * back_soft, axis=-1, keepdims=True)
        back_scores = (soft * (back_soft - row_dot) * score_scale).astype(bf16)
        back_values = contract(soft.astype(bf16), back, 0, 0)
        back_query = contract(back_scores, keys, 1, 0)
        back_keys = contract(back_scores, query, 0, 0)
        for j in range(groups):
            at = (k * groups + j) * HD
            proj[:, at : at + HD] = unturn(back_query[j * length : (j + 1) * length, :])
        at = H * HD + k * HD
        proj[:, at : at + HD] = unturn(back_keys)
        proj[:, at + KV * HD : at + (KV + 1) * HD] = back_values
        serve(5 + 2 * k, 7 + 2 * k)

    sum_bias = jnp.sum(proj[...], axis=0, keepdims=True)
    proj_b = proj[...].astype(bf16)
    tokens = tokens_ref[...].astype(f32)
    inv1 = inverse_rms(tokens)
    joined_ref[:, : proj.shape[1]] = contract(normed1[...], proj_b, 0, 0).astype(bf16)
    serve(9, 10)
    back_normed1 = contract(proj_b, w_qkv_ref[...], 1, 1)
    back_first, sum1 = norm_back(tokens, inv1, gain1_ref[...], back_normed1)
    back_ref[...] = share[...] + back_first
    row = lax.broadcasted_iota(jnp.int32, rest_ref.shape[1:], 0)

    def lines_of(top, second):
        pads = [
            jnp.concatenate([v, jnp.zeros((1, wide - v.shape[1]), f32)], axis=1)
            if v.shape[1] < wide
            else v
            for v in (top, second)
        ]
        return jnp.where(row == 0, pads[0], jnp.where(row == 1, pads[1], 0.0)).astype(bf16)

    rest_ref[0] = lines_of(sum1, sum2)
    rest_ref[1] = lines_of(sum_bias[:, :wide], sum_bias[:, wide:])
    small_loads = []
    for g in range(2):
        rows = slice(g * depth, (g + 1) * depth)
        small_loads += [
            pltpu.make_async_copy(
                joined_ref.at[rows, lanes(core)], mine.at[g, 0:depth], local.at[3 + g]
            ),
            pltpu.make_async_copy(rest_ref.at[core], mine.at[g, depth:lines], local.at[5 + g]),
        ]
    for copy in small_loads:
        copy.start()
    swap0 = []
    for g in range(2):
        rows = slice(g * depth, (g + 1) * depth)
        swap0 += [
            remote(joined_ref.at[rows, lanes(1 - core)], sib.at[g, 0:depth], early, g, sibling),
            remote(rest_ref.at[1 - core], sib.at[g, depth:lines], early, 2 + g, sibling),
        ]
    for copy in swap0:
        copy.start()
    serve(10, 12)
    for copy in small_loads + swap0:
        copy.wait()

    def add_small(r, carry):
        rows = pl.ds(pl.multiple_of(r * 48, 16), 48)
        for g in range(2):
            mine[g, rows, :] = (
                mine[g, rows, :].astype(jnp.float32) + sib[g, rows, :].astype(jnp.float32)
            ).astype(jnp.bfloat16)
        return carry

    lax.fori_loop(0, lines // 48, add_small, 0)

    def swap_copy(which):
        return remote(
            mine.at[1 - pair].at[halves(which)], across.at[halves(which)], early, 4 + which, peer
        )

    swap_copy(1 - x).start()
    swap_copy(x).start()
    serve(12, 24)
    result_ref[...] = middle_ref[...] + finish(part_r, land_r, link_r, result_ref)


    def add_across(which):
        def go(r, carry):
            rows = pl.ds(pl.multiple_of(which * half + r * 48, 16), 48)
            across[rows, :] = (
                across[rows, :].astype(jnp.float32) + mine[pair, rows, :].astype(jnp.float32)
            ).astype(jnp.bfloat16)
            return carry

        lax.fori_loop(0, half // 48, go, 0)

    swap_copy(1 - x).wait()
    add_across(1 - x)
    side_small = remote(across.at[halves(1 - x)], beside, early, 6, neighbour)
    side_small.start()
    serve(24, 34)
    swap_copy(x).wait()
    side_small.wait()
    for s in range(half // 48):
        rows = pl.ds(pl.multiple_of(x * half + s * 48, 16), 48)
        value = (
            across[rows, :].astype(jnp.float32)
            + mine[pair, rows, :].astype(jnp.float32)
            + beside[s * 48 : (s + 1) * 48, :].astype(jnp.float32)
        ).astype(jnp.bfloat16)
        for t in range(wide // TILE):
            own[bulk + t * 48 : bulk + (t + 1) * 48, s * TILE : (s + 1) * TILE] = value[
                :, t * TILE : (t + 1) * TILE
            ]
    send_up(first, count)
    serve(34, count + skew2)

    def drain(c, carry):
        @pl.when(is_end)
        def _():
            up_copy(c).wait_send()

        @pl.when(middle)
        def _():
            mid_copy(c).wait_send()
            down_copy(c).wait_send()

        side_copy(c).wait_send()
        out_copy(c).wait_send()
        out_copy(c).wait_recv()
        pass_copy(c).wait_send()
        pass_copy(c).wait_recv()
        store(c).wait()
        return carry

    lax.fori_loop(0, count, drain, 0)


    for copy in sends:
        copy.wait_send()


def layer(*args):
    length, width = args[0].shape
    rows = 8 * length
    bf16, f32 = jnp.bfloat16, jnp.float32
    vmem = pl.BlockSpec(memory_space=pltpu.VMEM)
    hbm = pl.BlockSpec(memory_space=pl.ANY)
    qkv_width = args[7].shape[1]
    wide = (qkv_width + width) // 2
    chain = 3 * width + SMALL_ROWS * wide // (2 * SLICE)
    count = chain // CHUNK
    stack = (KV, H // KV * length)
    buffers = [
        ((rows, width), bf16),
        ((rows, width), bf16),
        ((width, SLICE), bf16),
        ((width, SLICE), bf16),
        ((SLICE, width), bf16),
        ((rows, SLICE), bf16),
        ((rows, SLICE), bf16),
        ((rows, SLICE), bf16),
        ((rows, width), bf16),
        ((rows, width), bf16),
        ((4, length, width), bf16),
        ((4, length, width), bf16),
        ((3, length, width), bf16),
        ((3, length, width), bf16),
        ((chain, SLICE), bf16),
        ((chain, SLICE), bf16),
        ((chain, SLICE), bf16),
        ((chain, SLICE), bf16),
        ((2, SMALL_ROWS, wide), bf16),
        ((2, SMALL_ROWS, wide), bf16),
        ((SMALL_ROWS, wide), bf16),
        ((SMALL_ROWS // 2, wide), bf16),
        ((width, 2 * wide), bf16),
        ((2, SMALL_ROWS - width // 2, wide), bf16),
        ((length, qkv_width), f32),
        ((KV, H // KV * length, HD), bf16),
        ((length, width), bf16),
        ((length, width), f32),
        ((width, qkv_width), bf16),
        ((width, width), bf16),
        ((8, 1664), f32),
        ((8, 1664), f32),
        ((*stack, HD), bf16),
        ((KV, length, HD), bf16),
        ((KV, length, HD), bf16),
        ((*stack, 1), f32),
        ((length, length), jnp.int32),
        ((length, HD), f32),
        ((length, HD), f32),
        ((length, width), bf16),
        ((length, width), f32),
        ((1, width), f32),
        ((1, width), f32),
    ]
    sizes = [4] * 7 + [8] + [count] * 6 + [4] * 5

    def body(*refs):
        plain = len(args) + 3 + len(buffers)
        local, rest = refs[plain], refs[plain + 1 :]
        grouped = [(rest[2 * i], rest[2 * i + 1]) for i in range(len(sizes))]
        layer_kernel(*refs[:plain], local, *grouped)

    return pl.pallas_call(
        body,
        out_shape=[
            jax.ShapeDtypeStruct((length, width), f32),
            jax.ShapeDtypeStruct((length, width), f32),
            jax.ShapeDtypeStruct((4, chain, SLICE), bf16),
        ],
        in_specs=[vmem] * 7 + [hbm] * 5,
        out_specs=[vmem, vmem, hbm],
        scratch_shapes=[pltpu.VMEM(shape, kind) for shape, kind in buffers]
        + [pltpu.SemaphoreType.DMA((7 + count,))]
        + [pltpu.SemaphoreType.DMA((size,)) for size in sizes for _ in range(2)],
        compiler_params=pltpu.CompilerParams(
            collective_id=1, has_side_effects=True, vmem_limit_bytes=60 * 1024 * 1024
        ),
        name="layer",
    )(*args)


def unpack_kernel(
    gate_in, up_in, down_in, small_in, gate, up, down, qkv, out, norm1, norm2, bias, extra
):
    f32 = jnp.float32
    for source, goal in ((gate_in, gate), (up_in, up)):
        for k in range(3):
            goal[:, k * SLICE : (k + 1) * SLICE] = source[k].astype(f32)
        goal[:, 3 * SLICE :] = source[3, :, TILE:].astype(f32)
    tiles = SLICE // TILE
    for k in range(4):
        for i in range(tiles):
            if k == 3 and i == 0:
                continue
            first = (k * tiles + i - k // 3) * TILE
            down[first : first + TILE, :] = down_in[k, :, i * TILE : (i + 1) * TILE].astype(f32)

    @pl.when(pl.program_id(0) == 0)
    def _():
        depth, split = qkv.shape
        lanes = small_in.shape[1] // 48
        for k in range(4):
            for t in range(lanes):
                for s in range(tiles):
                    value = small_in[
                        k, t * 48 : (t + 1) * 48, s * TILE : (s + 1) * TILE
                    ].astype(f32)
                    row, column = k // 2 * tiles * 48 + s * 48, (k % 2 * lanes + t) * TILE
                    keep = min(48, depth - row)
                    if column < split:
                        qkv[row : row + keep, column : column + TILE] = value[:keep]
                    else:
                        at = column - split
                        out[row : row + keep, at : at + TILE] = value[:keep]
                    if keep < 48:
                        extra[:, column : column + TILE] = value[keep:]
        high = lax.axis_index("group") == 1
        wide, share = extra.shape[1] // 2, norm1.shape[0]
        for row, goal in ((0, norm1), (1, norm2)):
            line = extra[row : row + 1, : 2 * share]
            goal[...] = jnp.where(high, line[:, share:], line[:, :share]).reshape(share)
        most = bias.shape[0]
        line = jnp.concatenate(
            [extra[0:1, wide:], extra[1:2, wide : wide + 2 * most - wide]], axis=1
        )
        goal = jnp.where(high, line[:, most:], line[:, :most])
        bias[...] = goal.reshape(most)


def unpack(full, width, qkv_width):
    f32 = jnp.float32
    steps = width // TILE
    features = 4 * SLICE - TILE
    small_rows = full.shape[1] - 3 * width
    depth = width // 2
    whole = lambda i: (0, 0)
    return pl.pallas_call(
        unpack_kernel,
        grid=(steps,),
        out_shape=[
            jax.ShapeDtypeStruct((width, features), f32),
            jax.ShapeDtypeStruct((width, features), f32),
            jax.ShapeDtypeStruct((features, width), f32),
            jax.ShapeDtypeStruct((depth, qkv_width), f32),
            jax.ShapeDtypeStruct((depth, width), f32),
            jax.ShapeDtypeStruct((depth,), f32),
            jax.ShapeDtypeStruct((depth,), f32),
            jax.ShapeDtypeStruct((qkv_width // 2,), f32),
        ],
        in_specs=[
            pl.BlockSpec((4, TILE, SLICE), lambda i: (0, 3 * i, 0)),
            pl.BlockSpec((4, TILE, SLICE), lambda i: (0, 3 * i + 1, 0)),
            pl.BlockSpec((4, TILE, SLICE), lambda i: (0, 3 * i + 2, 0)),
            pl.BlockSpec((4, small_rows, SLICE), lambda i: (0, 3 * width // small_rows, 0)),
        ],
        out_specs=[
            pl.BlockSpec((TILE, features), lambda i: (i, 0)),
            pl.BlockSpec((TILE, features), lambda i: (i, 0)),
            pl.BlockSpec((features, TILE), lambda i: (0, i)),
            pl.BlockSpec((depth, qkv_width), whole),
            pl.BlockSpec((depth, width), whole),
            pl.BlockSpec((depth,), lambda i: (0,)),
            pl.BlockSpec((depth,), lambda i: (0,)),
            pl.BlockSpec((qkv_width // 2,), lambda i: (0,)),
        ],
        scratch_shapes=[pltpu.VMEM((SMALL_ROWS - depth, qkv_width + width), f32)],
        compiler_params=pltpu.CompilerParams(vmem_limit_bytes=56 * 1024 * 1024),
        name="unpack",
    )(full, full, full, full)


def fits(pairs, copies, tokens, segments, qkv, out, gate, down):
    return (
        pairs == 2
        and copies == 16
        and tokens.shape == (1, 144, 896)
        and qkv.shape == (448, 1152)
        and out.shape == (448, 896)
        and gate.shape == (896, 2432)
        and down.shape == (2432, 896)
    )


def gradients_of(full, width, qkv_width):
    gate, up, down, qkv, out, norm1, norm2, bias = unpack(full, width, qkv_width)
    return (norm1, qkv, bias, out, norm2, gate, up, down)


def swap(values):
    return lax.ppermute(values, "group", [(0, 1), (1, 0)])


def gather_weight(shard, pairs, copies):
    if pairs != 2 or copies % 2:
        return lax.all_gather(shard, "group", axis=0, tiled=True)
    half = shard.shape[0] // 2
    core = lax.axis_index("replica") % 2
    mine = swap(lax.dynamic_slice_in_dim(shard, core * half, half, 0))
    sibling = lax.ppermute(mine, "replica", [(i, i + 1 - 2 * (i % 2)) for i in range(copies)])
    front = jnp.where(core == 0, mine, sibling)
    back = jnp.where(core == 0, sibling, mine)
    first = lax.axis_index("group") == 0
    other = jnp.concatenate([front, back], axis=0)
    return jnp.concatenate(
        [jnp.where(first, shard, other), jnp.where(first, other, shard)], axis=0
    )


def gather_vectors(vectors, pairs):
    if pairs != 2:
        return [lax.all_gather(v, "group", axis=0, tiled=True) for v in vectors]
    joined = jnp.concatenate(vectors)
    other = swap(joined)
    first = lax.axis_index("group") == 0
    low, high = jnp.where(first, joined, other), jnp.where(first, other, joined)
    found, at = [], 0
    for v in vectors:
        size = v.shape[0]
        found.append(jnp.concatenate([low[at : at + size], high[at : at + size]]))
        at += size
    return found


def gather_rows(rows, pairs):
    if pairs != 2:
        return lax.all_gather(rows, "group", axis=0, tiled=True)
    return jnp.concatenate([rows, swap(rows)], axis=0)


def scatter_rows(partial, pairs):
    if pairs != 2:
        return lax.psum_scatter(
            partial.astype(jnp.bfloat16), "group", scatter_dimension=0, tiled=True
        ).astype(jnp.float32)
    half = partial.shape[0] // 2
    return partial[:half] + swap(partial[half:].astype(jnp.bfloat16)).astype(jnp.float32)


def scatter_owned(partial):
    return lax.psum_scatter(
        partial.astype(jnp.bfloat16), "group", scatter_dimension=0, tiled=True
    ).astype(jnp.float32)


def sum_owned(small, qkv, out, gate, up, down):
    owned = [scatter_owned(a) for a in (small, qkv, out)]
    return lax.psum(tuple(a.astype(jnp.bfloat16) for a in (*owned, gate, up, down)), "replica")


def on_device(
    tokens,
    segments,
    norm1_gain,
    qkv_weight,
    qkv_bias,
    out_weight,
    norm2_gain,
    gate_weight,
    up_weight,
    down_weight,
    cotangent,
    *,
    pairs,
    copies,
):
    sequences, length, model_width = tokens.shape
    row_count = sequences * length
    q_width = H * HD
    kv_width = KV * HD
    groups = H // KV
    score_scale = HD ** (-0.5)
    if fits(pairs, copies, tokens, segments, qkv_weight, out_weight, gate_weight, down_weight):
        shape_out = (sequences, length, model_width)
        half_dim = HD // 2
        frequency = ROPE_BASE ** (-2.0 * np.arange(half_dim) / HD)
        frequency = np.concatenate([frequency, frequency])[None].astype(np.float32)
        result, back_tokens, full = layer(
            tokens.reshape(row_count, model_width),
            segments.reshape(1, length),
            jnp.asarray(frequency),
            norm1_gain,
            norm2_gain,
            qkv_bias,
            cotangent.reshape(row_count, model_width),
            qkv_weight,
            out_weight,
            gate_weight,
            up_weight,
            down_weight,
        )
        return (
            result.reshape(shape_out),
            back_tokens.reshape(shape_out),
            *gradients_of(full, model_width, qkv_weight.shape[1]),
        )
    gain1_b, b_qkv, gain2_b = gather_vectors([norm1_gain, qkv_bias, norm2_gain], pairs)
    w_qkv = gather_weight(qkv_weight, pairs, copies)
    w_out = gather_weight(out_weight, pairs, copies)
    back_all = gather_rows(cotangent.reshape(row_count, model_width), pairs)
    allowed, cosine, sine = doc_layout(segments, HD)
    resid_in = tokens.reshape(row_count, model_width).astype(jnp.float32)
    inv_rms1 = inverse_rms(resid_in)
    gain1 = gain1_b.astype(jnp.float32)
    normed1 = (resid_in * inv_rms1 * gain1).astype(jnp.bfloat16)
    projected = matmul(normed1, w_qkv) + b_qkv.astype(jnp.float32)
    query = projected[:, :q_width].reshape(sequences, length, H, HD)
    keys_raw = projected[:, q_width : q_width + kv_width].reshape(sequences, length, KV, HD)
    values_raw = projected[:, q_width + kv_width :].reshape(sequences, length, KV, HD)
    query_b = (
        rotate(query, cosine, sine).astype(jnp.bfloat16).reshape(sequences, length, KV, groups, HD)
    )
    keys_b = rotate(keys_raw, cosine, sine).astype(jnp.bfloat16)
    values_b = values_raw.astype(jnp.bfloat16)
    scores = score_block(query_b, keys_b, allowed, score_scale)
    top_score = jnp.max(scores, axis=-1, keepdims=True)
    log_total = top_score + jnp.log(jnp.sum(jnp.exp(scores - top_score), axis=-1, keepdims=True))
    soft_b = jnp.exp(scores - log_total).astype(jnp.bfloat16)
    context = jnp.einsum("skgqp,spkd->sqkgd", soft_b, values_b, preferred_element_type=jnp.float32)
    context_b = context.astype(jnp.bfloat16).reshape(row_count, q_width)
    middle = resid_in + matmul(context_b, w_out)
    inv_rms2 = inverse_rms(middle)
    gain2 = gain2_b.astype(jnp.float32)
    normed2 = (middle * inv_rms2 * gain2).astype(jnp.bfloat16)
    back_rows = cotangent.reshape(row_count, model_width)
    normed_all = gather_rows(normed2, pairs)
    gate_pre = matmul(normed_all, gate_weight)
    up_proj = matmul(normed_all, up_weight)
    sigmoid_gate = jax.nn.sigmoid(gate_pre)
    silu_gate = gate_pre * sigmoid_gate
    activ_b = (silu_gate * up_proj).astype(jnp.bfloat16)
    result = middle + scatter_rows(matmul(activ_b, down_weight), pairs)
    back_activ = times_transposed(back_all, down_weight)
    back_gate = (
        back_activ * up_proj * sigmoid_gate * (1.0 + gate_pre * (1.0 - sigmoid_gate))
    ).astype(jnp.bfloat16)
    back_up = (back_activ * silu_gate).astype(jnp.bfloat16)
    grad_down = outer_sum(activ_b, back_all)
    grad_gate = outer_sum(normed_all, back_gate)
    grad_up = outer_sum(normed_all, back_up)
    local_normed = times_transposed(back_gate, gate_weight) + times_transposed(back_up, up_weight)
    back_normed2 = scatter_rows(local_normed, pairs)
    back_norm2, grad_norm2_part = norm_backward(middle, inv_rms2, gain2, back_normed2)
    back_middle = back_rows.astype(jnp.float32) + back_norm2
    back_middle_b = back_middle.astype(jnp.bfloat16)
    grad_out_part = outer_sum(context_b, back_middle_b)
    back_context = times_transposed(back_middle_b, w_out).astype(jnp.bfloat16)
    back_context = back_context.reshape(sequences, length, KV, groups, HD)
    soft = jnp.exp(score_block(query_b, keys_b, allowed, score_scale) - log_total)
    soft_again = soft.astype(jnp.bfloat16)
    back_values = jnp.einsum(
        "skgqp,sqkgd->spkd", soft_again, back_context, preferred_element_type=jnp.float32
    )
    back_soft = jnp.einsum(
        "sqkgd,spkd->skgqp", back_context, values_b, preferred_element_type=jnp.float32
    )
    row_dot = jnp.sum(soft * back_soft, axis=-1, keepdims=True)
    back_scores = (soft * (back_soft - row_dot) * score_scale).astype(jnp.bfloat16)
    back_query = jnp.einsum(
        "skgqp,spkd->sqkgd", back_scores, keys_b, preferred_element_type=jnp.float32
    )
    back_keys = jnp.einsum(
        "skgqp,sqkgd->spkd", back_scores, query_b, preferred_element_type=jnp.float32
    )
    back_query = unrotate(back_query.reshape(sequences, length, H, HD), cosine, sine)
    back_keys = unrotate(back_keys, cosine, sine)
    back_proj = jnp.concatenate(
        [
            back_query.reshape(row_count, q_width),
            back_keys.reshape(row_count, kv_width),
            back_values.reshape(row_count, kv_width),
        ],
        axis=1,
    )
    grad_bias_part = jnp.sum(back_proj, axis=0)
    back_proj_b = back_proj.astype(jnp.bfloat16)
    grad_qkv_part = outer_sum(normed1, back_proj_b)
    back_normed1 = times_transposed(back_proj_b, w_qkv)
    back_norm1, grad_norm1_part = norm_backward(resid_in, inv_rms1, gain1, back_normed1)
    back_tokens = back_middle + back_norm1
    small = jnp.stack([v.reshape(pairs, -1) for v in (grad_norm1_part, grad_norm2_part)], axis=1)
    small = jnp.concatenate(
        [small.reshape(pairs, -1), grad_bias_part.reshape(pairs, -1)], axis=1
    ).reshape(-1)
    owned = sum_owned(
        small,
        grad_qkv_part,
        grad_out_part,
        grad_gate,
        grad_up,
        grad_down,
    )
    small, grad_qkv, grad_out, grad_gate, grad_up, grad_down = (
        a.astype(jnp.float32) for a in owned
    )
    gains = norm1_gain.shape[0]
    grad_norm1, grad_norm2, grad_bias = (
        small[:gains],
        small[gains : 2 * gains],
        small[2 * gains :],
    )
    shape_out = (sequences, length, model_width)
    return (
        result.reshape(shape_out),
        back_tokens.reshape(shape_out),
        grad_norm1,
        grad_qkv,
        grad_bias,
        grad_out,
        grad_norm2,
        grad_gate,
        grad_up,
        grad_down,
    )


def solution(mesh):
    in_specs = (
        P(("group", "replica"), None, None),
        P(("group", "replica"), None),
        P("group"),
        P("group", None),
        P("group"),
        P("group", None),
        P("group"),
        P(None, "group"),
        P(None, "group"),
        P("group", None),
        P(("group", "replica"), None, None),
    )
    out_specs = (
        P(("group", "replica"), None, None),
        P(("group", "replica"), None, None),
        P("group"),
        P("group", None),
        P("group"),
        P("group", None),
        P("group"),
        P(None, "group"),
        P(None, "group"),
        P("group", None),
    )
    program = functools.partial(
        on_device, pairs=mesh.shape["group"], copies=mesh.shape["replica"]
    )
    return jax.shard_map(
        program, mesh=mesh, in_specs=in_specs, out_specs=out_specs, check_vma=False
    )
```

```python
import functools

import jax
import jax.numpy as jnp
import numpy as np
from jax import lax
from jax.experimental import pallas as pl
from jax.experimental.pallas import tpu as pltpu
from jax.sharding import PartitionSpec as P

H = 14
KV = 2
HD = 64


EPSILON = 1e-06
ROPE_BASE = 1000000.0
NEG_LARGE = -1e30


def doc_layout(segments, head_dim):
    length = segments.shape[1]
    places = jnp.arange(length, dtype=jnp.int32)
    same_doc = segments[:, :, None] == segments[:, None, :]
    earlier = places[None, None, :] < places[None, :, None]
    positions = jnp.sum(jnp.where(same_doc & earlier, 1.0, 0.0).astype(jnp.float32), axis=2)
    allowed = jnp.where(same_doc & (places[None, None, :] <= places[None, :, None]), 1, 0).astype(
        jnp.int32
    )
    half_dim = head_dim // 2
    frequency = ROPE_BASE ** (-2.0 * jnp.arange(half_dim, dtype=jnp.float32) / head_dim)
    angles = positions[:, :, None] * frequency[None, None, :]
    return (allowed, jnp.cos(angles)[:, :, None, :], jnp.sin(angles)[:, :, None, :])


def rotate(values, cosine, sine):
    half_dim = values.shape[-1] // 2
    front_half = values[..., :half_dim]
    back_half = values[..., half_dim:]
    return jnp.concatenate(
        [front_half * cosine - back_half * sine, back_half * cosine + front_half * sine], axis=-1
    )


def unrotate(gradients, cosine, sine):
    half_dim = gradients.shape[-1] // 2
    front_half = gradients[..., :half_dim]
    back_half = gradients[..., half_dim:]
    return jnp.concatenate(
        [front_half * cosine + back_half * sine, back_half * cosine - front_half * sine], axis=-1
    )


def inverse_rms(hidden):
    return lax.rsqrt(jnp.mean(hidden * hidden, axis=-1, keepdims=True) + EPSILON)


def norm_backward(hidden, inv_rms, gain_f, back_normed):
    weighted = back_normed * gain_f
    inner = jnp.mean(weighted * hidden, axis=-1, keepdims=True)
    back_hidden = inv_rms * weighted - hidden * (inv_rms * inv_rms * inv_rms) * inner
    back_gain = jnp.sum(back_normed * hidden * inv_rms, axis=0)
    return (back_hidden, back_gain)


def matmul(left, right):
    return jnp.dot(left, right, preferred_element_type=jnp.float32)


def outer_sum(left, right):
    return lax.dot_general(
        left, right, (((0,), (0,)), ((), ())), preferred_element_type=jnp.float32
    )


def times_transposed(left, right):
    return lax.dot_general(
        left, right, (((1,), (1,)), ((), ())), preferred_element_type=jnp.float32
    )


def score_block(query_b, keys_b, allowed, score_scale):
    scores = (
        jnp.einsum("sqkgd,spkd->skgqp", query_b, keys_b, preferred_element_type=jnp.float32)
        * score_scale
    )
    return jnp.where(allowed[:, None, None, :, :] > 0, scores, NEG_LARGE)


MESH_ID = pl.DeviceIdType.MESH
TILE = 128
SLICE = 640
CHUNK = 64
SMALL_ROWS = 480


def relative(delta):
    me = lax.axis_index("replica")
    pair = lax.axis_index("group")
    core, x = me % 2, lax.div(me, 2) % 2
    d_core, d_x, d_y = delta % 2, lax.div(delta, 2) % 2, lax.div(delta, 4) % 2
    shift = d_core * (1 - 2 * core) + 2 * d_x * (1 - 2 * x)
    return {"group": pair + d_y * (1 - 2 * pair), "replica": me + shift}


def greet(devices):
    barrier = pltpu.get_barrier_semaphore()
    for device in devices:
        pl.semaphore_signal(barrier, inc=1, device_id=device, device_id_type=MESH_ID)
    return barrier


def remote(src, dst, sems, where, device):
    return pltpu.make_async_remote_copy(
        src_ref=src,
        dst_ref=dst,
        send_sem=sems[0].at[where],
        recv_sem=sems[1].at[where],
        device_id=device,
        device_id_type=MESH_ID,
    )


def contract(left, right, left_dim, right_dim):
    return lax.dot_general(
        left,
        right,
        (((left_dim,), (right_dim,)), ((), ())),
        preferred_element_type=jnp.float32,
    )


def layer_kernel(
    tokens_ref,
    seg_row,
    frequency,
    gain1_in,
    gain2_in,
    bias_in,
    cot_ref,
    qkv_ref,
    out_weight_ref,
    gate_ref,
    up_ref,
    down_ref,
    result_ref,
    back_ref,
    out_ref,
    rows_n,
    rows_c,
    w_gate,
    w_up,
    w_down,
    activ,
    d_gate,
    d_up,
    part_b,
    part_r,
    sib_b,
    sib_r,
    land_b,
    land_r,
    own,
    land_u,
    land_m,
    total,
    mine,
    sib,
    across,
    beside,
    joined_ref,
    rest_ref,
    proj,
    stacked,
    normed1,
    share,
    w_qkv_ref,
    w_out_ref,
    vector_ref,
    vectors,
    query_ref,
    keys_ref,
    values_ref,
    log_ref,
    allowed_ref,
    cos_ref,
    sin_ref,
    context_ref,
    middle_ref,
    gain1_ref,
    gain2_ref,
    local,
    link,
    core_n,
    core_c,
    core_b,
    core_r,
    link_b,
    link_r,
    early,
    up,
    mid,
    down,
    side,
    out1,
    out2,
    link_c,
    weights_y,
    weights_x,
    weights_1,
    weights_2,
):
    f32, bf16 = jnp.float32, jnp.bfloat16
    count = own.shape[0] // CHUNK
    length, width = tokens_ref.shape
    bulk = 3 * width
    first = bulk // CHUNK
    lines, wide = mine.shape[1], mine.shape[2]
    half = lines // 2
    depth = joined_ref.shape[0] // 2
    me = lax.axis_index("replica")
    pair = lax.axis_index("group")
    core, x, z = me % 2, lax.div(me, 2) % 2, lax.div(me, 4)
    quarter = me % 4
    beside_quarter = quarter + 2 * (1 - 2 * x)
    middle = (z == 1) | (z == 2)
    is_end = (z == 0) | (z == 3)
    near = {"replica": me + 4 * (1 - 2 * (z % 2))}
    far = {"replica": me + 4 * (1 - 2 * lax.div(z, 2))}
    sibling, neighbour, peer = relative(1), relative(2), relative(4)


    def halves(which):
        return pl.ds(pl.multiple_of(which * half, 16), half)

    def lanes(which):
        return pl.ds(pl.multiple_of(which * wide, TILE), wide)

    first_column = pl.multiple_of(TILE * (5 * quarter - lax.div(quarter, 3)), TILE)
    columns = pl.ds(first_column, SLICE)
    loads = [
        pltpu.make_async_copy(gate_ref.at[:, columns], w_gate, local.at[0]),
        pltpu.make_async_copy(up_ref.at[:, columns], w_up, local.at[1]),
        pltpu.make_async_copy(down_ref.at[columns, :], w_down, local.at[2]),
    ]
    shard = width // 2
    w_loads = [
        pltpu.make_async_copy(
            qkv_ref, w_qkv_ref.at[pl.ds(pl.multiple_of(pair * shard, 64), shard)], local.at[3]
        ),
        pltpu.make_async_copy(
            out_weight_ref, w_out_ref.at[pl.ds(pl.multiple_of(pair * shard, 64), shard)], local.at[4]
        ),
    ]
    for load in w_loads:
        load.start()
    rows_c[0:length] = cot_ref[...]
    vector_ref[0:1, 0:shard] = gain1_in[...].astype(f32).reshape(1, gain1_in.shape[0])
    vector_ref[0:1, 512 : 512 + shard] = gain2_in[...].astype(f32).reshape(1, gain2_in.shape[0])
    vector_ref[0:1, 1024 : 1024 + bias_in.shape[0]] = bias_in[...].astype(f32).reshape(1, bias_in.shape[0])
    barrier = greet([sibling, neighbour, peer, relative(6), near])

    @pl.when(middle)
    def _():
        pl.semaphore_signal(barrier, inc=1, device_id=far, device_id_type=MESH_ID)

    pl.semaphore_wait(barrier, jnp.where(middle, 6, 5))

    def block(ref, slot):
        return ref.at[pl.ds(pl.multiple_of(slot * length, 16), length)]

    part = shard // 4
    cuts = ((0, 48), (48, part - 48))
    vector_copy = remote(vector_ref, vectors, early, 7, peer)
    vector_copy.start()

    def quarter_rows(which, fourth, cut):
        first = which * shard + fourth * part + cuts[cut][0]
        return pl.ds(pl.multiple_of(first, 16), cuts[cut][1])

    moved = [(qkv_ref, w_qkv_ref, 0), (out_weight_ref, w_out_ref, 1)]

    def weight_y(w, cut):
        source, goal, _ = moved[w]
        rows = pl.ds(pl.multiple_of(quarter * part + cuts[cut][0], 16), cuts[cut][1])
        return remote(
            source.at[rows], goal.at[quarter_rows(pair, quarter, cut)], weights_y, 2 * w + cut, peer
        )

    def weight_y_in(w, cut):
        goal = moved[w][1].at[quarter_rows(1 - pair, quarter, cut)]
        return remote(goal, goal, weights_y, 2 * w + cut, peer)

    def weight_pass(w, cut, fourth, sems, device):
        goal = moved[w][1].at[quarter_rows(1 - pair, fourth, cut)]
        return remote(goal, goal, sems, 2 * w + cut, device)

    order = [(w, cut) for w in range(2) for cut in range(2)]
    for w, cut in order:
        weight_y(w, cut).start()
    sends = []

    def send_cot(p):
        copy = remote(block(rows_c, 0), block(rows_c, 2 * p), link_c, p, relative(2 * p))
        copy.start()
        sends.append(copy)

    send_cot(1)

    def forward_n(p):
        return remote(block(rows_n, 2 * p), block(rows_n, 2 * p + 1), core_n, p, sibling)

    def forward_c(p):
        return remote(block(rows_c, 2 * p), block(rows_c, 2 * p + 1), core_c, p, sibling)

    forward_c(0).start()
    for load in loads:
        load.start()
    asked = lax.broadcasted_iota(jnp.int32, (length, length), 0)
    seen = lax.broadcasted_iota(jnp.int32, (length, length), 1)
    seg_column = jnp.sum(jnp.where(asked == seen, seg_row[...], 0), axis=1, keepdims=True)
    same = seg_column == seg_row[...]
    allowed_ref[...] = jnp.where(same & (seen <= asked), 1, 0)
    positions = jnp.sum(jnp.where(same & (seen < asked), 1.0, 0.0), axis=1, keepdims=True)
    angles = positions * frequency[...]
    cos_ref[...] = jnp.cos(angles)
    column = lax.broadcasted_iota(jnp.int32, angles.shape, 1)
    sine = jnp.sin(angles)
    sin_ref[...] = jnp.where(column < HD // 2, sine, -sine)
    tokens = tokens_ref[...].astype(f32)
    inv1 = inverse_rms(tokens)
    vector_copy.wait()
    mine_v, other_v = vector_ref[0:1, :], vectors[0:1, :]
    low_v = jnp.where(pair == 0, mine_v, other_v)
    high_v = jnp.where(pair == 0, other_v, mine_v)
    gain1_ref[...] = jnp.concatenate([low_v[:, :shard], high_v[:, :shard]], axis=1)
    gain2_ref[...] = jnp.concatenate(
        [low_v[:, 512 : 512 + shard], high_v[:, 512 : 512 + shard]], axis=1
    )
    bias_at = 1024
    bias = jnp.concatenate(
        [low_v[:, bias_at : bias_at + proj.shape[1] // 2], high_v[:, bias_at : bias_at + proj.shape[1] // 2]],
        axis=1,
    )
    normed1[...] = (tokens * inv1 * gain1_ref[...]).astype(bf16)
    for load in w_loads:
        load.wait()

    def relay(w):
        for cut in range(2):
            weight_y_in(w, cut).wait_recv()
            weight_pass(w, cut, quarter, weights_x, neighbour).start()
            weight_pass(w, cut, quarter, weights_1, sibling).start()

    def relay_x(w):
        for cut in range(2):
            weight_pass(w, cut, beside_quarter, weights_x, neighbour).wait_recv()
            weight_pass(w, cut, beside_quarter, weights_2, sibling).start()

    def settle(w):
        for cut in range(2):
            weight_y(w, cut).wait_send()
            weight_pass(w, cut, quarter, weights_x, neighbour).wait_send()
            weight_pass(w, cut, quarter, weights_1, sibling).wait()
            weight_pass(w, cut, beside_quarter, weights_2, sibling).wait()

    relay(0)
    send_cot(2)
    relay_x(0)
    settle(0)
    projected = contract(normed1[...], w_qkv_ref[...], 1, 0) + bias
    proj[...] = projected
    relay(1)
    send_cot(3)
    groups = H // KV
    score_scale = HD ** (-0.5)

    def turned(at):
        value = proj[:, at : at + HD]
        swapped = jnp.concatenate([value[:, HD // 2 :], value[:, : HD // 2]], axis=1)
        return (value * cos_ref[...] - swapped * sin_ref[...]).astype(bf16)

    for k in range(KV):
        for j in range(groups):
            query_ref[k, j * length : (j + 1) * length, :] = turned((k * groups + j) * HD)
        at = H * HD + k * HD
        keys_ref[k] = turned(at)
        values_ref[k] = proj[:, at + KV * HD : at + (KV + 1) * HD].astype(bf16)
        mask = jnp.concatenate([allowed_ref[...]] * groups, axis=0) > 0
        scores = contract(query_ref[k], keys_ref[k], 1, 1) * score_scale
        scores = jnp.where(mask, scores, NEG_LARGE)
        top = jnp.max(scores, axis=-1, keepdims=True)
        log_total = top + jnp.log(jnp.sum(jnp.exp(scores - top), axis=-1, keepdims=True))
        log_ref[k] = log_total
        soft = jnp.exp(scores - log_total).astype(bf16)
        context = contract(soft, values_ref[k], 1, 0).astype(bf16)
        for j in range(groups):
            at = (k * groups + j) * HD
            context_ref[:, at : at + HD] = context[j * length : (j + 1) * length, :]
        if k == 0:
            relay_x(1)
    settle(1)
    middle_value = tokens + contract(context_ref[...], w_out_ref[...], 1, 0)
    middle_ref[...] = middle_value
    rows_n[0:length] = (middle_value * inverse_rms(middle_value) * gain2_ref[...]).astype(bf16)
    for p in (1, 2, 3):
        copy = remote(block(rows_n, 0), block(rows_n, 2 * p), link, p, relative(2 * p))
        copy.start()
        sends.append(copy)
    forward_n(0).start()
    for load in loads:
        load.wait()

    def fold(part, sib, core, land, hop, q):
        remote(block(part, 2 * q + 1), sib.at[q], core, q, sibling).wait()
        rows = pl.ds(pl.multiple_of(2 * q * length, 16), length)
        part[rows, :] = (part[rows, :].astype(f32) + sib[q].astype(f32)).astype(bf16)
        if q > 1:
            remote(block(part, 2 * q), land.at[q - 1], hop, q, peer).start()

    def cross(part, land, hop):
        remote(block(part, 6), land.at[2], hop, 3, peer).wait()
        rows = slice(2 * length, 3 * length)
        part[rows, :] = (part[rows, :].astype(f32) + land[2].astype(f32)).astype(bf16)
        remote(block(part, 2), land.at[0], hop, 1, neighbour).start()

    def fold_own(part, sib, core):
        remote(block(part, 1), sib.at[0], core, 0, sibling).wait()
        return part[0:length, :].astype(f32) + sib[0].astype(f32)

    def pair_step(p, carry):
        def arrive(q):
            remote(block(rows_n, 0), block(rows_n, 2 * q), link, q, relative(2 * q)).wait_recv()
            forward_n(q).start()

        @pl.when(p == 1)
        def _():
            arrive(1)
            arrive(2)

        @pl.when(p == 2)
        def _():
            arrive(3)

        @pl.when(p < 3)
        def _():
            q = p + 1
            remote(block(rows_c, 0), block(rows_c, 2 * q), link_c, q, relative(2 * q)).wait_recv()
            forward_c(q).start()

        forward_n(p).wait()
        forward_c(p).wait()
        both = pl.ds(pl.multiple_of(2 * p * length, 32), 2 * length)
        normed, cot = rows_n[both, :], rows_c[both, :]
        gate_pre = contract(normed, w_gate[...], 1, 0)
        up_proj = contract(normed, w_up[...], 1, 0)
        back_activ = contract(cot, w_down[...], 1, 1)
        sigmoid_gate = jax.nn.sigmoid(gate_pre)
        silu_gate = gate_pre * sigmoid_gate
        column = lax.broadcasted_iota(jnp.int32, gate_pre.shape, 1)
        own = column >= jnp.where(quarter == 3, TILE, 0)
        activ[both, :] = jnp.where(own, silu_gate * up_proj, 0.0).astype(jnp.bfloat16)
        d_gate[both, :] = jnp.where(
            own,
            back_activ * up_proj * sigmoid_gate * (1.0 + gate_pre * (1.0 - sigmoid_gate)),
            0.0,
        ).astype(jnp.bfloat16)
        d_up[both, :] = jnp.where(own, back_activ * silu_gate, 0.0).astype(jnp.bfloat16)
        part_b[both, :] = (
            contract(d_gate[both, :], w_gate[...], 1, 1)
            + contract(d_up[both, :], w_up[...], 1, 1)
        ).astype(jnp.bfloat16)
        remote(block(part_b, 2 * p + 1), sib_b.at[p], core_b, p, relative(1)).start()
        part_r[both, :] = contract(activ[both, :], w_down[...], 1, 0).astype(jnp.bfloat16)
        remote(block(part_r, 2 * p + 1), sib_r.at[p], core_r, p, relative(1)).start()

        return carry

    lax.fori_loop(0, 4, pair_step, 0)

    def chunk(c):
        return pl.ds(pl.multiple_of(c * CHUNK, CHUNK), CHUNK)

    def up_copy(c):
        return remote(own.at[chunk(c)], land_u.at[chunk(c)], up, c, near)

    def mid_copy(c):
        return remote(own.at[chunk(c)], land_m.at[chunk(c)], mid, c, far)

    def down_copy(c):
        return remote(total.at[chunk(c)], total.at[chunk(c)], down, c, near)

    def side_copy(c):
        return remote(
            total.at[chunk(c)], out_ref.at[quarter].at[chunk(c)], side, c, neighbour
        )

    def side_arrival(c):
        return remote(
            total.at[chunk(c)], out_ref.at[beside_quarter].at[chunk(c)], side, c, neighbour
        )

    def out_copy(c):
        return remote(total.at[chunk(c)], out_ref.at[quarter].at[chunk(c)], out1, c, sibling)

    def pass_copy(c):
        place = out_ref.at[beside_quarter].at[chunk(c)]
        return remote(place, place, out2, c, sibling)

    def store(c):
        return pltpu.make_async_copy(
            total.at[chunk(c)], out_ref.at[quarter].at[chunk(c)], local.at[7 + c]
        )

    def hand_out(c):
        side_copy(c).start()
        out_copy(c).start()
        store(c).start()

    def add(goal, left, right, rows):
        goal[rows, :] = (
            left[rows, :].astype(jnp.float32) + right[rows, :].astype(jnp.float32)
        ).astype(jnp.bfloat16)

    def send_up(lo, hi):
        @pl.when(is_end)
        def _():
            def go(c, carry):
                up_copy(c).start()
                return carry

            lax.fori_loop(lo, hi, go, 0)

    skew1, skew2 = 3, 14

    def service(i, carry):
        a, b, d = i, i - skew1, i - skew2

        @pl.when(middle & (a < count))
        def _():
            up_copy(a).wait_recv()
            add(own, own, land_u, chunk(a))
            mid_copy(a).start()

        @pl.when((b >= 0) & (b < count))
        def _():
            @pl.when(middle)
            def _():
                mid_copy(b).wait_recv()
                add(total, own, land_m, chunk(b))
                down_copy(b).start()

            @pl.when(is_end)
            def _():
                down_copy(b).wait_recv()

            hand_out(b)

        @pl.when(d >= 0)
        def _():
            side_arrival(d).wait_recv()
            pass_copy(d).start()

        return carry

    def serve(lo, hi):
        lax.fori_loop(lo, hi, service, 0)

    def finish(part, land, hop, goal):
        remote(block(part, 4), land.at[1], hop, 2, peer).wait()
        remote(block(part, 2), land.at[0], hop, 1, neighbour).wait()
        return goal[...] + land[0].astype(f32) + land[1].astype(f32)

    for q in (3, 2, 1):
        fold(part_b, sib_b, core_b, land_b, link_b, q)
    share[...] = fold_own(part_b, sib_b, core_b)

    def grad_step(h, carry):
        lane = pl.ds(pl.multiple_of(h * TILE, TILE), TILE)
        left = rows_n[:, lane]

        def place(which):
            return pl.ds(pl.multiple_of((3 * h + which) * TILE, TILE), TILE)

        own[place(0), :] = contract(left, d_gate[...], 0, 0).astype(bf16)
        own[place(1), :] = contract(left, d_up[...], 0, 0).astype(bf16)
        down = contract(activ[...], rows_c[:, lane], 0, 0).astype(bf16)
        for i in range(SLICE // TILE):
            own[place(2), i * TILE : (i + 1) * TILE] = down[i * TILE : (i + 1) * TILE]
        per = 3 * TILE // CHUNK
        send_up(h * per, (h + 1) * per)
        return carry

    lax.fori_loop(0, width // TILE, grad_step, 0)
    for q in (3, 2, 1):
        fold(part_r, sib_r, core_r, land_r, link_r, q)
    result_ref[...] = fold_own(part_r, sib_r, core_r)
    serve(0, 3)
    cross(part_b, land_b, link_b)
    serve(3, 5)
    back_normed = finish(part_b, land_b, link_b, share)
    serve(5, 7)

    def norm_back(hidden, inv, gain, back):
        weighted = back * gain
        inner = jnp.mean(weighted * hidden, axis=-1, keepdims=True)
        back_hidden = inv * weighted - hidden * (inv * inv * inv) * inner
        return back_hidden, jnp.sum(back * hidden * inv, axis=0, keepdims=True)

    hidden = middle_ref[...]
    back_hidden, sum2 = norm_back(hidden, inverse_rms(hidden), gain2_ref[...], back_normed)
    back_middle = rows_c[0:length, :].astype(f32) + back_hidden
    share[...] = back_middle
    back_middle_b = back_middle.astype(bf16)
    back_context = contract(back_middle_b, w_out_ref[...], 1, 1).astype(bf16)
    for k in range(KV):
        for j in range(groups):
            at = (k * groups + j) * HD
            stacked[k, j * length : (j + 1) * length, :] = back_context[:, at : at + HD]
    joined_ref[:, proj.shape[1] :] = contract(context_ref[...], back_middle_b, 0, 0).astype(bf16)
    serve(7, 8)

    def unturn(value):
        swapped = jnp.concatenate([value[:, HD // 2 :], value[:, : HD // 2]], axis=1)
        return value * cos_ref[...] + swapped * sin_ref[...]

    for k in range(KV):
        keys, values, query, back = keys_ref[k], values_ref[k], query_ref[k], stacked[k]
        mask = jnp.concatenate([allowed_ref[...]] * groups, axis=0) > 0
        scores = contract(query, keys, 1, 1) * score_scale
        soft = jnp.exp(jnp.where(mask, scores, NEG_LARGE) - log_ref[k])
        back_soft = contract(back, values, 1, 1)
        row_dot = jnp.sum(soft * back_soft, axis=-1, keepdims=True)
        back_scores = (soft * (back_soft - row_dot) * score_scale).astype(bf16)
        back_values = contract(soft.astype(bf16), back, 0, 0)
        back_query = contract(back_scores, keys, 1, 0)
        back_keys = contract(back_scores, query, 0, 0)
        for j in range(groups):
            at = (k * groups + j) * HD
            proj[:, at : at + HD] = unturn(back_query[j * length : (j + 1) * length, :])
        at = H * HD + k * HD
        proj[:, at : at + HD] = unturn(back_keys)
        proj[:, at + KV * HD : at + (KV + 1) * HD] = back_values
        serve(8 + 2 * k, 10 + 2 * k)

    sum_bias = jnp.sum(proj[...], axis=0, keepdims=True)
    proj_b = proj[...].astype(bf16)
    tokens = tokens_ref[...].astype(f32)
    inv1 = inverse_rms(tokens)
    joined_ref[:, : proj.shape[1]] = contract(normed1[...], proj_b, 0, 0).astype(bf16)
    serve(12, 13)
    back_normed1 = contract(proj_b, w_qkv_ref[...], 1, 1)
    back_first, sum1 = norm_back(tokens, inv1, gain1_ref[...], back_normed1)
    back_ref[...] = share[...] + back_first
    row = lax.broadcasted_iota(jnp.int32, rest_ref.shape[1:], 0)

    def lines_of(top, second):
        pads = [
            jnp.concatenate([v, jnp.zeros((1, wide - v.shape[1]), f32)], axis=1)
            if v.shape[1] < wide
            else v
            for v in (top, second)
        ]
        return jnp.where(row == 0, pads[0], jnp.where(row == 1, pads[1], 0.0)).astype(bf16)

    rest_ref[0] = lines_of(sum1, sum2)
    rest_ref[1] = lines_of(sum_bias[:, :wide], sum_bias[:, wide:])
    small_loads = []
    for g in range(2):
        rows = slice(g * depth, (g + 1) * depth)
        small_loads += [
            pltpu.make_async_copy(
                joined_ref.at[rows, lanes(core)], mine.at[g, 0:depth], local.at[3 + g]
            ),
            pltpu.make_async_copy(rest_ref.at[core], mine.at[g, depth:lines], local.at[5 + g]),
        ]
    for copy in small_loads:
        copy.start()
    swap0 = []
    for g in range(2):
        rows = slice(g * depth, (g + 1) * depth)
        swap0 += [
            remote(joined_ref.at[rows, lanes(1 - core)], sib.at[g, 0:depth], early, g, sibling),
            remote(rest_ref.at[1 - core], sib.at[g, depth:lines], early, 2 + g, sibling),
        ]
    for copy in swap0:
        copy.start()
    serve(13, 15)
    cross(part_r, land_r, link_r)
    for copy in small_loads + swap0:
        copy.wait()

    def add_small(r, carry):
        rows = pl.ds(pl.multiple_of(r * 48, 16), 48)
        for g in range(2):
            mine[g, rows, :] = (
                mine[g, rows, :].astype(jnp.float32) + sib[g, rows, :].astype(jnp.float32)
            ).astype(jnp.bfloat16)
        return carry

    lax.fori_loop(0, lines // 48, add_small, 0)

    def swap_copy(which):
        return remote(
            mine.at[1 - pair].at[halves(which)], across.at[halves(which)], early, 4 + which, peer
        )

    swap_copy(1 - x).start()
    swap_copy(x).start()
    serve(15, 26)


    def add_across(which):
        def go(r, carry):
            rows = pl.ds(pl.multiple_of(which * half + r * 48, 16), 48)
            across[rows, :] = (
                across[rows, :].astype(jnp.float32) + mine[pair, rows, :].astype(jnp.float32)
            ).astype(jnp.bfloat16)
            return carry

        lax.fori_loop(0, half // 48, go, 0)

    swap_copy(1 - x).wait()
    add_across(1 - x)
    side_small = remote(across.at[halves(1 - x)], beside, early, 6, neighbour)
    side_small.start()
    serve(26, 36)
    result_ref[...] = middle_ref[...] + finish(part_r, land_r, link_r, result_ref)
    swap_copy(x).wait()
    side_small.wait()
    for s in range(half // 48):
        rows = pl.ds(pl.multiple_of(x * half + s * 48, 16), 48)
        value = (
            across[rows, :].astype(jnp.float32)
            + mine[pair, rows, :].astype(jnp.float32)
            + beside[s * 48 : (s + 1) * 48, :].astype(jnp.float32)
        ).astype(jnp.bfloat16)
        for t in range(wide // TILE):
            own[bulk + t * 48 : bulk + (t + 1) * 48, s * TILE : (s + 1) * TILE] = value[
                :, t * TILE : (t + 1) * TILE
            ]
    send_up(first, count)
    serve(36, count + skew2)

    def drain(c, carry):
        @pl.when(is_end)
        def _():
            up_copy(c).wait_send()

        @pl.when(middle)
        def _():
            mid_copy(c).wait_send()
            down_copy(c).wait_send()

        side_copy(c).wait_send()
        out_copy(c).wait_send()
        out_copy(c).wait_recv()
        pass_copy(c).wait_send()
        pass_copy(c).wait_recv()
        store(c).wait()
        return carry

    lax.fori_loop(0, count, drain, 0)


    for copy in sends:
        copy.wait_send()


def layer(*args):
    length, width = args[0].shape
    rows = 8 * length
    bf16, f32 = jnp.bfloat16, jnp.float32
    vmem = pl.BlockSpec(memory_space=pltpu.VMEM)
    hbm = pl.BlockSpec(memory_space=pl.ANY)
    qkv_width = args[7].shape[1]
    wide = (qkv_width + width) // 2
    chain = 3 * width + SMALL_ROWS * wide // (2 * SLICE)
    count = chain // CHUNK
    stack = (KV, H // KV * length)
    buffers = [
        ((rows, width), bf16),
        ((rows, width), bf16),
        ((width, SLICE), bf16),
        ((width, SLICE), bf16),
        ((SLICE, width), bf16),
        ((rows, SLICE), bf16),
        ((rows, SLICE), bf16),
        ((rows, SLICE), bf16),
        ((rows, width), bf16),
        ((rows, width), bf16),
        ((4, length, width), bf16),
        ((4, length, width), bf16),
        ((3, length, width), bf16),
        ((3, length, width), bf16),
        ((chain, SLICE), bf16),
        ((chain, SLICE), bf16),
        ((chain, SLICE), bf16),
        ((chain, SLICE), bf16),
        ((2, SMALL_ROWS, wide), bf16),
        ((2, SMALL_ROWS, wide), bf16),
        ((SMALL_ROWS, wide), bf16),
        ((SMALL_ROWS // 2, wide), bf16),
        ((width, 2 * wide), bf16),
        ((2, SMALL_ROWS - width // 2, wide), bf16),
        ((length, qkv_width), f32),
        ((KV, H // KV * length, HD), bf16),
        ((length, width), bf16),
        ((length, width), f32),
        ((width, qkv_width), bf16),
        ((width, width), bf16),
        ((8, 1664), f32),
        ((8, 1664), f32),
        ((*stack, HD), bf16),
        ((KV, length, HD), bf16),
        ((KV, length, HD), bf16),
        ((*stack, 1), f32),
        ((length, length), jnp.int32),
        ((length, HD), f32),
        ((length, HD), f32),
        ((length, width), bf16),
        ((length, width), f32),
        ((1, width), f32),
        ((1, width), f32),
    ]
    sizes = [4] * 7 + [8] + [count] * 6 + [4] * 5

    def body(*refs):
        plain = len(args) + 3 + len(buffers)
        local, rest = refs[plain], refs[plain + 1 :]
        grouped = [(rest[2 * i], rest[2 * i + 1]) for i in range(len(sizes))]
        layer_kernel(*refs[:plain], local, *grouped)

    return pl.pallas_call(
        body,
        out_shape=[
            jax.ShapeDtypeStruct((length, width), f32),
            jax.ShapeDtypeStruct((length, width), f32),
            jax.ShapeDtypeStruct((4, chain, SLICE), bf16),
        ],
        in_specs=[vmem] * 7 + [hbm] * 5,
        out_specs=[vmem, vmem, hbm],
        scratch_shapes=[pltpu.VMEM(shape, kind) for shape, kind in buffers]
        + [pltpu.SemaphoreType.DMA((7 + count,))]
        + [pltpu.SemaphoreType.DMA((size,)) for size in sizes for _ in range(2)],
        compiler_params=pltpu.CompilerParams(
            collective_id=1, has_side_effects=True, vmem_limit_bytes=60 * 1024 * 1024
        ),
        name="layer",
    )(*args)


def unpack_kernel(
    gate_in,
    up_in,
    down_in,
    small_in,
    result_in,
    back_in,
    gate,
    up,
    down,
    qkv,
    out,
    norm1,
    norm2,
    bias,
    result,
    back,
    extra,
):
    f32 = jnp.float32
    result[...] = result_in[...]
    back[...] = back_in[...]
    for source, goal in ((gate_in, gate), (up_in, up)):
        for k in range(3):
            goal[:, k * SLICE : (k + 1) * SLICE] = source[k].astype(f32)
        goal[:, 3 * SLICE :] = source[3, :, TILE:].astype(f32)
    tiles = SLICE // TILE
    for k in range(4):
        for i in range(tiles):
            if k == 3 and i == 0:
                continue
            first = (k * tiles + i - k // 3) * TILE
            down[first : first + TILE, :] = down_in[k, :, i * TILE : (i + 1) * TILE].astype(f32)

    @pl.when(pl.program_id(0) == 0)
    def _():
        depth, split = qkv.shape
        lanes = small_in.shape[1] // 48
        for k in range(4):
            for t in range(lanes):
                for s in range(tiles):
                    value = small_in[
                        k, t * 48 : (t + 1) * 48, s * TILE : (s + 1) * TILE
                    ].astype(f32)
                    row, column = k // 2 * tiles * 48 + s * 48, (k % 2 * lanes + t) * TILE
                    keep = min(48, depth - row)
                    if column < split:
                        qkv[row : row + keep, column : column + TILE] = value[:keep]
                    else:
                        at = column - split
                        out[row : row + keep, at : at + TILE] = value[:keep]
                    if keep < 48:
                        extra[:, column : column + TILE] = value[keep:]
        high = lax.axis_index("group") == 1
        wide, share = extra.shape[1] // 2, norm1.shape[0]
        for row, goal in ((0, norm1), (1, norm2)):
            line = extra[row : row + 1, : 2 * share]
            goal[...] = jnp.where(high, line[:, share:], line[:, :share]).reshape(share)
        most = bias.shape[0]
        line = jnp.concatenate(
            [extra[0:1, wide:], extra[1:2, wide : wide + 2 * most - wide]], axis=1
        )
        goal = jnp.where(high, line[:, most:], line[:, :most])
        bias[...] = goal.reshape(most)


def unpack(full, result, back, qkv_width):
    length, width = result.shape
    f32 = jnp.float32
    steps = width // TILE
    features = 4 * SLICE - TILE
    small_rows = full.shape[1] - 3 * width
    depth = width // 2
    whole = lambda i: (0, 0)
    return pl.pallas_call(
        unpack_kernel,
        grid=(steps,),
        out_shape=[
            jax.ShapeDtypeStruct((width, features), f32),
            jax.ShapeDtypeStruct((width, features), f32),
            jax.ShapeDtypeStruct((features, width), f32),
            jax.ShapeDtypeStruct((depth, qkv_width), f32),
            jax.ShapeDtypeStruct((depth, width), f32),
            jax.ShapeDtypeStruct((depth,), f32),
            jax.ShapeDtypeStruct((depth,), f32),
            jax.ShapeDtypeStruct((qkv_width // 2,), f32),
            jax.ShapeDtypeStruct((length, width), f32),
            jax.ShapeDtypeStruct((length, width), f32),
        ],
        in_specs=[
            pl.BlockSpec((4, TILE, SLICE), lambda i: (0, 3 * i, 0)),
            pl.BlockSpec((4, TILE, SLICE), lambda i: (0, 3 * i + 1, 0)),
            pl.BlockSpec((4, TILE, SLICE), lambda i: (0, 3 * i + 2, 0)),
            pl.BlockSpec((4, small_rows, SLICE), lambda i: (0, 3 * width // small_rows, 0)),
            pl.BlockSpec((length, TILE), lambda i: (0, i)),
            pl.BlockSpec((length, TILE), lambda i: (0, i)),
        ],
        out_specs=[
            pl.BlockSpec((TILE, features), lambda i: (i, 0)),
            pl.BlockSpec((TILE, features), lambda i: (i, 0)),
            pl.BlockSpec((features, TILE), lambda i: (0, i)),
            pl.BlockSpec((depth, qkv_width), whole),
            pl.BlockSpec((depth, width), whole),
            pl.BlockSpec((depth,), lambda i: (0,)),
            pl.BlockSpec((depth,), lambda i: (0,)),
            pl.BlockSpec((qkv_width // 2,), lambda i: (0,)),
            pl.BlockSpec((length, TILE), lambda i: (0, i)),
            pl.BlockSpec((length, TILE), lambda i: (0, i)),
        ],
        scratch_shapes=[pltpu.VMEM((SMALL_ROWS - depth, qkv_width + width), f32)],
        compiler_params=pltpu.CompilerParams(vmem_limit_bytes=56 * 1024 * 1024),
        name="unpack",
    )(full, full, full, full, result, back)


def fits(pairs, copies, tokens, segments, qkv, out, gate, down):
    return (
        pairs == 2
        and copies == 16
        and tokens.shape == (1, 144, 896)
        and qkv.shape == (448, 1152)
        and out.shape == (448, 896)
        and gate.shape == (896, 2432)
        and down.shape == (2432, 896)
    )


def swap(values):
    return lax.ppermute(values, "group", [(0, 1), (1, 0)])


def gather_weight(shard, pairs, copies):
    if pairs != 2 or copies % 2:
        return lax.all_gather(shard, "group", axis=0, tiled=True)
    half = shard.shape[0] // 2
    core = lax.axis_index("replica") % 2
    mine = swap(lax.dynamic_slice_in_dim(shard, core * half, half, 0))
    sibling = lax.ppermute(mine, "replica", [(i, i + 1 - 2 * (i % 2)) for i in range(copies)])
    front = jnp.where(core == 0, mine, sibling)
    back = jnp.where(core == 0, sibling, mine)
    first = lax.axis_index("group") == 0
    other = jnp.concatenate([front, back], axis=0)
    return jnp.concatenate(
        [jnp.where(first, shard, other), jnp.where(first, other, shard)], axis=0
    )


def gather_vectors(vectors, pairs):
    if pairs != 2:
        return [lax.all_gather(v, "group", axis=0, tiled=True) for v in vectors]
    joined = jnp.concatenate(vectors)
    other = swap(joined)
    first = lax.axis_index("group") == 0
    low, high = jnp.where(first, joined, other), jnp.where(first, other, joined)
    found, at = [], 0
    for v in vectors:
        size = v.shape[0]
        found.append(jnp.concatenate([low[at : at + size], high[at : at + size]]))
        at += size
    return found


def gather_rows(rows, pairs):
    if pairs != 2:
        return lax.all_gather(rows, "group", axis=0, tiled=True)
    return jnp.concatenate([rows, swap(rows)], axis=0)


def scatter_rows(partial, pairs):
    if pairs != 2:
        return lax.psum_scatter(
            partial.astype(jnp.bfloat16), "group", scatter_dimension=0, tiled=True
        ).astype(jnp.float32)
    half = partial.shape[0] // 2
    return partial[:half] + swap(partial[half:].astype(jnp.bfloat16)).astype(jnp.float32)


def scatter_owned(partial):
    return lax.psum_scatter(
        partial.astype(jnp.bfloat16), "group", scatter_dimension=0, tiled=True
    ).astype(jnp.float32)


def sum_owned(small, qkv, out, gate, up, down):
    owned = [scatter_owned(a) for a in (small, qkv, out)]
    return lax.psum(tuple(a.astype(jnp.bfloat16) for a in (*owned, gate, up, down)), "replica")


def on_device(
    tokens,
    segments,
    norm1_gain,
    qkv_weight,
    qkv_bias,
    out_weight,
    norm2_gain,
    gate_weight,
    up_weight,
    down_weight,
    cotangent,
    *,
    pairs,
    copies,
):
    sequences, length, model_width = tokens.shape
    row_count = sequences * length
    q_width = H * HD
    kv_width = KV * HD
    groups = H // KV
    score_scale = HD ** (-0.5)
    if fits(pairs, copies, tokens, segments, qkv_weight, out_weight, gate_weight, down_weight):
        shape_out = (sequences, length, model_width)
        half_dim = HD // 2
        frequency = ROPE_BASE ** (-2.0 * np.arange(half_dim) / HD)
        frequency = np.concatenate([frequency, frequency])[None].astype(np.float32)
        result, back_tokens, full = layer(
            tokens.reshape(row_count, model_width),
            segments.reshape(1, length),
            jnp.asarray(frequency),
            norm1_gain,
            norm2_gain,
            qkv_bias,
            cotangent.reshape(row_count, model_width),
            qkv_weight,
            out_weight,
            gate_weight,
            up_weight,
            down_weight,
        )
        gate, up, down, qkv, out, norm1, norm2, bias, result, back_tokens = unpack(
            full, result, back_tokens, qkv_weight.shape[1]
        )
        return (
            result.reshape(shape_out),
            back_tokens.reshape(shape_out),
            norm1,
            qkv,
            bias,
            out,
            norm2,
            gate,
            up,
            down,
        )
    gain1_b, b_qkv, gain2_b = gather_vectors([norm1_gain, qkv_bias, norm2_gain], pairs)
    w_qkv = gather_weight(qkv_weight, pairs, copies)
    w_out = gather_weight(out_weight, pairs, copies)
    back_all = gather_rows(cotangent.reshape(row_count, model_width), pairs)
    allowed, cosine, sine = doc_layout(segments, HD)
    resid_in = tokens.reshape(row_count, model_width).astype(jnp.float32)
    inv_rms1 = inverse_rms(resid_in)
    gain1 = gain1_b.astype(jnp.float32)
    normed1 = (resid_in * inv_rms1 * gain1).astype(jnp.bfloat16)
    projected = matmul(normed1, w_qkv) + b_qkv.astype(jnp.float32)
    query = projected[:, :q_width].reshape(sequences, length, H, HD)
    keys_raw = projected[:, q_width : q_width + kv_width].reshape(sequences, length, KV, HD)
    values_raw = projected[:, q_width + kv_width :].reshape(sequences, length, KV, HD)
    query_b = (
        rotate(query, cosine, sine).astype(jnp.bfloat16).reshape(sequences, length, KV, groups, HD)
    )
    keys_b = rotate(keys_raw, cosine, sine).astype(jnp.bfloat16)
    values_b = values_raw.astype(jnp.bfloat16)
    scores = score_block(query_b, keys_b, allowed, score_scale)
    top_score = jnp.max(scores, axis=-1, keepdims=True)
    log_total = top_score + jnp.log(jnp.sum(jnp.exp(scores - top_score), axis=-1, keepdims=True))
    soft_b = jnp.exp(scores - log_total).astype(jnp.bfloat16)
    context = jnp.einsum("skgqp,spkd->sqkgd", soft_b, values_b, preferred_element_type=jnp.float32)
    context_b = context.astype(jnp.bfloat16).reshape(row_count, q_width)
    middle = resid_in + matmul(context_b, w_out)
    inv_rms2 = inverse_rms(middle)
    gain2 = gain2_b.astype(jnp.float32)
    normed2 = (middle * inv_rms2 * gain2).astype(jnp.bfloat16)
    back_rows = cotangent.reshape(row_count, model_width)
    normed_all = gather_rows(normed2, pairs)
    gate_pre = matmul(normed_all, gate_weight)
    up_proj = matmul(normed_all, up_weight)
    sigmoid_gate = jax.nn.sigmoid(gate_pre)
    silu_gate = gate_pre * sigmoid_gate
    activ_b = (silu_gate * up_proj).astype(jnp.bfloat16)
    result = middle + scatter_rows(matmul(activ_b, down_weight), pairs)
    back_activ = times_transposed(back_all, down_weight)
    back_gate = (
        back_activ * up_proj * sigmoid_gate * (1.0 + gate_pre * (1.0 - sigmoid_gate))
    ).astype(jnp.bfloat16)
    back_up = (back_activ * silu_gate).astype(jnp.bfloat16)
    grad_down = outer_sum(activ_b, back_all)
    grad_gate = outer_sum(normed_all, back_gate)
    grad_up = outer_sum(normed_all, back_up)
    local_normed = times_transposed(back_gate, gate_weight) + times_transposed(back_up, up_weight)
    back_normed2 = scatter_rows(local_normed, pairs)
    back_norm2, grad_norm2_part = norm_backward(middle, inv_rms2, gain2, back_normed2)
    back_middle = back_rows.astype(jnp.float32) + back_norm2
    back_middle_b = back_middle.astype(jnp.bfloat16)
    grad_out_part = outer_sum(context_b, back_middle_b)
    back_context = times_transposed(back_middle_b, w_out).astype(jnp.bfloat16)
    back_context = back_context.reshape(sequences, length, KV, groups, HD)
    soft = jnp.exp(score_block(query_b, keys_b, allowed, score_scale) - log_total)
    soft_again = soft.astype(jnp.bfloat16)
    back_values = jnp.einsum(
        "skgqp,sqkgd->spkd", soft_again, back_context, preferred_element_type=jnp.float32
    )
    back_soft = jnp.einsum(
        "sqkgd,spkd->skgqp", back_context, values_b, preferred_element_type=jnp.float32
    )
    row_dot = jnp.sum(soft * back_soft, axis=-1, keepdims=True)
    back_scores = (soft * (back_soft - row_dot) * score_scale).astype(jnp.bfloat16)
    back_query = jnp.einsum(
        "skgqp,spkd->sqkgd", back_scores, keys_b, preferred_element_type=jnp.float32
    )
    back_keys = jnp.einsum(
        "skgqp,sqkgd->spkd", back_scores, query_b, preferred_element_type=jnp.float32
    )
    back_query = unrotate(back_query.reshape(sequences, length, H, HD), cosine, sine)
    back_keys = unrotate(back_keys, cosine, sine)
    back_proj = jnp.concatenate(
        [
            back_query.reshape(row_count, q_width),
            back_keys.reshape(row_count, kv_width),
            back_values.reshape(row_count, kv_width),
        ],
        axis=1,
    )
    grad_bias_part = jnp.sum(back_proj, axis=0)
    back_proj_b = back_proj.astype(jnp.bfloat16)
    grad_qkv_part = outer_sum(normed1, back_proj_b)
    back_normed1 = times_transposed(back_proj_b, w_qkv)
    back_norm1, grad_norm1_part = norm_backward(resid_in, inv_rms1, gain1, back_normed1)
    back_tokens = back_middle + back_norm1
    small = jnp.stack([v.reshape(pairs, -1) for v in (grad_norm1_part, grad_norm2_part)], axis=1)
    small = jnp.concatenate(
        [small.reshape(pairs, -1), grad_bias_part.reshape(pairs, -1)], axis=1
    ).reshape(-1)
    owned = sum_owned(
        small,
        grad_qkv_part,
        grad_out_part,
        grad_gate,
        grad_up,
        grad_down,
    )
    small, grad_qkv, grad_out, grad_gate, grad_up, grad_down = (
        a.astype(jnp.float32) for a in owned
    )
    gains = norm1_gain.shape[0]
    grad_norm1, grad_norm2, grad_bias = (
        small[:gains],
        small[gains : 2 * gains],
        small[2 * gains :],
    )
    shape_out = (sequences, length, model_width)
    return (
        result.reshape(shape_out),
        back_tokens.reshape(shape_out),
        grad_norm1,
        grad_qkv,
        grad_bias,
        grad_out,
        grad_norm2,
        grad_gate,
        grad_up,
        grad_down,
    )


def solution(mesh):
    in_specs = (
        P(("group", "replica"), None, None),
        P(("group", "replica"), None),
        P("group"),
        P("group", None),
        P("group"),
        P("group", None),
        P("group"),
        P(None, "group"),
        P(None, "group"),
        P("group", None),
        P(("group", "replica"), None, None),
    )
    out_specs = (
        P(("group", "replica"), None, None),
        P(("group", "replica"), None, None),
        P("group"),
        P("group", None),
        P("group"),
        P("group", None),
        P("group"),
        P(None, "group"),
        P(None, "group"),
        P("group", None),
    )
    program = functools.partial(
        on_device, pairs=mesh.shape["group"], copies=mesh.shape["replica"]
    )
    return jax.shard_map(
        program, mesh=mesh, in_specs=in_specs, out_specs=out_specs, check_vma=False
    )
```

```python
import functools

import jax
import jax.numpy as jnp
import numpy as np
from jax import lax
from jax.experimental import pallas as pl
from jax.experimental.pallas import tpu as pltpu
from jax.sharding import PartitionSpec as P

H = 14
KV = 2
HD = 64


EPSILON = 1e-06
ROPE_BASE = 1000000.0
NEG_LARGE = -1e30


def doc_layout(segments, head_dim):
    length = segments.shape[1]
    places = jnp.arange(length, dtype=jnp.int32)
    same_doc = segments[:, :, None] == segments[:, None, :]
    earlier = places[None, None, :] < places[None, :, None]
    positions = jnp.sum(jnp.where(same_doc & earlier, 1.0, 0.0).astype(jnp.float32), axis=2)
    allowed = jnp.where(same_doc & (places[None, None, :] <= places[None, :, None]), 1, 0).astype(
        jnp.int32
    )
    half_dim = head_dim // 2
    frequency = ROPE_BASE ** (-2.0 * jnp.arange(half_dim, dtype=jnp.float32) / head_dim)
    angles = positions[:, :, None] * frequency[None, None, :]
    return (allowed, jnp.cos(angles)[:, :, None, :], jnp.sin(angles)[:, :, None, :])


def rotate(values, cosine, sine):
    half_dim = values.shape[-1] // 2
    front_half = values[..., :half_dim]
    back_half = values[..., half_dim:]
    return jnp.concatenate(
        [front_half * cosine - back_half * sine, back_half * cosine + front_half * sine], axis=-1
    )


def unrotate(gradients, cosine, sine):
    half_dim = gradients.shape[-1] // 2
    front_half = gradients[..., :half_dim]
    back_half = gradients[..., half_dim:]
    return jnp.concatenate(
        [front_half * cosine + back_half * sine, back_half * cosine - front_half * sine], axis=-1
    )


def inverse_rms(hidden):
    return lax.rsqrt(jnp.mean(hidden * hidden, axis=-1, keepdims=True) + EPSILON)


def norm_backward(hidden, inv_rms, gain_f, back_normed):
    weighted = back_normed * gain_f
    inner = jnp.mean(weighted * hidden, axis=-1, keepdims=True)
    back_hidden = inv_rms * weighted - hidden * (inv_rms * inv_rms * inv_rms) * inner
    back_gain = jnp.sum(back_normed * hidden * inv_rms, axis=0)
    return (back_hidden, back_gain)


def matmul(left, right):
    return jnp.dot(left, right, preferred_element_type=jnp.float32)


def outer_sum(left, right):
    return lax.dot_general(
        left, right, (((0,), (0,)), ((), ())), preferred_element_type=jnp.float32
    )


def times_transposed(left, right):
    return lax.dot_general(
        left, right, (((1,), (1,)), ((), ())), preferred_element_type=jnp.float32
    )


def score_block(query_b, keys_b, allowed, score_scale):
    scores = (
        jnp.einsum("sqkgd,spkd->skgqp", query_b, keys_b, preferred_element_type=jnp.float32)
        * score_scale
    )
    return jnp.where(allowed[:, None, None, :, :] > 0, scores, NEG_LARGE)


MESH_ID = pl.DeviceIdType.MESH
TILE = 128
SLICE = 640
CHUNK = 64
SMALL_ROWS = 480


def relative(delta):
    me = lax.axis_index("replica")
    pair = lax.axis_index("group")
    core, x = me % 2, lax.div(me, 2) % 2
    d_core, d_x, d_y = delta % 2, lax.div(delta, 2) % 2, lax.div(delta, 4) % 2
    shift = d_core * (1 - 2 * core) + 2 * d_x * (1 - 2 * x)
    return {"group": pair + d_y * (1 - 2 * pair), "replica": me + shift}


def greet(devices):
    barrier = pltpu.get_barrier_semaphore()
    for device in devices:
        pl.semaphore_signal(barrier, inc=1, device_id=device, device_id_type=MESH_ID)
    return barrier


def remote(src, dst, sems, where, device):
    return pltpu.make_async_remote_copy(
        src_ref=src,
        dst_ref=dst,
        send_sem=sems[0].at[where],
        recv_sem=sems[1].at[where],
        device_id=device,
        device_id_type=MESH_ID,
    )


def contract(left, right, left_dim, right_dim):
    return lax.dot_general(
        left,
        right,
        (((left_dim,), (right_dim,)), ((), ())),
        preferred_element_type=jnp.float32,
    )


def layer_kernel(
    tokens_ref,
    seg_row,
    frequency,
    gain1_in,
    gain2_in,
    bias_in,
    cot_ref,
    qkv_ref,
    out_weight_ref,
    gate_ref,
    up_ref,
    down_ref,
    result_ref,
    back_ref,
    out_ref,
    rows_n,
    rows_c,
    w_gate,
    w_up,
    w_down,
    activ,
    d_gate,
    d_up,
    part_b,
    part_r,
    sib_b,
    sib_r,
    land_b,
    land_r,
    own,
    land_u,
    land_m,
    total,
    mine,
    sib,
    across,
    beside,
    joined_ref,
    rest_ref,
    proj,
    stacked,
    normed1,
    share,
    w_qkv_ref,
    w_out_ref,
    vector_ref,
    vectors,
    query_ref,
    keys_ref,
    values_ref,
    log_ref,
    allowed_ref,
    cos_ref,
    sin_ref,
    context_ref,
    middle_ref,
    gain1_ref,
    gain2_ref,
    local,
    link,
    core_n,
    core_c,
    core_b,
    core_r,
    link_b,
    link_r,
    early,
    up,
    mid,
    down,
    side,
    out1,
    out2,
    link_c,
    weights_y,
    weights_x,
    weights_1,
    weights_2,
):
    f32, bf16 = jnp.float32, jnp.bfloat16
    count = own.shape[0] // CHUNK
    length, width = tokens_ref.shape
    bulk = 3 * width
    first = bulk // CHUNK
    lines, wide = mine.shape[1], mine.shape[2]
    half = lines // 2
    depth = joined_ref.shape[0] // 2
    me = lax.axis_index("replica")
    pair = lax.axis_index("group")
    core, x, z = me % 2, lax.div(me, 2) % 2, lax.div(me, 4)
    quarter = me % 4
    beside_quarter = quarter + 2 * (1 - 2 * x)
    middle = (z == 1) | (z == 2)
    is_end = (z == 0) | (z == 3)
    near = {"replica": me + 4 * (1 - 2 * (z % 2))}
    far = {"replica": me + 4 * (1 - 2 * lax.div(z, 2))}
    sibling, neighbour, peer = relative(1), relative(2), relative(4)


    def halves(which):
        return pl.ds(pl.multiple_of(which * half, 16), half)

    def lanes(which):
        return pl.ds(pl.multiple_of(which * wide, TILE), wide)

    first_column = pl.multiple_of(TILE * (5 * quarter - lax.div(quarter, 3)), TILE)
    columns = pl.ds(first_column, SLICE)
    loads = [
        pltpu.make_async_copy(gate_ref.at[:, columns], w_gate, local.at[0]),
        pltpu.make_async_copy(up_ref.at[:, columns], w_up, local.at[1]),
        pltpu.make_async_copy(down_ref.at[columns, :], w_down, local.at[2]),
    ]
    shard = width // 2
    w_loads = [
        pltpu.make_async_copy(
            qkv_ref, w_qkv_ref.at[pl.ds(pl.multiple_of(pair * shard, 64), shard)], local.at[3]
        ),
        pltpu.make_async_copy(
            out_weight_ref, w_out_ref.at[pl.ds(pl.multiple_of(pair * shard, 64), shard)], local.at[4]
        ),
    ]
    for load in w_loads:
        load.start()
    rows_c[0:length] = cot_ref[...]
    vector_ref[0:1, 0:shard] = gain1_in[...].astype(f32).reshape(1, gain1_in.shape[0])
    vector_ref[0:1, 512 : 512 + shard] = gain2_in[...].astype(f32).reshape(1, gain2_in.shape[0])
    vector_ref[0:1, 1024 : 1024 + bias_in.shape[0]] = bias_in[...].astype(f32).reshape(1, bias_in.shape[0])
    barrier = greet([sibling, neighbour, peer, relative(6), near])

    @pl.when(middle)
    def _():
        pl.semaphore_signal(barrier, inc=1, device_id=far, device_id_type=MESH_ID)

    pl.semaphore_wait(barrier, jnp.where(middle, 6, 5))

    def block(ref, slot):
        return ref.at[pl.ds(pl.multiple_of(slot * length, 16), length)]

    part = shard // 4
    cuts = ((0, 48), (48, part - 48))
    vector_copy = remote(vector_ref, vectors, early, 7, peer)
    vector_copy.start()

    def quarter_rows(which, fourth, cut):
        first = which * shard + fourth * part + cuts[cut][0]
        return pl.ds(pl.multiple_of(first, 16), cuts[cut][1])

    moved = [(qkv_ref, w_qkv_ref, 0), (out_weight_ref, w_out_ref, 1)]

    def weight_y(w, cut):
        source, goal, _ = moved[w]
        rows = pl.ds(pl.multiple_of(quarter * part + cuts[cut][0], 16), cuts[cut][1])
        return remote(
            source.at[rows], goal.at[quarter_rows(pair, quarter, cut)], weights_y, 2 * w + cut, peer
        )

    def weight_y_in(w, cut):
        goal = moved[w][1].at[quarter_rows(1 - pair, quarter, cut)]
        return remote(goal, goal, weights_y, 2 * w + cut, peer)

    def weight_pass(w, cut, fourth, sems, device):
        goal = moved[w][1].at[quarter_rows(1 - pair, fourth, cut)]
        return remote(goal, goal, sems, 2 * w + cut, device)

    order = [(w, cut) for w in range(2) for cut in range(2)]
    for w, cut in order:
        weight_y(w, cut).start()
    sends = []

    def send_cot(p):
        copy = remote(block(rows_c, 0), block(rows_c, 2 * p), link_c, p, relative(2 * p))
        copy.start()
        sends.append(copy)

    send_cot(1)

    def forward_n(p):
        return remote(block(rows_n, 2 * p), block(rows_n, 2 * p + 1), core_n, p, sibling)

    def forward_c(p):
        return remote(block(rows_c, 2 * p), block(rows_c, 2 * p + 1), core_c, p, sibling)

    forward_c(0).start()
    for load in loads:
        load.start()
    asked = lax.broadcasted_iota(jnp.int32, (length, length), 0)
    seen = lax.broadcasted_iota(jnp.int32, (length, length), 1)
    seg_column = jnp.sum(jnp.where(asked == seen, seg_row[...], 0), axis=1, keepdims=True)
    same = seg_column == seg_row[...]
    allowed_ref[...] = jnp.where(same & (seen <= asked), 1, 0)
    positions = jnp.sum(jnp.where(same & (seen < asked), 1.0, 0.0), axis=1, keepdims=True)
    angles = positions * frequency[...]
    cos_ref[...] = jnp.cos(angles)
    column = lax.broadcasted_iota(jnp.int32, angles.shape, 1)
    sine = jnp.sin(angles)
    sin_ref[...] = jnp.where(column < HD // 2, sine, -sine)
    tokens = tokens_ref[...].astype(f32)
    inv1 = inverse_rms(tokens)
    vector_copy.wait()
    mine_v, other_v = vector_ref[0:1, :], vectors[0:1, :]
    low_v = jnp.where(pair == 0, mine_v, other_v)
    high_v = jnp.where(pair == 0, other_v, mine_v)
    gain1_ref[...] = jnp.concatenate([low_v[:, :shard], high_v[:, :shard]], axis=1)
    gain2_ref[...] = jnp.concatenate(
        [low_v[:, 512 : 512 + shard], high_v[:, 512 : 512 + shard]], axis=1
    )
    bias_at = 1024
    bias = jnp.concatenate(
        [low_v[:, bias_at : bias_at + proj.shape[1] // 2], high_v[:, bias_at : bias_at + proj.shape[1] // 2]],
        axis=1,
    )
    normed1[...] = (tokens * inv1 * gain1_ref[...]).astype(bf16)
    for load in w_loads:
        load.wait()

    def relay(w):
        for cut in range(2):
            weight_y_in(w, cut).wait_recv()
            weight_pass(w, cut, quarter, weights_x, neighbour).start()
            weight_pass(w, cut, quarter, weights_1, sibling).start()

    def relay_x(w):
        for cut in range(2):
            weight_pass(w, cut, beside_quarter, weights_x, neighbour).wait_recv()
            weight_pass(w, cut, beside_quarter, weights_2, sibling).start()

    def settle(w):
        for cut in range(2):
            weight_y(w, cut).wait_send()
            weight_pass(w, cut, quarter, weights_x, neighbour).wait_send()
            weight_pass(w, cut, quarter, weights_1, sibling).wait()
            weight_pass(w, cut, beside_quarter, weights_2, sibling).wait()

    relay(0)
    send_cot(2)
    relay_x(0)
    settle(0)
    projected = contract(normed1[...], w_qkv_ref[...], 1, 0) + bias
    proj[...] = projected
    relay(1)
    send_cot(3)
    groups = H // KV
    score_scale = HD ** (-0.5)

    def turned(at):
        value = proj[:, at : at + HD]
        swapped = jnp.concatenate([value[:, HD // 2 :], value[:, : HD // 2]], axis=1)
        return (value * cos_ref[...] - swapped * sin_ref[...]).astype(bf16)

    for k in range(KV):
        for j in range(groups):
            query_ref[k, j * length : (j + 1) * length, :] = turned((k * groups + j) * HD)
        at = H * HD + k * HD
        keys_ref[k] = turned(at)
        values_ref[k] = proj[:, at + KV * HD : at + (KV + 1) * HD].astype(bf16)
        mask = jnp.concatenate([allowed_ref[...]] * groups, axis=0) > 0
        scores = contract(query_ref[k], keys_ref[k], 1, 1) * score_scale
        scores = jnp.where(mask, scores, NEG_LARGE)
        top = jnp.max(scores, axis=-1, keepdims=True)
        log_total = top + jnp.log(jnp.sum(jnp.exp(scores - top), axis=-1, keepdims=True))
        log_ref[k] = log_total
        soft = jnp.exp(scores - log_total).astype(bf16)
        context = contract(soft, values_ref[k], 1, 0).astype(bf16)
        for j in range(groups):
            at = (k * groups + j) * HD
            context_ref[:, at : at + HD] = context[j * length : (j + 1) * length, :]
        if k == 0:
            relay_x(1)
    settle(1)
    middle_value = tokens + contract(context_ref[...], w_out_ref[...], 1, 0)
    middle_ref[...] = middle_value
    rows_n[0:length] = (middle_value * inverse_rms(middle_value) * gain2_ref[...]).astype(bf16)
    for p in (1, 2, 3):
        copy = remote(block(rows_n, 0), block(rows_n, 2 * p), link, p, relative(2 * p))
        copy.start()
        sends.append(copy)
    forward_n(0).start()
    for load in loads:
        load.wait()

    def fold(part, sib, core, land, hop, q):
        remote(block(part, 2 * q + 1), sib.at[q], core, q, sibling).wait()
        rows = pl.ds(pl.multiple_of(2 * q * length, 16), length)
        part[rows, :] = (part[rows, :].astype(f32) + sib[q].astype(f32)).astype(bf16)
        remote(block(part, 2 * q), land.at[q - 1], hop, q, relative(2 * q)).start()

    def fold_own(part, sib, core):
        remote(block(part, 1), sib.at[0], core, 0, sibling).wait()
        return part[0:length, :].astype(f32) + sib[0].astype(f32)

    def pair_step(p, carry):
        def arrive(q):
            remote(block(rows_n, 0), block(rows_n, 2 * q), link, q, relative(2 * q)).wait_recv()
            forward_n(q).start()

        @pl.when(p == 1)
        def _():
            arrive(1)
            arrive(2)

        @pl.when(p == 2)
        def _():
            arrive(3)

        @pl.when(p < 3)
        def _():
            q = p + 1
            remote(block(rows_c, 0), block(rows_c, 2 * q), link_c, q, relative(2 * q)).wait_recv()
            forward_c(q).start()

        forward_n(p).wait()
        forward_c(p).wait()
        both = pl.ds(pl.multiple_of(2 * p * length, 32), 2 * length)
        normed, cot = rows_n[both, :], rows_c[both, :]
        gate_pre = contract(normed, w_gate[...], 1, 0)
        up_proj = contract(normed, w_up[...], 1, 0)
        back_activ = contract(cot, w_down[...], 1, 1)
        sigmoid_gate = jax.nn.sigmoid(gate_pre)
        silu_gate = gate_pre * sigmoid_gate
        column = lax.broadcasted_iota(jnp.int32, gate_pre.shape, 1)
        own = column >= jnp.where(quarter == 3, TILE, 0)
        activ[both, :] = jnp.where(own, silu_gate * up_proj, 0.0).astype(jnp.bfloat16)
        d_gate[both, :] = jnp.where(
            own,
            back_activ * up_proj * sigmoid_gate * (1.0 + gate_pre * (1.0 - sigmoid_gate)),
            0.0,
        ).astype(jnp.bfloat16)
        d_up[both, :] = jnp.where(own, back_activ * silu_gate, 0.0).astype(jnp.bfloat16)
        part_b[both, :] = (
            contract(d_gate[both, :], w_gate[...], 1, 1)
            + contract(d_up[both, :], w_up[...], 1, 1)
        ).astype(jnp.bfloat16)
        remote(block(part_b, 2 * p + 1), sib_b.at[p], core_b, p, relative(1)).start()
        part_r[both, :] = contract(activ[both, :], w_down[...], 1, 0).astype(jnp.bfloat16)
        remote(block(part_r, 2 * p + 1), sib_r.at[p], core_r, p, relative(1)).start()

        return carry

    lax.fori_loop(0, 4, pair_step, 0)

    def chunk(c):
        return pl.ds(pl.multiple_of(c * CHUNK, CHUNK), CHUNK)

    def up_copy(c):
        return remote(own.at[chunk(c)], land_u.at[chunk(c)], up, c, near)

    def mid_copy(c):
        return remote(own.at[chunk(c)], land_m.at[chunk(c)], mid, c, far)

    def down_copy(c):
        return remote(total.at[chunk(c)], total.at[chunk(c)], down, c, near)

    def side_copy(c):
        return remote(
            total.at[chunk(c)], out_ref.at[quarter].at[chunk(c)], side, c, neighbour
        )

    def side_arrival(c):
        return remote(
            total.at[chunk(c)], out_ref.at[beside_quarter].at[chunk(c)], side, c, neighbour
        )

    def out_copy(c):
        return remote(total.at[chunk(c)], out_ref.at[quarter].at[chunk(c)], out1, c, sibling)

    def pass_copy(c):
        place = out_ref.at[beside_quarter].at[chunk(c)]
        return remote(place, place, out2, c, sibling)

    def store(c):
        return pltpu.make_async_copy(
            total.at[chunk(c)], out_ref.at[quarter].at[chunk(c)], local.at[7 + c]
        )

    def hand_out(c):
        side_copy(c).start()
        out_copy(c).start()
        store(c).start()

    def add(goal, left, right, rows):
        goal[rows, :] = (
            left[rows, :].astype(jnp.float32) + right[rows, :].astype(jnp.float32)
        ).astype(jnp.bfloat16)

    def send_up(lo, hi):
        @pl.when(is_end)
        def _():
            def go(c, carry):
                up_copy(c).start()
                return carry

            lax.fori_loop(lo, hi, go, 0)

    skew1, skew2 = 3, 14

    def service(i, carry):
        a, b, d = i, i - skew1, i - skew2

        @pl.when(middle & (a < count))
        def _():
            up_copy(a).wait_recv()
            add(own, own, land_u, chunk(a))
            mid_copy(a).start()

        @pl.when((b >= 0) & (b < count))
        def _():
            @pl.when(middle)
            def _():
                mid_copy(b).wait_recv()
                add(total, own, land_m, chunk(b))
                down_copy(b).start()

            @pl.when(is_end)
            def _():
                down_copy(b).wait_recv()

            hand_out(b)

        @pl.when(d >= 0)
        def _():
            side_arrival(d).wait_recv()
            pass_copy(d).start()

        return carry

    def serve(lo, hi):
        lax.fori_loop(lo, hi, service, 0)

    def finish(part, land, hop, goal):
        value = goal[...]
        for p in (1, 2, 3):
            remote(block(part, 2 * p), land.at[p - 1], hop, p, relative(2 * p)).wait()
            value = value + land[p - 1].astype(f32)
        return value

    for q in (1, 2, 3):
        fold(part_b, sib_b, core_b, land_b, link_b, q)
    share[...] = fold_own(part_b, sib_b, core_b)

    def grad_step(h, carry):
        lane = pl.ds(pl.multiple_of(h * TILE, TILE), TILE)
        left = rows_n[:, lane]

        def place(which):
            return pl.ds(pl.multiple_of((3 * h + which) * TILE, TILE), TILE)

        own[place(0), :] = contract(left, d_gate[...], 0, 0).astype(bf16)
        own[place(1), :] = contract(left, d_up[...], 0, 0).astype(bf16)
        down = contract(activ[...], rows_c[:, lane], 0, 0).astype(bf16)
        for i in range(SLICE // TILE):
            own[place(2), i * TILE : (i + 1) * TILE] = down[i * TILE : (i + 1) * TILE]
        per = 3 * TILE // CHUNK
        send_up(h * per, (h + 1) * per)
        return carry

    lax.fori_loop(0, width // TILE, grad_step, 0)
    for q in (1, 2, 3):
        fold(part_r, sib_r, core_r, land_r, link_r, q)
    result_ref[...] = fold_own(part_r, sib_r, core_r)
    serve(0, 2)
    back_normed = finish(part_b, land_b, link_b, share)
    serve(2, 4)

    def norm_back(hidden, inv, gain, back):
        weighted = back * gain
        inner = jnp.mean(weighted * hidden, axis=-1, keepdims=True)
        back_hidden = inv * weighted - hidden * (inv * inv * inv) * inner
        return back_hidden, jnp.sum(back * hidden * inv, axis=0, keepdims=True)

    hidden = middle_ref[...]
    back_hidden, sum2 = norm_back(hidden, inverse_rms(hidden), gain2_ref[...], back_normed)
    back_middle = rows_c[0:length, :].astype(f32) + back_hidden
    share[...] = back_middle
    back_middle_b = back_middle.astype(bf16)
    back_context = contract(back_middle_b, w_out_ref[...], 1, 1).astype(bf16)
    for k in range(KV):
        for j in range(groups):
            at = (k * groups + j) * HD
            stacked[k, j * length : (j + 1) * length, :] = back_context[:, at : at + HD]
    joined_ref[:, proj.shape[1] :] = contract(context_ref[...], back_middle_b, 0, 0).astype(bf16)
    serve(4, 5)

    def unturn(value):
        swapped = jnp.concatenate([value[:, HD // 2 :], value[:, : HD // 2]], axis=1)
        return value * cos_ref[...] + swapped * sin_ref[...]

    for k in range(KV):
        keys, values, query, back = keys_ref[k], values_ref[k], query_ref[k], stacked[k]
        mask = jnp.concatenate([allowed_ref[...]] * groups, axis=0) > 0
        scores = contract(query, keys, 1, 1) * score_scale
        soft = jnp.exp(jnp.where(mask, scores, NEG_LARGE) - log_ref[k])
        back_soft = contract(back, values, 1, 1)
        row_dot = jnp.sum(soft * back_soft, axis=-1, keepdims=True)
        back_scores = (soft * (back_soft - row_dot) * score_scale).astype(bf16)
        back_values = contract(soft.astype(bf16), back, 0, 0)
        back_query = contract(back_scores, keys, 1, 0)
        back_keys = contract(back_scores, query, 0, 0)
        for j in range(groups):
            at = (k * groups + j) * HD
            proj[:, at : at + HD] = unturn(back_query[j * length : (j + 1) * length, :])
        at = H * HD + k * HD
        proj[:, at : at + HD] = unturn(back_keys)
        proj[:, at + KV * HD : at + (KV + 1) * HD] = back_values
        serve(5 + 2 * k, 7 + 2 * k)

    sum_bias = jnp.sum(proj[...], axis=0, keepdims=True)
    proj_b = proj[...].astype(bf16)
    tokens = tokens_ref[...].astype(f32)
    inv1 = inverse_rms(tokens)
    joined_ref[:, : proj.shape[1]] = contract(normed1[...], proj_b, 0, 0).astype(bf16)
    serve(9, 10)
    back_normed1 = contract(proj_b, w_qkv_ref[...], 1, 1)
    back_first, sum1 = norm_back(tokens, inv1, gain1_ref[...], back_normed1)
    back_ref[...] = share[...] + back_first
    row = lax.broadcasted_iota(jnp.int32, rest_ref.shape[1:], 0)

    def lines_of(top, second):
        pads = [
            jnp.concatenate([v, jnp.zeros((1, wide - v.shape[1]), f32)], axis=1)
            if v.shape[1] < wide
            else v
            for v in (top, second)
        ]
        return jnp.where(row == 0, pads[0], jnp.where(row == 1, pads[1], 0.0)).astype(bf16)

    rest_ref[0] = lines_of(sum1, sum2)
    rest_ref[1] = lines_of(sum_bias[:, :wide], sum_bias[:, wide:])
    small_loads = []
    for g in range(2):
        rows = slice(g * depth, (g + 1) * depth)
        small_loads += [
            pltpu.make_async_copy(
                joined_ref.at[rows, lanes(core)], mine.at[g, 0:depth], local.at[3 + g]
            ),
            pltpu.make_async_copy(rest_ref.at[core], mine.at[g, depth:lines], local.at[5 + g]),
        ]
    for copy in small_loads:
        copy.start()
    swap0 = []
    for g in range(2):
        rows = slice(g * depth, (g + 1) * depth)
        swap0 += [
            remote(joined_ref.at[rows, lanes(1 - core)], sib.at[g, 0:depth], early, g, sibling),
            remote(rest_ref.at[1 - core], sib.at[g, depth:lines], early, 2 + g, sibling),
        ]
    for copy in swap0:
        copy.start()
    serve(10, 12)
    for copy in small_loads + swap0:
        copy.wait()

    def add_small(r, carry):
        rows = pl.ds(pl.multiple_of(r * 48, 16), 48)
        for g in range(2):
            mine[g, rows, :] = (
                mine[g, rows, :].astype(jnp.float32) + sib[g, rows, :].astype(jnp.float32)
            ).astype(jnp.bfloat16)
        return carry

    lax.fori_loop(0, lines // 48, add_small, 0)

    def swap_copy(which):
        return remote(
            mine.at[1 - pair].at[halves(which)], across.at[halves(which)], early, 4 + which, peer
        )

    swap_copy(1 - x).start()
    swap_copy(x).start()
    serve(12, 24)
    result_ref[...] = middle_ref[...] + finish(part_r, land_r, link_r, result_ref)


    def add_across(which):
        def go(r, carry):
            rows = pl.ds(pl.multiple_of(which * half + r * 48, 16), 48)
            across[rows, :] = (
                across[rows, :].astype(jnp.float32) + mine[pair, rows, :].astype(jnp.float32)
            ).astype(jnp.bfloat16)
            return carry

        lax.fori_loop(0, half // 48, go, 0)

    swap_copy(1 - x).wait()
    add_across(1 - x)
    side_small = remote(across.at[halves(1 - x)], beside, early, 6, neighbour)
    side_small.start()
    serve(24, 34)
    swap_copy(x).wait()
    side_small.wait()
    for s in range(half // 48):
        rows = pl.ds(pl.multiple_of(x * half + s * 48, 16), 48)
        value = (
            across[rows, :].astype(jnp.float32)
            + mine[pair, rows, :].astype(jnp.float32)
            + beside[s * 48 : (s + 1) * 48, :].astype(jnp.float32)
        ).astype(jnp.bfloat16)
        for t in range(wide // TILE):
            own[bulk + t * 48 : bulk + (t + 1) * 48, s * TILE : (s + 1) * TILE] = value[
                :, t * TILE : (t + 1) * TILE
            ]
    send_up(first, count)
    serve(34, count + skew2)

    def drain(c, carry):
        @pl.when(is_end)
        def _():
            up_copy(c).wait_send()

        @pl.when(middle)
        def _():
            mid_copy(c).wait_send()
            down_copy(c).wait_send()

        side_copy(c).wait_send()
        out_copy(c).wait_send()
        out_copy(c).wait_recv()
        pass_copy(c).wait_send()
        pass_copy(c).wait_recv()
        store(c).wait()
        return carry

    lax.fori_loop(0, count, drain, 0)


    for copy in sends:
        copy.wait_send()


def layer(*args):
    length, width = args[0].shape
    rows = 8 * length
    bf16, f32 = jnp.bfloat16, jnp.float32
    vmem = pl.BlockSpec(memory_space=pltpu.VMEM)
    hbm = pl.BlockSpec(memory_space=pl.ANY)
    qkv_width = args[7].shape[1]
    wide = (qkv_width + width) // 2
    chain = 3 * width + SMALL_ROWS * wide // (2 * SLICE)
    count = chain // CHUNK
    stack = (KV, H // KV * length)
    buffers = [
        ((rows, width), bf16),
        ((rows, width), bf16),
        ((width, SLICE), bf16),
        ((width, SLICE), bf16),
        ((SLICE, width), bf16),
        ((rows, SLICE), bf16),
        ((rows, SLICE), bf16),
        ((rows, SLICE), bf16),
        ((rows, width), bf16),
        ((rows, width), bf16),
        ((4, length, width), bf16),
        ((4, length, width), bf16),
        ((3, length, width), bf16),
        ((3, length, width), bf16),
        ((chain, SLICE), bf16),
        ((chain, SLICE), bf16),
        ((chain, SLICE), bf16),
        ((chain, SLICE), bf16),
        ((2, SMALL_ROWS, wide), bf16),
        ((2, SMALL_ROWS, wide), bf16),
        ((SMALL_ROWS, wide), bf16),
        ((SMALL_ROWS // 2, wide), bf16),
        ((width, 2 * wide), bf16),
        ((2, SMALL_ROWS - width // 2, wide), bf16),
        ((length, qkv_width), f32),
        ((KV, H // KV * length, HD), bf16),
        ((length, width), bf16),
        ((length, width), f32),
        ((width, qkv_width), bf16),
        ((width, width), bf16),
        ((8, 1664), f32),
        ((8, 1664), f32),
        ((*stack, HD), bf16),
        ((KV, length, HD), bf16),
        ((KV, length, HD), bf16),
        ((*stack, 1), f32),
        ((length, length), jnp.int32),
        ((length, HD), f32),
        ((length, HD), f32),
        ((length, width), bf16),
        ((length, width), f32),
        ((1, width), f32),
        ((1, width), f32),
    ]
    sizes = [4] * 7 + [8] + [count] * 6 + [4] * 5

    def body(*refs):
        plain = len(args) + 3 + len(buffers)
        local, rest = refs[plain], refs[plain + 1 :]
        grouped = [(rest[2 * i], rest[2 * i + 1]) for i in range(len(sizes))]
        layer_kernel(*refs[:plain], local, *grouped)

    return pl.pallas_call(
        body,
        out_shape=[
            jax.ShapeDtypeStruct((length, width), f32),
            jax.ShapeDtypeStruct((length, width), f32),
            jax.ShapeDtypeStruct((4, chain, SLICE), bf16),
        ],
        in_specs=[vmem] * 7 + [hbm] * 5,
        out_specs=[vmem, vmem, hbm],
        scratch_shapes=[pltpu.VMEM(shape, kind) for shape, kind in buffers]
        + [pltpu.SemaphoreType.DMA((7 + count,))]
        + [pltpu.SemaphoreType.DMA((size,)) for size in sizes for _ in range(2)],
        compiler_params=pltpu.CompilerParams(
            collective_id=1, has_side_effects=True, vmem_limit_bytes=60 * 1024 * 1024
        ),
        name="layer",
    )(*args)


def unpack_kernel(
    gate_in,
    up_in,
    down_in,
    small_in,
    result_in,
    back_in,
    gate,
    up,
    down,
    qkv,
    out,
    norm1,
    norm2,
    bias,
    result,
    back,
    extra,
):
    f32 = jnp.float32
    result[...] = result_in[...]
    back[...] = back_in[...]
    for source, goal in ((gate_in, gate), (up_in, up)):
        for k in range(3):
            goal[:, k * SLICE : (k + 1) * SLICE] = source[k].astype(f32)
        goal[:, 3 * SLICE :] = source[3, :, TILE:].astype(f32)
    tiles = SLICE // TILE
    for k in range(4):
        for i in range(tiles):
            if k == 3 and i == 0:
                continue
            first = (k * tiles + i - k // 3) * TILE
            down[first : first + TILE, :] = down_in[k, :, i * TILE : (i + 1) * TILE].astype(f32)

    @pl.when(pl.program_id(0) == 0)
    def _():
        depth, split = qkv.shape
        lanes = small_in.shape[1] // 48
        for k in range(4):
            for t in range(lanes):
                for s in range(tiles):
                    value = small_in[
                        k, t * 48 : (t + 1) * 48, s * TILE : (s + 1) * TILE
                    ].astype(f32)
                    row, column = k // 2 * tiles * 48 + s * 48, (k % 2 * lanes + t) * TILE
                    keep = min(48, depth - row)
                    if column < split:
                        qkv[row : row + keep, column : column + TILE] = value[:keep]
                    else:
                        at = column - split
                        out[row : row + keep, at : at + TILE] = value[:keep]
                    if keep < 48:
                        extra[:, column : column + TILE] = value[keep:]
        high = lax.axis_index("group") == 1
        wide, share = extra.shape[1] // 2, norm1.shape[0]
        for row, goal in ((0, norm1), (1, norm2)):
            line = extra[row : row + 1, : 2 * share]
            goal[...] = jnp.where(high, line[:, share:], line[:, :share]).reshape(share)
        most = bias.shape[0]
        line = jnp.concatenate(
            [extra[0:1, wide:], extra[1:2, wide : wide + 2 * most - wide]], axis=1
        )
        goal = jnp.where(high, line[:, most:], line[:, :most])
        bias[...] = goal.reshape(most)


def unpack(full, result, back, qkv_width):
    length, width = result.shape
    f32 = jnp.float32
    steps = width // TILE
    features = 4 * SLICE - TILE
    small_rows = full.shape[1] - 3 * width
    depth = width // 2
    whole = lambda i: (0, 0)
    return pl.pallas_call(
        unpack_kernel,
        grid=(steps,),
        out_shape=[
            jax.ShapeDtypeStruct((width, features), f32),
            jax.ShapeDtypeStruct((width, features), f32),
            jax.ShapeDtypeStruct((features, width), f32),
            jax.ShapeDtypeStruct((depth, qkv_width), f32),
            jax.ShapeDtypeStruct((depth, width), f32),
            jax.ShapeDtypeStruct((depth,), f32),
            jax.ShapeDtypeStruct((depth,), f32),
            jax.ShapeDtypeStruct((qkv_width // 2,), f32),
            jax.ShapeDtypeStruct((length, width), f32),
            jax.ShapeDtypeStruct((length, width), f32),
        ],
        in_specs=[
            pl.BlockSpec((4, TILE, SLICE), lambda i: (0, 3 * i, 0)),
            pl.BlockSpec((4, TILE, SLICE), lambda i: (0, 3 * i + 1, 0)),
            pl.BlockSpec((4, TILE, SLICE), lambda i: (0, 3 * i + 2, 0)),
            pl.BlockSpec((4, small_rows, SLICE), lambda i: (0, 3 * width // small_rows, 0)),
            pl.BlockSpec((length, TILE), lambda i: (0, i)),
            pl.BlockSpec((length, TILE), lambda i: (0, i)),
        ],
        out_specs=[
            pl.BlockSpec((TILE, features), lambda i: (i, 0)),
            pl.BlockSpec((TILE, features), lambda i: (i, 0)),
            pl.BlockSpec((features, TILE), lambda i: (0, i)),
            pl.BlockSpec((depth, qkv_width), whole),
            pl.BlockSpec((depth, width), whole),
            pl.BlockSpec((depth,), lambda i: (0,)),
            pl.BlockSpec((depth,), lambda i: (0,)),
            pl.BlockSpec((qkv_width // 2,), lambda i: (0,)),
            pl.BlockSpec((length, TILE), lambda i: (0, i)),
            pl.BlockSpec((length, TILE), lambda i: (0, i)),
        ],
        scratch_shapes=[pltpu.VMEM((SMALL_ROWS - depth, qkv_width + width), f32)],
        compiler_params=pltpu.CompilerParams(vmem_limit_bytes=56 * 1024 * 1024),
        name="unpack",
    )(full, full, full, full, result, back)


def fits(pairs, copies, tokens, segments, qkv, out, gate, down):
    return (
        pairs == 2
        and copies == 16
        and tokens.shape == (1, 144, 896)
        and qkv.shape == (448, 1152)
        and out.shape == (448, 896)
        and gate.shape == (896, 2432)
        and down.shape == (2432, 896)
    )


def swap(values):
    return lax.ppermute(values, "group", [(0, 1), (1, 0)])


def gather_weight(shard, pairs, copies):
    if pairs != 2 or copies % 2:
        return lax.all_gather(shard, "group", axis=0, tiled=True)
    half = shard.shape[0] // 2
    core = lax.axis_index("replica") % 2
    mine = swap(lax.dynamic_slice_in_dim(shard, core * half, half, 0))
    sibling = lax.ppermute(mine, "replica", [(i, i + 1 - 2 * (i % 2)) for i in range(copies)])
    front = jnp.where(core == 0, mine, sibling)
    back = jnp.where(core == 0, sibling, mine)
    first = lax.axis_index("group") == 0
    other = jnp.concatenate([front, back], axis=0)
    return jnp.concatenate(
        [jnp.where(first, shard, other), jnp.where(first, other, shard)], axis=0
    )


def gather_vectors(vectors, pairs):
    if pairs != 2:
        return [lax.all_gather(v, "group", axis=0, tiled=True) for v in vectors]
    joined = jnp.concatenate(vectors)
    other = swap(joined)
    first = lax.axis_index("group") == 0
    low, high = jnp.where(first, joined, other), jnp.where(first, other, joined)
    found, at = [], 0
    for v in vectors:
        size = v.shape[0]
        found.append(jnp.concatenate([low[at : at + size], high[at : at + size]]))
        at += size
    return found


def gather_rows(rows, pairs):
    if pairs != 2:
        return lax.all_gather(rows, "group", axis=0, tiled=True)
    return jnp.concatenate([rows, swap(rows)], axis=0)


def scatter_rows(partial, pairs):
    if pairs != 2:
        return lax.psum_scatter(
            partial.astype(jnp.bfloat16), "group", scatter_dimension=0, tiled=True
        ).astype(jnp.float32)
    half = partial.shape[0] // 2
    return partial[:half] + swap(partial[half:].astype(jnp.bfloat16)).astype(jnp.float32)


def scatter_owned(partial):
    return lax.psum_scatter(
        partial.astype(jnp.bfloat16), "group", scatter_dimension=0, tiled=True
    ).astype(jnp.float32)


def sum_owned(small, qkv, out, gate, up, down):
    owned = [scatter_owned(a) for a in (small, qkv, out)]
    return lax.psum(tuple(a.astype(jnp.bfloat16) for a in (*owned, gate, up, down)), "replica")


def on_device(
    tokens,
    segments,
    norm1_gain,
    qkv_weight,
    qkv_bias,
    out_weight,
    norm2_gain,
    gate_weight,
    up_weight,
    down_weight,
    cotangent,
    *,
    pairs,
    copies,
):
    sequences, length, model_width = tokens.shape
    row_count = sequences * length
    q_width = H * HD
    kv_width = KV * HD
    groups = H // KV
    score_scale = HD ** (-0.5)
    if fits(pairs, copies, tokens, segments, qkv_weight, out_weight, gate_weight, down_weight):
        shape_out = (sequences, length, model_width)
        half_dim = HD // 2
        frequency = ROPE_BASE ** (-2.0 * np.arange(half_dim) / HD)
        frequency = np.concatenate([frequency, frequency])[None].astype(np.float32)
        result, back_tokens, full = layer(
            tokens.reshape(row_count, model_width),
            segments.reshape(1, length),
            jnp.asarray(frequency),
            norm1_gain,
            norm2_gain,
            qkv_bias,
            cotangent.reshape(row_count, model_width),
            qkv_weight,
            out_weight,
            gate_weight,
            up_weight,
            down_weight,
        )
        gate, up, down, qkv, out, norm1, norm2, bias, result, back_tokens = unpack(
            full, result, back_tokens, qkv_weight.shape[1]
        )
        return (
            result.reshape(shape_out),
            back_tokens.reshape(shape_out),
            norm1,
            qkv,
            bias,
            out,
            norm2,
            gate,
            up,
            down,
        )
    gain1_b, b_qkv, gain2_b = gather_vectors([norm1_gain, qkv_bias, norm2_gain], pairs)
    w_qkv = gather_weight(qkv_weight, pairs, copies)
    w_out = gather_weight(out_weight, pairs, copies)
    back_all = gather_rows(cotangent.reshape(row_count, model_width), pairs)
    allowed, cosine, sine = doc_layout(segments, HD)
    resid_in = tokens.reshape(row_count, model_width).astype(jnp.float32)
    inv_rms1 = inverse_rms(resid_in)
    gain1 = gain1_b.astype(jnp.float32)
    normed1 = (resid_in * inv_rms1 * gain1).astype(jnp.bfloat16)
    projected = matmul(normed1, w_qkv) + b_qkv.astype(jnp.float32)
    query = projected[:, :q_width].reshape(sequences, length, H, HD)
    keys_raw = projected[:, q_width : q_width + kv_width].reshape(sequences, length, KV, HD)
    values_raw = projected[:, q_width + kv_width :].reshape(sequences, length, KV, HD)
    query_b = (
        rotate(query, cosine, sine).astype(jnp.bfloat16).reshape(sequences, length, KV, groups, HD)
    )
    keys_b = rotate(keys_raw, cosine, sine).astype(jnp.bfloat16)
    values_b = values_raw.astype(jnp.bfloat16)
    scores = score_block(query_b, keys_b, allowed, score_scale)
    top_score = jnp.max(scores, axis=-1, keepdims=True)
    log_total = top_score + jnp.log(jnp.sum(jnp.exp(scores - top_score), axis=-1, keepdims=True))
    soft_b = jnp.exp(scores - log_total).astype(jnp.bfloat16)
    context = jnp.einsum("skgqp,spkd->sqkgd", soft_b, values_b, preferred_element_type=jnp.float32)
    context_b = context.astype(jnp.bfloat16).reshape(row_count, q_width)
    middle = resid_in + matmul(context_b, w_out)
    inv_rms2 = inverse_rms(middle)
    gain2 = gain2_b.astype(jnp.float32)
    normed2 = (middle * inv_rms2 * gain2).astype(jnp.bfloat16)
    back_rows = cotangent.reshape(row_count, model_width)
    normed_all = gather_rows(normed2, pairs)
    gate_pre = matmul(normed_all, gate_weight)
    up_proj = matmul(normed_all, up_weight)
    sigmoid_gate = jax.nn.sigmoid(gate_pre)
    silu_gate = gate_pre * sigmoid_gate
    activ_b = (silu_gate * up_proj).astype(jnp.bfloat16)
    result = middle + scatter_rows(matmul(activ_b, down_weight), pairs)
    back_activ = times_transposed(back_all, down_weight)
    back_gate = (
        back_activ * up_proj * sigmoid_gate * (1.0 + gate_pre * (1.0 - sigmoid_gate))
    ).astype(jnp.bfloat16)
    back_up = (back_activ * silu_gate).astype(jnp.bfloat16)
    grad_down = outer_sum(activ_b, back_all)
    grad_gate = outer_sum(normed_all, back_gate)
    grad_up = outer_sum(normed_all, back_up)
    local_normed = times_transposed(back_gate, gate_weight) + times_transposed(back_up, up_weight)
    back_normed2 = scatter_rows(local_normed, pairs)
    back_norm2, grad_norm2_part = norm_backward(middle, inv_rms2, gain2, back_normed2)
    back_middle = back_rows.astype(jnp.float32) + back_norm2
    back_middle_b = back_middle.astype(jnp.bfloat16)
    grad_out_part = outer_sum(context_b, back_middle_b)
    back_context = times_transposed(back_middle_b, w_out).astype(jnp.bfloat16)
    back_context = back_context.reshape(sequences, length, KV, groups, HD)
    soft = jnp.exp(score_block(query_b, keys_b, allowed, score_scale) - log_total)
    soft_again = soft.astype(jnp.bfloat16)
    back_values = jnp.einsum(
        "skgqp,sqkgd->spkd", soft_again, back_context, preferred_element_type=jnp.float32
    )
    back_soft = jnp.einsum(
        "sqkgd,spkd->skgqp", back_context, values_b, preferred_element_type=jnp.float32
    )
    row_dot = jnp.sum(soft * back_soft, axis=-1, keepdims=True)
    back_scores = (soft * (back_soft - row_dot) * score_scale).astype(jnp.bfloat16)
    back_query = jnp.einsum(
        "skgqp,spkd->sqkgd", back_scores, keys_b, preferred_element_type=jnp.float32
    )
    back_keys = jnp.einsum(
        "skgqp,sqkgd->spkd", back_scores, query_b, preferred_element_type=jnp.float32
    )
    back_query = unrotate(back_query.reshape(sequences, length, H, HD), cosine, sine)
    back_keys = unrotate(back_keys, cosine, sine)
    back_proj = jnp.concatenate(
        [
            back_query.reshape(row_count, q_width),
            back_keys.reshape(row_count, kv_width),
            back_values.reshape(row_count, kv_width),
        ],
        axis=1,
    )
    grad_bias_part = jnp.sum(back_proj, axis=0)
    back_proj_b = back_proj.astype(jnp.bfloat16)
    grad_qkv_part = outer_sum(normed1, back_proj_b)
    back_normed1 = times_transposed(back_proj_b, w_qkv)
    back_norm1, grad_norm1_part = norm_backward(resid_in, inv_rms1, gain1, back_normed1)
    back_tokens = back_middle + back_norm1
    small = jnp.stack([v.reshape(pairs, -1) for v in (grad_norm1_part, grad_norm2_part)], axis=1)
    small = jnp.concatenate(
        [small.reshape(pairs, -1), grad_bias_part.reshape(pairs, -1)], axis=1
    ).reshape(-1)
    owned = sum_owned(
        small,
        grad_qkv_part,
        grad_out_part,
        grad_gate,
        grad_up,
        grad_down,
    )
    small, grad_qkv, grad_out, grad_gate, grad_up, grad_down = (
        a.astype(jnp.float32) for a in owned
    )
    gains = norm1_gain.shape[0]
    grad_norm1, grad_norm2, grad_bias = (
        small[:gains],
        small[gains : 2 * gains],
        small[2 * gains :],
    )
    shape_out = (sequences, length, model_width)
    return (
        result.reshape(shape_out),
        back_tokens.reshape(shape_out),
        grad_norm1,
        grad_qkv,
        grad_bias,
        grad_out,
        grad_norm2,
        grad_gate,
        grad_up,
        grad_down,
    )


def solution(mesh):
    in_specs = (
        P(("group", "replica"), None, None),
        P(("group", "replica"), None),
        P("group"),
        P("group", None),
        P("group"),
        P("group", None),
        P("group"),
        P(None, "group"),
        P(None, "group"),
        P("group", None),
        P(("group", "replica"), None, None),
    )
    out_specs = (
        P(("group", "replica"), None, None),
        P(("group", "replica"), None, None),
        P("group"),
        P("group", None),
        P("group"),
        P("group", None),
        P("group"),
        P(None, "group"),
        P(None, "group"),
        P("group", None),
    )
    program = functools.partial(
        on_device, pairs=mesh.shape["group"], copies=mesh.shape["replica"]
    )
    return jax.shard_map(
        program, mesh=mesh, in_specs=in_specs, out_specs=out_specs, check_vma=False
    )
```
